256 devices in a mesh: seq: 32 (over y, x, core), seg: 8 (over z).
Axes of the slice: x: 4, y: 4, z: 8, core: 2. Of those that a mesh axis runs over, the one named last changes fastest.
Arguments:
- query_rows: bfloat16 [8, 8192, 4, 128], P('seg', 'seq'), may hold values from -6 to 6
- key_rows: bfloat16 [8, 8192, 2, 4, 128], P('seg', 'seq'), may hold values from -6 to 6
- value_rows: bfloat16 [8, 8192, 2, 4, 128], P('seg', 'seq'), may hold values from -6 to 6
- out_gain: float32 [4, 128], replicated, may hold values from 0.5 to 1.5
- initial_state: float32 [4, 128, 128], replicated, may hold values from -24 to 24
Outputs:
- normed_out: bfloat16 [8, 8192, 4, 128], P('seg', 'seq')
The draws below stay inside these ranges and needn't reach their ends.
All inputs are finite; a program needn't handle non-finite values.
Results may differ from the reference program's by a relative error of at most 0.004.
Values sent between devices are 32-bit elements; how exact they have to be, the bound alone decides.
No kernel may reach another device: no remote copies, remote signals or barrier semaphores. Data moves between devices by JAX's collectives and lax.ppermute only.
A program may use at most 128 MiB of HBM per device.

```python
import jax
import jax.numpy as jnp
from jax import lax

DK = 128
DV = 128
HEADS = 4
REFL = 2
GROUP = 128
SEGTOK = 8192
SEGS = 8


def steps_of(key, shape, pieces, low, top_value):
    loudness = 1.0
    for position, shards_of in pieces:
        heights = jax.random.uniform(jax.random.fold_in(jax.random.fold_in(key, 6), position), (shards_of,), jnp.float32, low / len(pieces), top_value / len(pieces))
        loudness = loudness * jnp.repeat(jnp.exp(heights), shape[position] // shards_of).reshape((-1,) + (1,) * (len(shape) - 1 - position))
    return loudness


def normal_values(rng, dims, spread, reach, split=(), kind=jnp.bfloat16):
    values = jax.random.normal(rng, dims, jnp.float32) * spread
    if len(split) > 0:
        values = steps_of(rng, dims, split, -0.22, 0.18) * values
    return jnp.clip(values, min=-reach, max=reach).astype(kind)


def setup_inputs(seed: int = 0) -> dict:
    key_list = jax.random.split(jax.random.key(seed), 6)
    return {
        "query_rows": normal_values(key_list[0], (SEGS, SEGTOK, HEADS, DK), 1.0, 6.0, ((0, 8), (1, 32))),
        "key_rows": normal_values(key_list[1], (SEGS, SEGTOK, REFL, HEADS, DK), 1.0, 6.0, ((0, 8), (1, 32))),
        "value_rows": normal_values(key_list[2], (SEGS, SEGTOK, REFL, HEADS, DV), 1.0, 6.0, ((0, 8), (1, 32))),
        "out_gain": jnp.clip(1.0 + 0.1 * jax.random.normal(key_list[3], (HEADS, DV), jnp.float32), 0.5, 1.5),
        "initial_state": normal_values(key_list[4], (HEADS, DK, DV), 4.0, 24.0, (), jnp.float32),
    }


highest = lax.Precision.HIGHEST

def unit_keys(raw):
    raw = raw.astype(jnp.float32)
    return raw * lax.rsqrt(lax.optimization_barrier(jnp.sum(raw * raw, axis=-1, keepdims=True)) + 1e-06)

def solve_single(matrix, target):
    return jax.scipy.linalg.solve_triangular(matrix, target, lower=True, unit_diagonal=True)

def block_factors(query, keyed, valued):
    steps = keyed.shape[-2]
    tokens = query.shape[-2]
    key_gram = jnp.einsum('...id,...jd->...ij', keyed, keyed, precision=highest)
    lower_unit = jnp.eye(steps, dtype=jnp.float32) + jnp.tril(2.0 * key_gram, -1)
    target = jnp.concatenate([2.0 * keyed, 2.0 * valued], axis=-1)
    flat_lower = lower_unit.reshape(-1, steps, steps)
    flat_target = target.reshape(-1, steps, target.shape[-1])
    solved = jax.vmap(solve_single)(flat_lower, flat_target).reshape(target.shape)
    weights = solved[..., :keyed.shape[-1]]
    updates = solved[..., keyed.shape[-1]:]
    visible = jnp.arange(steps)[None, :] <= REFL * jnp.arange(tokens)[:, None] + (REFL - 1)
    scores = jnp.where(visible, jnp.einsum('...td,...ld->...tl', query, keyed, precision=highest), 0.0)
    return (weights, updates, scores)

def reference(query_rows, key_rows, value_rows, out_gain, initial_state):
    total = query_rows.shape[0] * query_rows.shape[1]
    nblock = total // GROUP
    query = query_rows.astype(jnp.float32).reshape(nblock, GROUP, HEADS, DK).transpose(0, 2, 1, 3)
    keyed = unit_keys(key_rows).reshape(nblock, GROUP * REFL, HEADS, DK).transpose(0, 2, 1, 3)
    valued = value_rows.astype(jnp.float32).reshape(nblock, GROUP * REFL, HEADS, DV).transpose(0, 2, 1, 3)

    def advance(state, block):
        query_block, key_block, value_block = block
        weights, updates, scores = block_factors(query_block, key_block, value_block)
        residue = updates - jnp.einsum('hld,hde->hle', weights, state, precision=highest)
        read = jnp.einsum('htd,hde->hte', query_block, state, precision=highest)
        read = read + jnp.einsum('htl,hle->hte', scores, residue, precision=highest)
        state = state + jnp.einsum('hld,hle->hde', key_block, residue, precision=highest)
        return (state, read)
    final_state, reads = lax.scan(advance, initial_state.astype(jnp.float32), (query, keyed, valued))
    reads = reads.transpose(0, 2, 1, 3).reshape(query_rows.shape[0], query_rows.shape[1], HEADS, DV)
    scale = lax.rsqrt(lax.optimization_barrier(jnp.mean(reads * reads, axis=-1, keepdims=True)) + 1e-06)
    return (reads * scale * out_gain).astype(jnp.bfloat16)
```

```python
import jax
import jax.numpy as jnp
from jax import lax
from jax.experimental import pallas as pl
from jax.experimental.pallas import tpu as pltpu
from jax.sharding import PartitionSpec as P

D = 128
HEADS = 4
REFL = 2
BLK = 128
XS = 4
YS = 4
CS = 2
HALF = D // CS
MSG = D + HALF

f32 = jnp.float32
bf16 = jnp.bfloat16


def split(x):
    high = x.astype(bf16)
    low = (x - high.astype(f32)).astype(bf16)
    return high, low


def dot_nn(a, b):
    return lax.dot_general(a, b, (((1,), (0,)), ((), ())), preferred_element_type=f32)


def dot_nt(a, b):
    return lax.dot_general(a, b, (((1,), (1,)), ((), ())), preferred_element_type=f32)


def wide(x):
    high, low = split(x)
    return jnp.concatenate([high, low], axis=1)


def tall_wide(x):
    row = wide(x)
    return jnp.concatenate([row, row], axis=0)


def mm_pre(left_wide, right_tall):
    out = dot_nn(left_wide, right_tall)
    n = out.shape[1] // 2
    return out[:, :n] + out[:, n:]


def mm(a, b):
    return mm_pre(wide(a), tall_wide(b))


def mm_nt(a, b):
    ah, al = split(a)
    bh, bl = split(b)
    return dot_nt(ah, bh) + dot_nt(ah, bl) + dot_nt(al, bh)


def iota2(shape, dim):
    return lax.broadcasted_iota(jnp.int32, shape, dim)


def factor_kernel(r_ref, v_ref, m_ref, z_ref, p_ref):
    heads = r_ref.shape[0]
    nblk = r_ref.shape[1] // BLK
    row = iota2((BLK, BLK), 0)
    col = iota2((BLK, BLK), 1)
    eye = row == col
    chains = [(h, b) for h in range(heads) for b in range(nblk)]
    rs, rts, vts, uppers, invs, ccols, crows = [], [], [], [], [], [], []
    for h, b in chains:
        r = r_ref[h, b * BLK : (b + 1) * BLK, :]
        v = v_ref[h, b * BLK : (b + 1) * BLK, :]
        rt = r.T
        gram = dot_nn(r, rt)
        diag = jnp.where(eye, gram, 0.0)
        ccol = lax.rsqrt(jnp.sum(diag, axis=1, keepdims=True) + 1e-06)
        crow = lax.rsqrt(jnp.sum(diag, axis=0, keepdims=True) + 1e-06)
        upper = jnp.where(row < col, 2.0 * ccol * crow * gram, 0.0)
        pair = ((row >> 1) == (col >> 1)) & (row < col)
        inv = jnp.where(eye, 1.0, 0.0) - jnp.where(pair, upper, 0.0)
        rs.append(r)
        rts.append(rt)
        vts.append(v.T)
        uppers.append(upper)
        invs.append(inv)
        ccols.append(ccol)
        crows.append(crow)
    for level in range(1, 7):
        off = ((row >> (level + 1)) == (col >> (level + 1))) & (
            (row >> level) < (col >> level)
        )
        talls = [tall_wide(inv) for inv in invs]
        mids = [
            mm_pre(wide(jnp.where(off, upper, 0.0)), tall) for upper, tall in zip(uppers, talls)
        ]
        invs = [inv - mm(inv, mid) for inv, mid in zip(invs, mids)]
    pairs = []
    base = jnp.where(iota2((2 * D, D), 0) == iota2((2 * D, D), 1), 1.0, 0.0)
    sign = jnp.where(iota2((2 * D, D), 0) < D, -1.0, 1.0)
    for i, (h, b) in enumerate(chains):
        wh, wl = split(2.0 * ccols[i] * invs[i])
        uh, ul = split(2.0 * invs[i])
        wt = dot_nn(jnp.concatenate([rts[i], rts[i]], axis=1), jnp.concatenate([wh, wl], axis=0))
        ut = dot_nn(jnp.concatenate([vts[i], vts[i]], axis=1), jnp.concatenate([uh, ul], axis=0))
        z = jnp.concatenate([wt, ut], axis=0) * crows[i]
        z_ref[h, b] = z
        rr = jnp.concatenate([rs[i], rs[i]], axis=0)
        pairs.append(base + sign * dot_nn(wide(z), rr))
    for h in range(heads):
        own = pairs[h * nblk : (h + 1) * nblk]
        for b in range(nblk - 1):
            p_ref[h, b] = own[b]
        while len(own) > 1:
            own = [compose(own[i], own[i + 1]) for i in range(0, len(own), 2)]
        m_ref[h] = own[0]


def compose(first, second):
    moved = mm(first, second[:D])
    keep = jnp.concatenate([jnp.zeros((D, D), f32), second[D:]], axis=0)
    return moved + keep


def factor_call(r, v, group):
    heads, steps, _ = r.shape
    nblk = steps // BLK
    return pl.pallas_call(
        factor_kernel,
        grid=(heads // group,),
        in_specs=[pl.BlockSpec((group, steps, D), lambda i: (i, 0, 0))] * 2,
        out_specs=[
            pl.BlockSpec((group, 2 * D, D), lambda i: (i, 0, 0)),
            pl.BlockSpec((group, nblk, 2 * D, D), lambda i: (i, 0, 0, 0)),
            pl.BlockSpec((group, nblk - 1, 2 * D, D), lambda i: (i, 0, 0, 0)),
        ],
        out_shape=[
            jax.ShapeDtypeStruct((heads, 2 * D, D), f32),
            jax.ShapeDtypeStruct((heads, nblk, 2 * D, D), f32),
            jax.ShapeDtypeStruct((heads, nblk - 1, 2 * D, D), f32),
        ],
        compiler_params=pltpu.CompilerParams(vmem_limit_bytes=48 << 20),
        name="factor",
    )(r, v)


def chip_kernel(pos_ref, own_ref, sib_ref, *out_refs):
    x = pos_ref[0]
    core = pos_ref[2]
    half = pl.ds(pl.multiple_of(D + core * HALF, HALF), HALF)
    both = [own_ref, sib_ref]
    for k in range(XS):
        head = lax.rem(x + k, HEADS)

        def run(first, second, k=k, head=head):
            rows = jnp.concatenate([first[head, :D, :], first[head, half, :]], axis=0)
            moved = mm(rows, second[head, :D, :])
            out_refs[k][:D, :] = moved[:D]
            out_refs[k][D:, :] = moved[D:] + second[head, half, :]

        @pl.when(core == 0)
        def _():
            run(both[0], both[1])

        @pl.when(core == 1)
        def _():
            run(both[1], both[0])


def ordered_load(slots, place, scratch):
    n = len(slots)
    for k in range(n):
        scratch[lax.rem(place + n - k, n)] = slots[k][...]


def msg_compose(rows, second):
    moved = mm(rows, second[:D])
    return jnp.concatenate([moved[:D], moved[D:] + second[D:]], axis=0)


def row_kernel(pos_ref, s0, s1, s2, s3, total_ref, pre_ref, scratch):
    ordered_load([s0, s1, s2, s3], pos_ref[0], scratch)
    p1 = scratch[0]
    tail = msg_compose(scratch[2], scratch[3])
    p2 = msg_compose(p1, scratch[1])
    total_ref[...] = msg_compose(p2, tail)
    pre_ref[0] = p1
    pre_ref[1] = p2
    pre_ref[2] = msg_compose(p2, scratch[2])


def column_kernel(pos_ref, s0, s1, s2, s3, total_ref, pre_ref, scratch, hold):
    y = pos_ref[1]
    ordered_load([s0, s1, s2, s3], y, scratch)
    p1 = scratch[0]
    tail = msg_compose(scratch[2], scratch[3])
    p2 = msg_compose(p1, scratch[1])
    total_ref[...] = msg_compose(p2, tail)
    hold[0] = jnp.where(iota2((MSG, D), 0) == iota2((MSG, D), 1), 1.0, 0.0)
    hold[1] = p1
    hold[2] = p2
    hold[3] = msg_compose(p2, scratch[2])
    pre_ref[...] = hold[y]


def window_kernel(pos_ref, own, s1, s2, s3, init_ref, win_ref, state_ref, incl_ref):
    g = pos_ref[3]
    rows = jnp.concatenate(
        [jnp.where(iota2((MSG, D), 0) == iota2((MSG, D), 1), 1.0, 0.0), init_ref[...]], axis=0
    )
    for k, ref in ((3, s3), (2, s2), (1, s1)):
        b = ref[D:, :]
        moved = mm(rows, ref[:D, :])
        moved = jnp.concatenate([moved[:D], moved[D : D + HALF] + b, moved[D + HALF :] + b], axis=0)
        rows = jnp.where(g >= k, moved, rows)
    win_ref[...] = rows[:MSG]
    state = rows[MSG:]
    state_ref[...] = state
    incl_ref[...] = mm(state, own[:D, :]) + own[D:, :]


def entry_kernel(pos_ref, win_ref, state_ref, early_ref, ypre_ref, xpre_ref, *refs):
    outs, scratch = refs[:-1], refs[-1]
    x = pos_ref[0]
    g = pos_ref[3]
    late = mm(early_ref[...], win_ref[:D, :]) + win_ref[D:, :]
    state = jnp.where(g >= 4, late, state_ref[...])
    state = mm(state, ypre_ref[:D, :]) + ypre_ref[D:, :]
    scratch[0] = state
    left = wide(state)
    for i in range(XS - 1):
        scratch[i + 1] = mm_pre(left, tall_wide(xpre_ref[i, :D, :])) + xpre_ref[i, D:, :]
    for k in range(XS):
        outs[k][...] = scratch[lax.rem(x + k, XS)]


def reach_kernel(q_ref, r_ref, z_ref, p_ref, pre_ref, reach_ref, base_ref):
    tokens = q_ref.shape[1]
    nblk = z_ref.shape[1]
    span = tokens // nblk
    prefix = pre_ref[0]
    visible = iota2((span, BLK), 1) <= REFL * iota2((span, BLK), 0) + (REFL - 1)
    for b in range(nblk):
        q = q_ref[0, b * span : (b + 1) * span, :]
        scores = jnp.where(visible, dot_nt(q, r_ref[0, b * BLK : (b + 1) * BLK, :]), 0.0)
        sz = mm_nt(scores, z_ref[0, b])
        project = q.astype(f32) - sz[:, :D]
        moved = mm_nt(project, prefix)
        reach_ref[0, b * span : (b + 1) * span, :] = moved[:, :D]
        base_ref[0, b * span : (b + 1) * span, :] = moved[:, D:] + sz[:, D:]
        if b + 1 < nblk:
            prefix = compose(prefix, p_ref[0, b])


def read_kernel(reach_ref, base_ref, state_ref, gain_ref, out_ref):
    for h in range(HEADS):
        read = mm_nt(reach_ref[h], state_ref[h]) + base_ref[h]
        scale = lax.rsqrt(jnp.mean(read * read, axis=-1, keepdims=True) + 1e-06)
        out_ref[h] = (read * scale * gain_ref[h : h + 1, :]).astype(bf16)


def full(*shape):
    return pl.BlockSpec(shape, lambda: (0,) * len(shape))


def small_call(kernel, name, pos, arrays, outs, scratch=()):
    return pl.pallas_call(
        kernel,
        in_specs=[pl.BlockSpec(memory_space=pltpu.SMEM)]
        + [pl.BlockSpec(memory_space=pltpu.VMEM)] * len(arrays),
        out_specs=[pl.BlockSpec(memory_space=pltpu.VMEM)] * len(outs),
        out_shape=[jax.ShapeDtypeStruct(s, f32) for s in outs],
        scratch_shapes=[pltpu.VMEM(s, f32) for s in scratch],
        name=name,
    )(pos, *arrays)


def seq_perm(move):
    pairs = []
    for y in range(YS):
        for x in range(XS):
            for c in range(CS):
                ny, nx, nc = move(y, x, c)
                pairs.append(((y * XS + x) * CS + c, (ny * XS + nx) * CS + nc))
    return pairs


def per_device(query_rows, key_rows, value_rows, out_gain, initial_state):
    tokens = query_rows.shape[1]
    steps = tokens * REFL
    nblk = steps // BLK
    place = lax.axis_index("seq")
    seg = lax.axis_index("seg")
    core = place % CS
    x = (place // CS) % XS
    y = place // (CS * XS)
    pos = jnp.stack([x, y, core, seg]).astype(jnp.int32)

    swap = seq_perm(lambda y, x, c: (y, x, 1 - c))
    along_x = [seq_perm(lambda y, x, c, k=k: (y, (x + k) % XS, c)) for k in range(1, XS)]
    along_y = [seq_perm(lambda y, x, c, k=k: ((y + k) % YS, x, c)) for k in range(1, YS)]
    segs = 8
    along_z = [[(i, (i + k) % segs) for i in range(segs)] for k in range(1, 4)]
    jump = [(i, (i + 4) % segs) for i in range(segs)]

    r = key_rows[0].reshape(steps, HEADS, D).transpose(1, 0, 2)
    v = value_rows[0].reshape(steps, HEADS, D).transpose(1, 0, 2)
    q = query_rows[0].transpose(1, 0, 2)
    pair, z, parts = factor_call(r, v, 1)
    sib = lax.ppermute(pair, "seq", swap)
    slots = small_call(chip_kernel, "chip", pos, [pair, sib], [(MSG, D)] * XS)
    slots = [slots[0]] + [
        lax.ppermute(s, "seq", p) for s, p in zip(slots[1:], along_x)
    ]
    total, xpre = small_call(
        row_kernel, "row", pos, slots, [(MSG, D), (XS - 1, MSG, D)], [(XS, MSG, D)]
    )
    slots = [total] + [lax.ppermute(total, "seq", p) for p in along_y]
    total, ypre = small_call(
        column_kernel, "column", pos, slots, [(MSG, D), (MSG, D)], [(YS, MSG, D), (YS, MSG, D)]
    )
    slots = [total] + [lax.ppermute(total, "seg", p) for p in along_z]
    start = lax.dynamic_index_in_dim(initial_state, x, 0, False).T
    start = lax.dynamic_slice_in_dim(start, core * HALF, HALF, 0)
    win, state, incl = small_call(
        window_kernel, "window", pos, slots + [start], [(MSG, D), (HALF, D), (HALF, D)]
    )
    early = lax.ppermute(incl, "seg", jump)
    slots = small_call(
        entry_kernel,
        "entry",
        pos,
        [win, state, early, ypre, xpre],
        [(HALF, D)] * XS,
        [(XS, HALF, D)],
    )
    slots = [slots[0]] + [lax.ppermute(s, "seq", p) for s, p in zip(slots[1:], along_x)]

    eye_pair = jnp.concatenate([jnp.eye(D, dtype=f32), jnp.zeros((D, D), f32)], axis=0)
    before = jnp.where(core == 1, sib, jnp.broadcast_to(eye_pair, sib.shape))
    reach, base = pl.pallas_call(
        reach_kernel,
        grid=(HEADS,),
        in_specs=[
            pl.BlockSpec((1, tokens, D), lambda i: (i, 0, 0)),
            pl.BlockSpec((1, steps, D), lambda i: (i, 0, 0)),
            pl.BlockSpec((1, nblk, 2 * D, D), lambda i: (i, 0, 0, 0)),
            pl.BlockSpec((1, nblk - 1, 2 * D, D), lambda i: (i, 0, 0, 0)),
            pl.BlockSpec((1, 2 * D, D), lambda i: (i, 0, 0)),
        ],
        out_specs=[pl.BlockSpec((1, tokens, D), lambda i: (i, 0, 0))] * 2,
        out_shape=[jax.ShapeDtypeStruct((HEADS, tokens, D), f32)] * 2,
        name="reach",
    )(q, r, z, parts, before)

    mine = jnp.stack(slots)
    other = lax.ppermute(mine, "seq", swap)
    low = jnp.where(core == 0, mine, other)
    high = jnp.where(core == 0, other, mine)
    states = jnp.concatenate([low, high], axis=1)
    order = (x - jnp.arange(HEADS)) % HEADS
    states = jnp.take(states, order, axis=0)
    out = pl.pallas_call(
        read_kernel,
        out_shape=jax.ShapeDtypeStruct((HEADS, tokens, D), bf16),
        name="read",
    )(reach, base, states, out_gain)
    return out.transpose(1, 0, 2)[None]


def solution(mesh):
    return jax.shard_map(
        per_device,
        mesh=mesh,
        in_specs=(
            P("seg", "seq", None, None),
            P("seg", "seq", None, None, None),
            P("seg", "seq", None, None, None),
            P(),
            P(),
        ),
        out_specs=P("seg", "seq", None, None),
        check_vma=False,
    )
```

```python
import functools

import jax
import jax.numpy as jnp
from jax import lax
from jax.experimental import pallas as pl
from jax.experimental.pallas import tpu as pltpu
from jax.sharding import PartitionSpec as P

D = 128
HEADS = 4
REFL = 2
BLK = 128
XS = 4
YS = 4
CS = 2
HALF = D // CS
MSG = D + HALF

f32 = jnp.float32
bf16 = jnp.bfloat16


def split(x):
    high = x.astype(bf16)
    low = (x - high.astype(f32)).astype(bf16)
    return high, low


def dot_nn(a, b):
    return lax.dot_general(a, b, (((1,), (0,)), ((), ())), preferred_element_type=f32)


def dot_nt(a, b):
    return lax.dot_general(a, b, (((1,), (1,)), ((), ())), preferred_element_type=f32)


def wide(x):
    high, low = split(x)
    return jnp.concatenate([high, low], axis=1)


def tall_wide(x):
    row = wide(x)
    return jnp.concatenate([row, row], axis=0)


def mm_pre(left_wide, right_tall):
    out = dot_nn(left_wide, right_tall)
    n = out.shape[1] // 2
    return out[:, :n] + out[:, n:]


def mm(a, b):
    return mm_pre(wide(a), tall_wide(b))


def mm_nt(a, b):
    ah, al = split(a)
    bh, bl = split(b)
    return dot_nt(ah, bh) + dot_nt(ah, bl) + dot_nt(al, bh)


def iota2(shape, dim):
    return lax.broadcasted_iota(jnp.int32, shape, dim)


def factor_kernel(k_ref, v_ref, m_ref, z_ref, p_ref, r_ref, keys, values):
    keys[...] = k_ref[...].astype(f32)
    values[...] = v_ref[...].astype(f32)
    nblk = r_ref.shape[1] // BLK
    row = iota2((BLK, BLK), 0)
    col = iota2((BLK, BLK), 1)
    eye = row == col
    chains = [(h, b) for h in range(HEADS) for b in range(nblk)]
    rs, rts, vts, uppers, invs, ccols, crows = [], [], [], [], [], [], []
    for h, b in chains:
        rows = pl.ds(h + HEADS * BLK * b, BLK, stride=HEADS)
        r = keys[rows, :].astype(bf16)
        v = values[rows, :].astype(bf16)
        r_ref[h, b * BLK : (b + 1) * BLK, :] = r
        rt = r.T
        gram = dot_nn(r, rt)
        diag = jnp.where(eye, gram, 0.0)
        ccol = lax.rsqrt(jnp.sum(diag, axis=1, keepdims=True) + 1e-06)
        crow = lax.rsqrt(jnp.sum(diag, axis=0, keepdims=True) + 1e-06)
        upper = jnp.where(row < col, 2.0 * ccol * crow * gram, 0.0)
        pair = ((row >> 1) == (col >> 1)) & (row < col)
        inv = jnp.where(eye, 1.0, 0.0) - jnp.where(pair, upper, 0.0)
        rs.append(r)
        rts.append(rt)
        vts.append(v.T)
        uppers.append(upper)
        invs.append(inv)
        ccols.append(ccol)
        crows.append(crow)
    for level in range(1, 7):
        off = ((row >> (level + 1)) == (col >> (level + 1))) & (
            (row >> level) < (col >> level)
        )
        talls = [tall_wide(inv) for inv in invs]
        mids = [
            mm_pre(wide(jnp.where(off, upper, 0.0)), tall) for upper, tall in zip(uppers, talls)
        ]
        invs = [inv - mm(inv, mid) for inv, mid in zip(invs, mids)]
    pairs = []
    base = jnp.where(iota2((2 * D, D), 0) == iota2((2 * D, D), 1), 1.0, 0.0)
    sign = jnp.where(iota2((2 * D, D), 0) < D, -1.0, 1.0)
    for i, (h, b) in enumerate(chains):
        wh, wl = split(2.0 * ccols[i] * invs[i])
        uh, ul = split(2.0 * invs[i])
        wt = dot_nn(jnp.concatenate([rts[i], rts[i]], axis=1), jnp.concatenate([wh, wl], axis=0))
        ut = dot_nn(jnp.concatenate([vts[i], vts[i]], axis=1), jnp.concatenate([uh, ul], axis=0))
        z = jnp.concatenate([wt, ut], axis=0) * crows[i]
        z_ref[h, b] = z
        rr = jnp.concatenate([rs[i], rs[i]], axis=0)
        pairs.append(base + sign * dot_nn(wide(z), rr))
    for h in range(HEADS):
        own = pairs[h * nblk : (h + 1) * nblk]
        for b in range(nblk - 1):
            p_ref[h, b] = own[b]
        while len(own) > 1:
            own = [compose(own[i], own[i + 1]) for i in range(0, len(own), 2)]
        m_ref[h] = own[0]


def compose(first, second):
    moved = mm(first, second[:D])
    keep = jnp.concatenate([jnp.zeros((D, D), f32), second[D:]], axis=0)
    return moved + keep


def whole(*arrays):
    return [pl.BlockSpec(memory_space=pltpu.VMEM)] * len(arrays)


def factor_call(k, v):
    steps = k.shape[0] // HEADS
    nblk = steps // BLK
    return pl.pallas_call(
        factor_kernel,
        in_specs=whole(k, v),
        out_specs=[pl.BlockSpec(memory_space=pltpu.VMEM)] * 4,
        out_shape=[
            jax.ShapeDtypeStruct((HEADS, 2 * D, D), f32),
            jax.ShapeDtypeStruct((HEADS, nblk, 2 * D, D), f32),
            jax.ShapeDtypeStruct((HEADS, nblk - 1, 2 * D, D), f32),
            jax.ShapeDtypeStruct((HEADS, steps, D), bf16),
        ],
        scratch_shapes=[pltpu.VMEM((HEADS * steps, D), f32)] * 2,
        compiler_params=pltpu.CompilerParams(vmem_limit_bytes=40 << 20),
        name="factor",
    )(k, v)


def chip_kernel(pos_ref, own_ref, sib_ref, *out_refs):
    x = pos_ref[0]
    core = pos_ref[2]
    half = pl.ds(pl.multiple_of(D + core * HALF, HALF), HALF)
    lower = core == 0
    for k in range(XS):
        head = lax.rem(x + k, HEADS)
        own_t, sib_t = own_ref[head, :D, :], sib_ref[head, :D, :]
        own_s, sib_s = own_ref[head, half, :], sib_ref[head, half, :]
        rows = jnp.concatenate(
            [jnp.where(lower, own_t, sib_t), jnp.where(lower, own_s, sib_s)], axis=0
        )
        moved = mm(rows, jnp.where(lower, sib_t, own_t))
        out_refs[k][:D, :] = moved[:D]
        out_refs[k][D:, :] = moved[D:] + jnp.where(lower, sib_s, own_s)


def ordered_load(slots, place, scratch):
    n = len(slots)
    for k in range(n):
        scratch[lax.rem(place + n - k, n)] = slots[k][...]


def msg_compose(rows, second):
    moved = mm(rows, second[:D])
    return jnp.concatenate([moved[:D], moved[D:] + second[D:]], axis=0)


def advance(state, second):
    return mm(state, second[:D]) + second[D:]


def prefix_totals(slots, place, total_ref, pre_ref, scratch):
    ordered_load(slots, place, scratch)
    first = scratch[0]
    tail = msg_compose(scratch[2], scratch[3])
    second = msg_compose(first, scratch[1])
    total_ref[...] = msg_compose(second, tail)
    pre_ref[0] = first
    pre_ref[1] = second
    pre_ref[2] = msg_compose(second, scratch[2])


def row_kernel(pos_ref, s0, s1, s2, s3, total_ref, pre_ref, scratch):
    prefix_totals([s0, s1, s2, s3], pos_ref[0], total_ref, pre_ref, scratch)


def column_kernel(pos_ref, s0, s1, s2, s3, total_ref, pre_ref, scratch):
    prefix_totals([s0, s1, s2, s3], pos_ref[1], total_ref, pre_ref, scratch)


def path_kernel(pos_ref, ypre_ref, xpre_ref, init_ref, after_ref, path_ref, start_ref, hold):
    x = pos_ref[0]
    y = pos_ref[1]
    core = pos_ref[2]
    here = ypre_ref[lax.max(y, 1) - 1]
    here = jnp.where(
        y == 0, jnp.where(iota2((MSG, D), 0) == iota2((MSG, D), 1), 1.0, 0.0), here
    )
    path_ref[0] = here
    left = wide(here)
    for i in range(XS - 1):
        moved = mm_pre(left, tall_wide(xpre_ref[i, :D, :]))
        path_ref[i + 1, :D, :] = moved[:D]
        path_ref[i + 1, D:, :] = moved[D:] + xpre_ref[i, D:, :]
    hold[...] = init_ref[x].T
    start_ref[...] = hold[pl.ds(pl.multiple_of(core * HALF, HALF), HALF), :]


def early_states(g, s2, s3, start):
    state = jnp.where(g >= 3, advance(start, s3), start)
    return jnp.where(g >= 2, advance(state, s2), state)


def lead_kernel(pos_ref, own, s1, s2, s3, start_ref, lead_ref):
    g = pos_ref[3]
    state = early_states(g, s2[...], s3[...], start_ref[...])
    step = jnp.where(g >= 1, msg_compose(s1[...], own[...]), own[...])
    lead_ref[...] = advance(state, step)


def fuse_kernel(pos_ref, s1, s2, s3, start_ref, path_ref, after_ref, fuse_ref, state_ref):
    g = pos_ref[3]
    state = early_states(g, s2[...], s3[...], start_ref[...])
    state_ref[...] = jnp.where(g >= 1, advance(state, s1[...]), state)
    window = msg_compose(msg_compose(s3[...], s2[...]), s1[...])
    left = wide(window)
    for i in range(XS):
        path = path_ref[i]
        moved = mm_pre(left, tall_wide(path[:D]))
        moved = jnp.concatenate([moved[:D], moved[D:] + path[D:]], axis=0)
        fuse_ref[i] = jnp.where(g >= 4, moved, path)


def entry_kernel(pos_ref, state_ref, early_ref, fuse_ref, after_ref, o0, o1, o2, o3, scratch):
    x = pos_ref[0]
    state = jnp.where(pos_ref[3] >= 4, early_ref[...], state_ref[...])
    left = wide(state)
    for i in range(XS):
        scratch[i] = mm_pre(left, tall_wide(fuse_ref[i, :D, :])) + fuse_ref[i, D:, :]
    for k, out in enumerate((o0, o1, o2, o3)):
        out[...] = scratch[lax.rem(x + k, XS)]


def reach_kernel(pos_ref, q_ref, r_ref, z_ref, p_ref, sib_ref, after_ref, reach_ref, base_ref, rows, *, head):
    tokens = reach_ref.shape[1]
    nblk = z_ref.shape[1]
    span = tokens // nblk
    group = reach_ref.shape[0]
    rows[...] = q_ref[...].astype(f32)
    visible = iota2((span, BLK), 1) <= REFL * iota2((span, BLK), 0) + (REFL - 1)
    base = jnp.where(iota2((2 * D, D), 0) == iota2((2 * D, D), 1), 1.0, 0.0)
    prefixes = [jnp.where(pos_ref[2] == 1, sib_ref[h], base) for h in range(group)]
    for b in range(nblk):
        for h in range(group):
            part = slice(b * span, (b + 1) * span)
            q = rows[pl.ds(head + h + HEADS * span * b, span, stride=HEADS), :]
            scores = dot_nt(q.astype(bf16), r_ref[h, b * BLK : (b + 1) * BLK, :])
            sz = mm_nt(jnp.where(visible, scores, 0.0), z_ref[h, b])
            project = q - sz[:, :D]
            moved = mm_nt(project, prefixes[h])
            reach_ref[h, part, :] = moved[:, :D]
            base_ref[h, part, :] = moved[:, D:] + sz[:, D:]
            if b + 1 < nblk:
                prefixes[h] = compose(prefixes[h], p_ref[h, b])


def reach_call(pos, q, r, z, p, sib, after, head, group):
    tokens = q.shape[0] // HEADS
    place = head // group

    def spec(array):
        rest = array.shape[1:]
        return pl.BlockSpec((group, *rest), lambda i: (place,) + (0,) * len(rest))

    return pl.pallas_call(
        functools.partial(reach_kernel, head=head),
        grid=(1,),
        in_specs=[
            pl.BlockSpec(memory_space=pltpu.SMEM),
            pl.BlockSpec(q.shape, lambda i: (0, 0)),
            spec(r),
            spec(z),
            spec(p),
            spec(sib),
            pl.BlockSpec(memory_space=pl.ANY),
        ],
        out_specs=[pl.BlockSpec((group, tokens, D), lambda i: (0, 0, 0))] * 2,
        out_shape=[jax.ShapeDtypeStruct((group, tokens, D), f32)] * 2,
        scratch_shapes=[pltpu.VMEM(q.shape, f32)],
        compiler_params=pltpu.CompilerParams(vmem_limit_bytes=16 << 20),
        cost_estimate=pl.CostEstimate(flops=400_000_000 * group, bytes_accessed=3_000_000 * group, transcendentals=0),
        name="reach",
    )(pos, q, r, z, p, sib, after)


def read_kernel(pos_ref, ra, ba, rb, bb, mine_ref, other_ref, gain_ref, out_ref, rows):
    x = pos_ref[0]
    lower = pos_ref[2] == 0
    tokens = ra.shape[1]
    group = ra.shape[0]
    for h in range(HEADS):
        reach, base = (ra, ba) if h < group else (rb, bb)
        slot = lax.rem(x + HEADS - h, HEADS)
        mine, other = mine_ref[slot], other_ref[slot]
        state = jnp.concatenate(
            [jnp.where(lower, mine, other), jnp.where(lower, other, mine)], axis=0
        )
        read = mm_nt(reach[h % group], state) + base[h % group]
        scale = lax.rsqrt(jnp.mean(read * read, axis=-1, keepdims=True) + 1e-06)
        rows[pl.ds(h, tokens, stride=HEADS), :] = read * scale * gain_ref[h : h + 1, :]
    out_ref[...] = rows[...].astype(bf16)


def small_call(kernel, name, pos, arrays, outs, scratch=(), after=None, limit=4, out_dtype=f32):
    extra = [] if after is None else [after]
    return pl.pallas_call(
        kernel,
        in_specs=[pl.BlockSpec(memory_space=pltpu.SMEM)]
        + whole(*arrays)
        + [pl.BlockSpec(memory_space=pl.ANY)] * len(extra),
        out_specs=whole(*outs),
        out_shape=[jax.ShapeDtypeStruct(s, out_dtype) for s in outs],
        scratch_shapes=[pltpu.VMEM(s, f32) for s in scratch],
        compiler_params=pltpu.CompilerParams(vmem_limit_bytes=limit << 20),
        name=name,
    )(pos, *arrays, *extra)


def seq_perm(move):
    pairs = []
    for y in range(YS):
        for x in range(XS):
            for c in range(CS):
                ny, nx, nc = move(y, x, c)
                pairs.append(((y * XS + x) * CS + c, (ny * XS + nx) * CS + nc))
    return pairs


def per_device(query_rows, key_rows, value_rows, out_gain, initial_state):
    tokens = query_rows.shape[1]
    steps = tokens * REFL
    place = lax.axis_index("seq")
    seg = lax.axis_index("seg")
    core = place % CS
    x = (place // CS) % XS
    y = place // (CS * XS)
    pos = jnp.stack([x, y, core, seg]).astype(jnp.int32)

    swap = seq_perm(lambda y, x, c: (y, x, 1 - c))
    along_x = [seq_perm(lambda y, x, c, k=k: (y, (x + k) % XS, c)) for k in range(1, XS)]
    along_y = [seq_perm(lambda y, x, c, k=k: ((y + k) % YS, x, c)) for k in range(1, YS)]
    segs = 8
    along_z = [[(i, (i + k) % segs) for i in range(segs)] for k in range(1, 4)]
    jump = [(i, (i + 4) % segs) for i in range(segs)]

    keys = key_rows.reshape(steps * HEADS, D)
    values = value_rows.reshape(steps * HEADS, D)
    query = query_rows.reshape(tokens * HEADS, D)
    pair, z, parts, r = factor_call(keys, values)
    sib = lax.ppermute(pair, "seq", swap)
    slots = small_call(chip_kernel, "chip", pos, [pair, sib], [(MSG, D)] * XS)
    slots = [slots[0]] + [lax.ppermute(s, "seq", p) for s, p in zip(slots[1:], along_x)]
    total, xpre = small_call(
        row_kernel, "row", pos, slots, [(MSG, D), (XS - 1, MSG, D)], [(XS, MSG, D)]
    )
    slots = [total] + [lax.ppermute(total, "seq", p) for p in along_y]
    total, ypre = small_call(
        column_kernel, "column", pos, slots, [(MSG, D), (YS - 1, MSG, D)], [(YS, MSG, D)]
    )
    slots = [lax.ppermute(total, "seg", p) for p in along_z]
    path, start = small_call(
        path_kernel,
        "path",
        pos,
        [ypre, xpre, initial_state],
        [(XS, MSG, D), (HALF, D)],
        [(D, D)],
        after=total,
    )
    reach_a, base_a = reach_call(pos, query, r, z, parts, sib, path, 0, 2)
    (lead,) = small_call(
        lead_kernel, "lead", pos, [total, *slots, start], [(HALF, D)]
    )
    early = lax.ppermute(lead, "seg", jump)
    fused, state = small_call(
        fuse_kernel, "fuse", pos, [*slots, start, path], [(XS, MSG, D), (HALF, D)], after=lead
    )
    reach_b, base_b = reach_call(pos, query, r, z, parts, sib, lead, 2, 2)
    slots = small_call(
        entry_kernel,
        "entry",
        pos,
        [state, early, fused],
        [(HALF, D)] * XS,
        [(XS, HALF, D)],
        after=reach_b,
    )
    slots = [slots[0]] + [lax.ppermute(s, "seq", p) for s, p in zip(slots[1:], along_x)]
    mine = jnp.stack(slots)
    other = lax.ppermute(mine, "seq", swap)
    (out,) = small_call(
        read_kernel,
        "read",
        pos,
        [reach_a, base_a, reach_b, base_b, mine, other, out_gain],
        [(tokens * HEADS, D)],
        [(tokens * HEADS, D)],
        limit=8,
        out_dtype=bf16,
    )
    return out.reshape(1, tokens, HEADS, D)


def solution(mesh):
    return jax.shard_map(
        per_device,
        mesh=mesh,
        in_specs=(
            P("seg", "seq", None, None),
            P("seg", "seq", None, None, None),
            P("seg", "seq", None, None, None),
            P(),
            P(),
        ),
        out_specs=P("seg", "seq", None, None),
        check_vma=False,
    )
```

```python
import functools

import jax
import jax.numpy as jnp
from jax import lax
from jax.experimental import pallas as pl
from jax.experimental.pallas import tpu as pltpu
from jax.sharding import PartitionSpec as P

D = 128
HEADS = 4
REFL = 2
BLK = 128
XS = 4
YS = 4
CS = 2
ZG = 4
HALF = D // CS
MSG = D + HALF

f32 = jnp.float32
bf16 = jnp.bfloat16


def split(x):
    high = x.astype(bf16)
    low = (x - high.astype(f32)).astype(bf16)
    return high, low


def dot_nn(a, b):
    return lax.dot_general(a, b, (((1,), (0,)), ((), ())), preferred_element_type=f32)


def dot_nt(a, b):
    return lax.dot_general(a, b, (((1,), (1,)), ((), ())), preferred_element_type=f32)


def wide(x):
    high, low = split(x)
    return jnp.concatenate([high, low], axis=1)


def tall_wide(x):
    row = wide(x)
    return jnp.concatenate([row, row], axis=0)


def mm_pre(left_wide, right_tall):
    out = dot_nn(left_wide, right_tall)
    n = out.shape[1] // 2
    return out[:, :n] + out[:, n:]


def mm(a, b):
    return mm_pre(wide(a), tall_wide(b))


def mm_nt(a, b):
    ah, al = split(a)
    bh, bl = split(b)
    return dot_nt(ah, bh) + dot_nt(ah, bl) + dot_nt(al, bh)


def iota2(shape, dim):
    return lax.broadcasted_iota(jnp.int32, shape, dim)


def factor_kernel(k_hbm, v_hbm, m_ref, z_ref, r_ref, k_ref, v_ref, keys, values, sems):
    pieces = sems.shape[1]
    size = k_ref.shape[0] // pieces
    copies = [
        [
            pltpu.make_async_copy(
                src.at[pl.ds(i * size, size)], dst.at[pl.ds(i * size, size)], sems.at[j, i]
            )
            for i in range(pieces)
        ]
        for j, (src, dst) in enumerate(((k_hbm, k_ref), (v_hbm, v_ref)))
    ]
    for group in copies:
        for copy in group:
            copy.start()
    for i, copy in enumerate(copies[0]):
        copy.wait()
        keys[i * size : (i + 1) * size] = k_ref[i * size : (i + 1) * size].astype(f32)
    nblk = r_ref.shape[1] // BLK
    row = iota2((BLK, BLK), 0)
    col = iota2((BLK, BLK), 1)
    eye = row == col
    chains = [(h, b) for h in range(HEADS) for b in range(nblk)]
    rs, rts, vts, uppers, invs, ccols, crows = [], [], [], [], [], [], []
    for h, b in chains:
        rows = pl.ds(h + HEADS * BLK * b, BLK, stride=HEADS)
        r = keys[rows, :].astype(bf16)
        r_ref[h, b * BLK : (b + 1) * BLK, :] = r
        rt = r.T
        gram = dot_nn(r, rt)
        diag = jnp.where(eye, gram, 0.0)
        ccol = lax.rsqrt(jnp.sum(diag, axis=1, keepdims=True) + 1e-06)
        crow = lax.rsqrt(jnp.sum(diag, axis=0, keepdims=True) + 1e-06)
        upper = jnp.where(row < col, 2.0 * ccol * crow * gram, 0.0)
        pair = ((row >> 1) == (col >> 1)) & (row < col)
        inv = jnp.where(eye, 1.0, 0.0) - jnp.where(pair, upper, 0.0)
        rs.append(r)
        rts.append(rt)
        uppers.append(upper)
        invs.append(inv)
        ccols.append(ccol)
        crows.append(crow)
    for level in range(1, 7):
        off = ((row >> (level + 1)) == (col >> (level + 1))) & (
            (row >> level) < (col >> level)
        )
        talls = [tall_wide(inv) for inv in invs]
        mids = [
            mm_pre(wide(jnp.where(off, upper, 0.0)), tall) for upper, tall in zip(uppers, talls)
        ]
        invs = [inv - mm(inv, mid) for inv, mid in zip(invs, mids)]
    for i, copy in enumerate(copies[1]):
        copy.wait()
        values[i * size : (i + 1) * size] = v_ref[i * size : (i + 1) * size].astype(f32)
    for h, b in chains:
        rows = pl.ds(h + HEADS * BLK * b, BLK, stride=HEADS)
        vts.append(values[rows, :].astype(bf16).T)
    pairs = []
    base = jnp.where(iota2((2 * D, D), 0) == iota2((2 * D, D), 1), 1.0, 0.0)
    sign = jnp.where(iota2((2 * D, D), 0) < D, -1.0, 1.0)
    for i, (h, b) in enumerate(chains):
        wh, wl = split(2.0 * ccols[i] * invs[i])
        uh, ul = split(2.0 * invs[i])
        wt = dot_nn(jnp.concatenate([rts[i], rts[i]], axis=1), jnp.concatenate([wh, wl], axis=0))
        ut = dot_nn(jnp.concatenate([vts[i], vts[i]], axis=1), jnp.concatenate([uh, ul], axis=0))
        z = jnp.concatenate([wt, ut], axis=0) * crows[i]
        z_ref[h, b] = z
        rr = jnp.concatenate([rs[i], rs[i]], axis=0)
        pairs.append(base + sign * dot_nn(wide(z), rr))
    for h in range(HEADS):
        own = pairs[h * nblk : (h + 1) * nblk]
        while len(own) > 1:
            own = [compose(own[i], own[i + 1]) for i in range(0, len(own), 2)]
        m_ref[h] = own[0]


def compose(first, second):
    moved = mm(first, second[:D])
    keep = jnp.concatenate([jnp.zeros((D, D), f32), second[D:]], axis=0)
    return moved + keep


def whole(*arrays):
    return [pl.BlockSpec(memory_space=pltpu.VMEM)] * len(arrays)


def factor_call(k, v):
    steps = k.shape[0] // HEADS
    nblk = steps // BLK
    return pl.pallas_call(
        factor_kernel,
        in_specs=[pl.BlockSpec(memory_space=pl.ANY)] * 2,
        out_specs=[pl.BlockSpec(memory_space=pltpu.VMEM)] * 3,
        out_shape=[
            jax.ShapeDtypeStruct((HEADS, 2 * D, D), f32),
            jax.ShapeDtypeStruct((HEADS, nblk, 2 * D, D), f32),
            jax.ShapeDtypeStruct((HEADS, steps, D), bf16),
        ],
        scratch_shapes=[pltpu.VMEM((HEADS * steps, D), bf16)] * 2
        + [pltpu.VMEM((HEADS * steps, D), f32)] * 2
        + [pltpu.SemaphoreType.DMA((2, 4))],
        compiler_params=pltpu.CompilerParams(vmem_limit_bytes=16 << 20),
        name="factor",
    )(k, v)


def chip_kernel(pos_ref, own_ref, sib_ref, *out_refs):
    x = pos_ref[0]
    core = pos_ref[2]
    half = pl.ds(pl.multiple_of(D + core * HALF, HALF), HALF)
    lower = core == 0
    for k in range(XS):
        head = lax.rem(x + k, HEADS)
        own_t, sib_t = own_ref[head, :D, :], sib_ref[head, :D, :]
        own_s, sib_s = own_ref[head, half, :], sib_ref[head, half, :]
        rows = jnp.concatenate(
            [jnp.where(lower, own_t, sib_t), jnp.where(lower, own_s, sib_s)], axis=0
        )
        moved = mm(rows, jnp.where(lower, sib_t, own_t))
        out_refs[k][:D, :] = moved[:D]
        out_refs[k][D:, :] = moved[D:] + jnp.where(lower, sib_s, own_s)


def ordered_load(slots, place, scratch):
    n = len(slots)
    for k in range(n):
        scratch[lax.rem(place + n - k, n)] = slots[k][...]


def msg_compose(rows, second):
    moved = mm(rows, second[:D])
    return jnp.concatenate([moved[:D], moved[D:] + second[D:]], axis=0)


def advance(state, second):
    return mm(state, second[:D]) + second[D:]


def prefix_totals(slots, place, total_ref, pre_ref, scratch):
    ordered_load(slots, place, scratch)
    first = scratch[0]
    tail = msg_compose(scratch[2], scratch[3])
    second = msg_compose(first, scratch[1])
    total_ref[...] = msg_compose(second, tail)
    pre_ref[0] = first
    pre_ref[1] = second
    pre_ref[2] = msg_compose(second, scratch[2])


def row_kernel(pos_ref, s0, s1, s2, s3, after_ref, total_ref, pre_ref, scratch):
    prefix_totals([s0, s1, s2, s3], pos_ref[0], total_ref, pre_ref, scratch)


def column_kernel(pos_ref, s0, s1, s2, s3, after_ref, total_ref, pre_ref, scratch):
    prefix_totals([s0, s1, s2, s3], pos_ref[1], total_ref, pre_ref, scratch)


def path_kernel(pos_ref, ypre_ref, xpre_ref, init_ref, after_ref, path_ref, start_ref, hold):
    x = pos_ref[0]
    y = pos_ref[1]
    core = pos_ref[2]
    here = ypre_ref[lax.max(y, 1) - 1]
    here = jnp.where(
        y == 0, jnp.where(iota2((MSG, D), 0) == iota2((MSG, D), 1), 1.0, 0.0), here
    )
    path_ref[0] = here
    left = wide(here)
    for i in range(XS - 1):
        moved = mm_pre(left, tall_wide(xpre_ref[i, :D, :]))
        path_ref[i + 1, :D, :] = moved[:D]
        path_ref[i + 1, D:, :] = moved[D:] + xpre_ref[i, D:, :]
    hold[...] = init_ref[x].T
    start_ref[...] = hold[pl.ds(pl.multiple_of(core * HALF, HALF), HALF), :]


def lead_kernel(pos_ref, s0, s1, s2, s3, start_ref, after_ref, lead_ref, hold):
    ordered_load([s0, s1, s2, s3], lax.rem(pos_ref[3], ZG), hold)
    tail = msg_compose(hold[2], hold[3])
    state = advance(advance(start_ref[...], hold[0]), hold[1])
    lead_ref[...] = advance(state, tail)


def fuse_kernel(pos_ref, s0, s1, s2, s3, path_ref, after_ref, fuse_ref, hold):
    g = lax.rem(pos_ref[3], ZG)
    ordered_load([s0, s1, s2, s3], g, hold)
    window = jnp.where(iota2((MSG, D), 0) == iota2((MSG, D), 1), 1.0, 0.0)
    first = hold[0]
    second = msg_compose(first, hold[1])
    third = msg_compose(second, hold[2])
    window = jnp.where(g == 1, first, window)
    window = jnp.where(g == 2, second, window)
    window = jnp.where(g == 3, third, window)
    left = wide(window)
    for i in range(XS):
        path = path_ref[i]
        moved = mm_pre(left, tall_wide(path[:D]))
        fuse_ref[i, :D, :] = moved[:D]
        fuse_ref[i, D:, :] = moved[D:] + path[D:]


def entry_kernel(pos_ref, start_ref, early_ref, fuse_ref, after_ref, o0, o1, o2, o3, scratch):
    x = pos_ref[0]
    state = jnp.where(pos_ref[3] >= ZG, early_ref[...], start_ref[...])
    left = wide(state)
    for i in range(XS):
        scratch[i] = mm_pre(left, tall_wide(fuse_ref[i, :D, :])) + fuse_ref[i, D:, :]
    for k, out in enumerate((o0, o1, o2, o3)):
        out[...] = scratch[lax.rem(x + k, XS)]


def reach_kernel(
    pos_ref, q_ref, r_ref, z_ref, sib_ref, after_ref, reach_ref, base_ref, rows, *, head
):
    tokens = reach_ref.shape[0]
    nblk = z_ref.shape[0]
    span = tokens // nblk
    rows[...] = q_ref[...].astype(f32)
    visible = iota2((span, BLK), 1) <= REFL * iota2((span, BLK), 0) + (REFL - 1)
    base = jnp.where(iota2((2 * D, D), 0) == iota2((2 * D, D), 1), 1.0, 0.0)
    sign = jnp.where(iota2((2 * D, D), 0) < D, -1.0, 1.0)
    prefixes = [jnp.where(pos_ref[2] == 1, sib_ref[...], base)]
    for b in range(nblk - 1):
        rr = jnp.concatenate([r_ref[b * BLK : (b + 1) * BLK, :]] * 2, axis=0)
        piece = base + sign * dot_nn(wide(z_ref[b]), rr)
        prefixes.append(compose(prefixes[b], piece))
    projects, locals_ = [], []
    for b in range(nblk):
        q = rows[pl.ds(head + HEADS * span * b, span, stride=HEADS), :]
        scores = dot_nt(q.astype(bf16), r_ref[b * BLK : (b + 1) * BLK, :])
        sz = mm_nt(jnp.where(visible, scores, 0.0), z_ref[b])
        projects.append(q - sz[:, :D])
        locals_.append(sz[:, D:])
    moves = [mm_nt(projects[b], prefixes[b]) for b in range(nblk)]
    for b in range(nblk):
        part = slice(b * span, (b + 1) * span)
        reach_ref[part, :] = moves[b][:, :D]
        base_ref[part, :] = moves[b][:, D:] + locals_[b]


def reach_call(pos, q, r, z, sib, after, head):
    tokens = q.shape[0] // HEADS

    def spec(array):
        rest = array.shape[1:]
        return pl.BlockSpec((None, *rest), lambda i: (head,) + (0,) * len(rest))

    return pl.pallas_call(
        functools.partial(reach_kernel, head=head),
        grid=(1,),
        in_specs=[
            pl.BlockSpec(memory_space=pltpu.SMEM),
            pl.BlockSpec(q.shape, lambda i: (0, 0)),
            spec(r),
            spec(z),
            spec(sib),
            pl.BlockSpec(memory_space=pl.ANY),
        ],
        out_specs=[pl.BlockSpec((tokens, D), lambda i: (0, 0))] * 2,
        out_shape=[jax.ShapeDtypeStruct((tokens, D), f32)] * 2,
        scratch_shapes=[pltpu.VMEM(q.shape, f32)],
        compiler_params=pltpu.CompilerParams(vmem_limit_bytes=6 << 20),
        cost_estimate=pl.CostEstimate(
            flops=400_000_000, bytes_accessed=3_000_000, transcendentals=0
        ),
        name="reach",
    )(pos, q, r, z, sib, after)


def read_kernel(pos_ref, *refs):
    reaches, bases = refs[: 2 * HEADS : 2], refs[1 : 2 * HEADS : 2]
    mine_ref, other_ref, gain_ref, out_ref, rows = refs[2 * HEADS :]
    x = pos_ref[0]
    lower = pos_ref[2] == 0
    tokens = reaches[0].shape[0]
    for h in range(HEADS):
        slot = lax.rem(x + HEADS - h, HEADS)
        mine, other = mine_ref[slot], other_ref[slot]
        state = jnp.concatenate(
            [jnp.where(lower, mine, other), jnp.where(lower, other, mine)], axis=0
        )
        read = mm_nt(reaches[h][...], state) + bases[h][...]
        scale = lax.rsqrt(jnp.mean(read * read, axis=-1, keepdims=True) + 1e-06)
        rows[pl.ds(h, tokens, stride=HEADS), :] = read * scale * gain_ref[h : h + 1, :]
    out_ref[...] = rows[...].astype(bf16)


def small_call(kernel, name, pos, arrays, outs, scratch=(), after=None, limit=4, out_dtype=f32):
    extra = [] if after is None else [after]
    return pl.pallas_call(
        kernel,
        in_specs=[pl.BlockSpec(memory_space=pltpu.SMEM)]
        + whole(*arrays)
        + [pl.BlockSpec(memory_space=pl.ANY)] * len(extra),
        out_specs=whole(*outs),
        out_shape=[jax.ShapeDtypeStruct(s, out_dtype) for s in outs],
        scratch_shapes=[pltpu.VMEM(s, f32) for s in scratch],
        compiler_params=pltpu.CompilerParams(vmem_limit_bytes=limit << 20),
        name=name,
    )(pos, *arrays, *extra)


def seq_perm(move):
    pairs = []
    for y in range(YS):
        for x in range(XS):
            for c in range(CS):
                ny, nx, nc = move(y, x, c)
                pairs.append(((y * XS + x) * CS + c, (ny * XS + nx) * CS + nc))
    return pairs


def per_device(query_rows, key_rows, value_rows, out_gain, initial_state):
    tokens = query_rows.shape[1]
    steps = tokens * REFL
    place = lax.axis_index("seq")
    seg = lax.axis_index("seg")
    core = place % CS
    x = (place // CS) % XS
    y = place // (CS * XS)
    pos = jnp.stack([x, y, core, seg]).astype(jnp.int32)

    swap = seq_perm(lambda y, x, c: (y, x, 1 - c))
    along_x = [seq_perm(lambda y, x, c, k=k: (y, (x + k) % XS, c)) for k in range(1, XS)]
    along_y = [seq_perm(lambda y, x, c, k=k: ((y + k) % YS, x, c)) for k in range(1, YS)]
    segs = 8
    along_z = [
        [(i, i // ZG * ZG + (i + k) % ZG) for i in range(segs)] for k in range(1, ZG)
    ]
    jump = [(i, (i + ZG) % segs) for i in range(segs)]

    keys = key_rows.reshape(steps * HEADS, D)
    values = value_rows.reshape(steps * HEADS, D)
    query = query_rows.reshape(tokens * HEADS, D)
    keys = pltpu.with_memory_space_constraint(keys, pltpu.HBM)
    values = pltpu.with_memory_space_constraint(values, pltpu.HBM)
    pair, z, r = factor_call(keys, values)
    sib = lax.ppermute(pair, "seq", swap)
    slots = small_call(chip_kernel, "chip", pos, [pair, sib], [(MSG, D)] * XS)
    slots = [slots[0]] + [lax.ppermute(s, "seq", p) for s, p in zip(slots[1:], along_x)]
    reaches = [reach_call(pos, query, r, z, sib, slots[0], 0)]
    total, xpre = small_call(
        row_kernel,
        "row",
        pos,
        slots,
        [(MSG, D), (XS - 1, MSG, D)],
        [(XS, MSG, D)],
        after=reaches[-1][0],
    )
    slots = [total] + [lax.ppermute(total, "seq", p) for p in along_y]
    reaches.append(reach_call(pos, query, r, z, sib, total, 1))
    total, ypre = small_call(
        column_kernel,
        "column",
        pos,
        slots,
        [(MSG, D), (YS - 1, MSG, D)],
        [(YS, MSG, D)],
        after=reaches[-1][0],
    )
    slots = [total] + [lax.ppermute(total, "seg", p) for p in along_z]
    path, start = small_call(
        path_kernel,
        "path",
        pos,
        [ypre, xpre, initial_state],
        [(XS, MSG, D), (HALF, D)],
        [(D, D)],
        after=total,
    )
    reaches.append(reach_call(pos, query, r, z, sib, path, 2))
    (lead,) = small_call(
        lead_kernel,
        "lead",
        pos,
        [*slots, start],
        [(HALF, D)],
        [(ZG, MSG, D)],
        after=reaches[-1][0],
    )
    early = lax.ppermute(lead, "seg", jump)
    (fused,) = small_call(
        fuse_kernel,
        "fuse",
        pos,
        [*slots, path],
        [(XS, MSG, D)],
        [(ZG, MSG, D)],
        after=lead,
    )
    reaches.append(reach_call(pos, query, r, z, sib, fused, 3))
    slots = small_call(
        entry_kernel,
        "entry",
        pos,
        [start, early, fused],
        [(HALF, D)] * XS,
        [(XS, HALF, D)],
        after=reaches[-1][0],
    )
    slots = [slots[0]] + [lax.ppermute(s, "seq", p) for s, p in zip(slots[1:], along_x)]
    mine = jnp.stack(slots)
    other = lax.ppermute(mine, "seq", swap)
    (out,) = small_call(
        read_kernel,
        "read",
        pos,
        [a for pair in reaches for a in pair] + [mine, other, out_gain],
        [(tokens * HEADS, D)],
        [(tokens * HEADS, D)],
        limit=8,
        out_dtype=bf16,
    )
    return out.reshape(1, tokens, HEADS, D)


def solution(mesh):
    return jax.shard_map(
        per_device,
        mesh=mesh,
        in_specs=(
            P("seg", "seq", None, None),
            P("seg", "seq", None, None, None),
            P("seg", "seq", None, None, None),
            P(),
            P(),
        ),
        out_specs=P("seg", "seq", None, None),
        check_vma=False,
    )
```

```python
import functools

import jax
import jax.numpy as jnp
from jax import lax
from jax.experimental import pallas as pl
from jax.experimental.pallas import tpu as pltpu
from jax.sharding import PartitionSpec as P

D = 128
HEADS = 4
REFL = 2
BLK = 128
XS = 4
YS = 4
CS = 2
ZG = 4
HALF = D // CS
MSG = D + HALF

f32 = jnp.float32
bf16 = jnp.bfloat16


def split(x):
    high = x.astype(bf16)
    low = (x - high.astype(f32)).astype(bf16)
    return high, low


def dot_nn(a, b):
    return lax.dot_general(a, b, (((1,), (0,)), ((), ())), preferred_element_type=f32)


def dot_nt(a, b):
    return lax.dot_general(a, b, (((1,), (1,)), ((), ())), preferred_element_type=f32)


def wide(x):
    high, low = split(x)
    return jnp.concatenate([high, low], axis=1)


def tall_wide(x):
    row = wide(x)
    return jnp.concatenate([row, row], axis=0)


def mm_pre(left_wide, right_tall):
    out = dot_nn(left_wide, right_tall)
    n = out.shape[1] // 2
    return out[:, :n] + out[:, n:]


def mm(a, b):
    return mm_pre(wide(a), tall_wide(b))


def mm_nt(a, b):
    ah, al = split(a)
    bh, bl = split(b)
    return dot_nt(ah, bh) + dot_nt(ah, bl) + dot_nt(al, bh)


def iota2(shape, dim):
    return lax.broadcasted_iota(jnp.int32, shape, dim)


def factor_kernel(k_hbm, v_hbm, m_ref, z_ref, r_ref, k_ref, v_ref, keys, values, sems):
    pieces = sems.shape[1]
    size = k_ref.shape[0] // pieces
    copies = [
        [
            pltpu.make_async_copy(
                src.at[pl.ds(i * size, size)], dst.at[pl.ds(i * size, size)], sems.at[j, i]
            )
            for i in range(pieces)
        ]
        for j, (src, dst) in enumerate(((k_hbm, k_ref), (v_hbm, v_ref)))
    ]
    for group in copies:
        for copy in group:
            copy.start()
    for i, copy in enumerate(copies[0]):
        copy.wait()
        keys[i * size : (i + 1) * size] = k_ref[i * size : (i + 1) * size].astype(f32)
    nblk = r_ref.shape[1] // BLK
    row = iota2((BLK, BLK), 0)
    col = iota2((BLK, BLK), 1)
    eye = row == col
    chains = [(h, b) for h in range(HEADS) for b in range(nblk)]
    rs, rts, vts, uppers, invs, ccols, crows = [], [], [], [], [], [], []
    for h, b in chains:
        rows = pl.ds(h + HEADS * BLK * b, BLK, stride=HEADS)
        r = keys[rows, :].astype(bf16)
        r_ref[h, b * BLK : (b + 1) * BLK, :] = r
        rt = r.T
        gram = dot_nn(r, rt)
        diag = jnp.where(eye, gram, 0.0)
        ccol = lax.rsqrt(jnp.sum(diag, axis=1, keepdims=True) + 1e-06)
        crow = lax.rsqrt(jnp.sum(diag, axis=0, keepdims=True) + 1e-06)
        upper = jnp.where(row < col, 2.0 * ccol * crow * gram, 0.0)
        pair = ((row >> 1) == (col >> 1)) & (row < col)
        inv = jnp.where(eye, 1.0, 0.0) - jnp.where(pair, upper, 0.0)
        rs.append(r)
        rts.append(rt)
        uppers.append(upper)
        invs.append(inv)
        ccols.append(ccol)
        crows.append(crow)
    for level in range(1, 7):
        off = ((row >> (level + 1)) == (col >> (level + 1))) & (
            (row >> level) < (col >> level)
        )
        talls = [tall_wide(inv) for inv in invs]
        mids = [
            mm_pre(wide(jnp.where(off, upper, 0.0)), tall) for upper, tall in zip(uppers, talls)
        ]
        invs = [inv - mm(inv, mid) for inv, mid in zip(invs, mids)]
    for i, copy in enumerate(copies[1]):
        copy.wait()
        values[i * size : (i + 1) * size] = v_ref[i * size : (i + 1) * size].astype(f32)
    for h, b in chains:
        rows = pl.ds(h + HEADS * BLK * b, BLK, stride=HEADS)
        vts.append(values[rows, :].astype(bf16).T)
    pairs = []
    base = jnp.where(iota2((2 * D, D), 0) == iota2((2 * D, D), 1), 1.0, 0.0)
    sign = jnp.where(iota2((2 * D, D), 0) < D, -1.0, 1.0)
    for i, (h, b) in enumerate(chains):
        wh, wl = split(2.0 * ccols[i] * invs[i])
        uh, ul = split(2.0 * invs[i])
        wt = dot_nn(jnp.concatenate([rts[i], rts[i]], axis=1), jnp.concatenate([wh, wl], axis=0))
        ut = dot_nn(jnp.concatenate([vts[i], vts[i]], axis=1), jnp.concatenate([uh, ul], axis=0))
        z = jnp.concatenate([wt, ut], axis=0) * crows[i]
        z_ref[h, b] = z
        rr = jnp.concatenate([rs[i], rs[i]], axis=0)
        pairs.append(base + sign * dot_nn(wide(z), rr))
    for h in range(HEADS):
        own = pairs[h * nblk : (h + 1) * nblk]
        while len(own) > 1:
            own = [compose(own[i], own[i + 1]) for i in range(0, len(own), 2)]
        m_ref[h] = own[0]


def compose(first, second):
    moved = mm(first, second[:D])
    keep = jnp.concatenate([jnp.zeros((D, D), f32), second[D:]], axis=0)
    return moved + keep


def whole(*arrays):
    return [pl.BlockSpec(memory_space=pltpu.VMEM)] * len(arrays)


def factor_call(k, v):
    steps = k.shape[0] // HEADS
    nblk = steps // BLK
    return pl.pallas_call(
        factor_kernel,
        in_specs=[pl.BlockSpec(memory_space=pl.ANY)] * 2,
        out_specs=[pl.BlockSpec(memory_space=pltpu.VMEM)] * 3,
        out_shape=[
            jax.ShapeDtypeStruct((HEADS, 2 * D, D), f32),
            jax.ShapeDtypeStruct((HEADS, nblk, 2 * D, D), f32),
            jax.ShapeDtypeStruct((HEADS, steps, D), bf16),
        ],
        scratch_shapes=[pltpu.VMEM((HEADS * steps, D), bf16)] * 2
        + [pltpu.VMEM((HEADS * steps, D), f32)] * 2
        + [pltpu.SemaphoreType.DMA((2, 4))],
        compiler_params=pltpu.CompilerParams(vmem_limit_bytes=16 << 20),
        name="factor",
    )(k, v)


def chip_kernel(pos_ref, own_ref, sib_ref, *out_refs):
    x = pos_ref[0]
    core = pos_ref[2]
    half = pl.ds(pl.multiple_of(D + core * HALF, HALF), HALF)
    lower = core == 0
    for k in range(XS):
        head = lax.rem(x + k, HEADS)
        own_t, sib_t = own_ref[head, :D, :], sib_ref[head, :D, :]
        own_s, sib_s = own_ref[head, half, :], sib_ref[head, half, :]
        rows = jnp.concatenate(
            [jnp.where(lower, own_t, sib_t), jnp.where(lower, own_s, sib_s)], axis=0
        )
        moved = mm(rows, jnp.where(lower, sib_t, own_t))
        out_refs[k][:D, :] = moved[:D]
        out_refs[k][D:, :] = moved[D:] + jnp.where(lower, sib_s, own_s)


def ordered_cyclic(slots, place, scratch):
    n = len(slots)
    for k in range(n):
        scratch[lax.rem(place + n - k, n)] = slots[k][...]


def ordered_xor(slots, place, scratch):
    for k, slot in enumerate(slots):
        scratch[place ^ k] = slot[...]


def msg_compose(rows, second):
    moved = mm(rows, second[:D])
    return jnp.concatenate([moved[:D], moved[D:] + second[D:]], axis=0)


def advance(state, second):
    return mm(state, second[:D]) + second[D:]


def write_total(total_ref, hold):
    tail = msg_compose(hold[2], hold[3])
    total_ref[...] = msg_compose(msg_compose(hold[0], hold[1]), tail)


def row_kernel(pos_ref, s0, s1, s2, s3, after_ref, total_ref, hold):
    ordered_cyclic([s0, s1, s2, s3], pos_ref[0], hold)
    write_total(total_ref, hold)


def column_kernel(pos_ref, s0, s1, s2, s3, after_ref, total_ref, hold):
    ordered_xor([s0, s1, s2, s3], pos_ref[1], hold)
    write_total(total_ref, hold)


def place_prefix(place, hold):
    first = hold[0]
    second = msg_compose(first, hold[1])
    third = msg_compose(second, hold[2])
    out = jnp.where(iota2((MSG, D), 0) == iota2((MSG, D), 1), 1.0, 0.0)
    for i, prefix in enumerate((first, second, third)):
        out = jnp.where(place == i + 1, prefix, out)
    return out


def path_kernel(pos_ref, *refs):
    xslots, yslots = refs[:4], refs[4:8]
    init_ref, after_ref, path_ref, start_ref, xhold, yhold, turn = refs[8:]
    x = pos_ref[0]
    y = pos_ref[1]
    core = pos_ref[2]
    ordered_cyclic(xslots, x, xhold)
    ordered_xor(yslots, y, yhold)
    here = place_prefix(y, yhold)
    first = xhold[0]
    second = msg_compose(first, xhold[1])
    third = msg_compose(second, xhold[2])
    path_ref[0] = here
    left = wide(here)
    for i, prefix in enumerate((first, second, third)):
        moved = mm_pre(left, tall_wide(prefix[:D]))
        path_ref[i + 1, :D, :] = moved[:D]
        path_ref[i + 1, D:, :] = moved[D:] + prefix[D:]
    turn[...] = init_ref[x].T
    start_ref[...] = turn[pl.ds(pl.multiple_of(core * HALF, HALF), HALF), :]


def lead_kernel(pos_ref, s0, s1, s2, s3, start_ref, after_ref, lead_ref, hold):
    ordered_xor([s0, s1, s2, s3], lax.rem(pos_ref[3], ZG), hold)
    tail = msg_compose(hold[2], hold[3])
    state = advance(advance(start_ref[...], hold[0]), hold[1])
    lead_ref[...] = advance(state, tail)


def fuse_kernel(pos_ref, s0, s1, s2, s3, path_ref, after_ref, fuse_ref, hold):
    g = lax.rem(pos_ref[3], ZG)
    ordered_xor([s0, s1, s2, s3], g, hold)
    window = place_prefix(g, hold)
    left = wide(window)
    for i in range(XS):
        path = path_ref[i]
        moved = mm_pre(left, tall_wide(path[:D]))
        fuse_ref[i, :D, :] = moved[:D]
        fuse_ref[i, D:, :] = moved[D:] + path[D:]


def entry_kernel(pos_ref, start_ref, early_ref, fuse_ref, after_ref, o0, o1, o2, o3, scratch):
    x = pos_ref[0]
    state = jnp.where(pos_ref[3] >= ZG, early_ref[...], start_ref[...])
    left = wide(state)
    for i in range(XS):
        scratch[i] = mm_pre(left, tall_wide(fuse_ref[i, :D, :])) + fuse_ref[i, D:, :]
    for k, out in enumerate((o0, o1, o2, o3)):
        out[...] = scratch[lax.rem(x + k, XS)]


def reach_kernel(
    pos_ref, q_ref, r_ref, z_ref, sib_ref, after_ref, reach_ref, base_ref, rows, *, head
):
    tokens = reach_ref.shape[0]
    nblk = z_ref.shape[0]
    span = tokens // nblk
    rows[...] = q_ref[...].astype(f32)
    visible = iota2((span, BLK), 1) <= REFL * iota2((span, BLK), 0) + (REFL - 1)
    base = jnp.where(iota2((2 * D, D), 0) == iota2((2 * D, D), 1), 1.0, 0.0)
    sign = jnp.where(iota2((2 * D, D), 0) < D, -1.0, 1.0)
    prefixes = [jnp.where(pos_ref[2] == 1, sib_ref[...], base)]
    for b in range(nblk - 1):
        rr = jnp.concatenate([r_ref[b * BLK : (b + 1) * BLK, :]] * 2, axis=0)
        piece = base + sign * dot_nn(wide(z_ref[b]), rr)
        prefixes.append(compose(prefixes[b], piece))
    projects, locals_ = [], []
    for b in range(nblk):
        q = rows[pl.ds(head + HEADS * span * b, span, stride=HEADS), :]
        scores = dot_nt(q.astype(bf16), r_ref[b * BLK : (b + 1) * BLK, :])
        sz = mm_nt(jnp.where(visible, scores, 0.0), z_ref[b])
        projects.append(q - sz[:, :D])
        locals_.append(sz[:, D:])
    moves = [mm_nt(projects[b], prefixes[b]) for b in range(nblk)]
    for b in range(nblk):
        part = slice(b * span, (b + 1) * span)
        reach_ref[part, :] = wide(moves[b][:, :D])
        base_ref[part, :] = moves[b][:, D:] + locals_[b]


def reach_call(pos, q, r, z, sib, after, head):
    tokens = q.shape[0] // HEADS

    def spec(array):
        rest = array.shape[1:]
        return pl.BlockSpec((None, *rest), lambda i: (head,) + (0,) * len(rest))

    return pl.pallas_call(
        functools.partial(reach_kernel, head=head),
        grid=(1,),
        in_specs=[
            pl.BlockSpec(memory_space=pltpu.SMEM),
            pl.BlockSpec(q.shape, lambda i: (0, 0)),
            spec(r),
            spec(z),
            spec(sib),
            pl.BlockSpec(memory_space=pl.ANY),
        ],
        out_specs=[
            pl.BlockSpec((tokens, 2 * D), lambda i: (0, 0)),
            pl.BlockSpec((tokens, D), lambda i: (0, 0)),
        ],
        out_shape=[
            jax.ShapeDtypeStruct((tokens, 2 * D), bf16),
            jax.ShapeDtypeStruct((tokens, D), f32),
        ],
        scratch_shapes=[pltpu.VMEM(q.shape, f32)],
        compiler_params=pltpu.CompilerParams(vmem_limit_bytes=6 << 20),
        cost_estimate=pl.CostEstimate(
            flops=400_000_000, bytes_accessed=3_000_000, transcendentals=0
        ),
        name="reach",
    )(pos, q, r, z, sib, after)


def read_kernel(pos_ref, *refs):
    reaches, bases = refs[: 2 * HEADS : 2], refs[1 : 2 * HEADS : 2]
    mine_ref, other_ref, gain_ref, out_ref, rows = refs[2 * HEADS :]
    x = pos_ref[0]
    lower = pos_ref[2] == 0
    tokens = reaches[0].shape[0]
    for h in range(HEADS):
        slot = lax.rem(x + HEADS - h, HEADS)
        mine, other = mine_ref[slot], other_ref[slot]
        state = jnp.concatenate(
            [jnp.where(lower, mine, other), jnp.where(lower, other, mine)], axis=0
        )
        high, low = split(state)
        both = jnp.concatenate([high, low], axis=0)
        moved = dot_nt(reaches[h][...], jnp.concatenate([both, both], axis=1))
        read = moved[:, :D] + moved[:, D:] + bases[h][...]
        scale = lax.rsqrt(jnp.mean(read * read, axis=-1, keepdims=True) + 1e-06)
        rows[pl.ds(h, tokens, stride=HEADS), :] = read * scale * gain_ref[h : h + 1, :]
    out_ref[...] = rows[...].astype(bf16)


def small_call(kernel, name, pos, arrays, outs, scratch=(), after=None, limit=4, out_dtype=f32):
    extra = [] if after is None else [after]
    return pl.pallas_call(
        kernel,
        in_specs=[pl.BlockSpec(memory_space=pltpu.SMEM)]
        + whole(*arrays)
        + [pl.BlockSpec(memory_space=pl.ANY)] * len(extra),
        out_specs=whole(*outs),
        out_shape=[jax.ShapeDtypeStruct(s, out_dtype) for s in outs],
        scratch_shapes=[pltpu.VMEM(s, f32) for s in scratch],
        compiler_params=pltpu.CompilerParams(vmem_limit_bytes=limit << 20),
        name=name,
    )(pos, *arrays, *extra)


def seq_perm(move):
    pairs = []
    for y in range(YS):
        for x in range(XS):
            for c in range(CS):
                ny, nx, nc = move(y, x, c)
                pairs.append(((y * XS + x) * CS + c, (ny * XS + nx) * CS + nc))
    return pairs


def per_device(query_rows, key_rows, value_rows, out_gain, initial_state):
    tokens = query_rows.shape[1]
    steps = tokens * REFL
    place = lax.axis_index("seq")
    seg = lax.axis_index("seg")
    core = place % CS
    x = (place // CS) % XS
    y = place // (CS * XS)
    pos = jnp.stack([x, y, core, seg]).astype(jnp.int32)

    swap = seq_perm(lambda y, x, c: (y, x, 1 - c))
    along_x = [seq_perm(lambda y, x, c, k=k: (y, (x + k) % XS, c)) for k in range(1, XS)]
    along_y = [seq_perm(lambda y, x, c, k=k: (y ^ k, x, c)) for k in range(1, YS)]
    segs = 8
    along_z = [[(i, i ^ k) for i in range(segs)] for k in range(1, ZG)]
    jump = [(i, segs - 1 - i) for i in range(segs)]

    keys = key_rows.reshape(steps * HEADS, D)
    values = value_rows.reshape(steps * HEADS, D)
    query = query_rows.reshape(tokens * HEADS, D)
    keys = pltpu.with_memory_space_constraint(keys, pltpu.HBM)
    values = pltpu.with_memory_space_constraint(values, pltpu.HBM)
    pair, z, r = factor_call(keys, values)
    sib = lax.ppermute(pair, "seq", swap)
    slots = small_call(chip_kernel, "chip", pos, [pair, sib], [(MSG, D)] * XS)
    slots = [slots[0]] + [lax.ppermute(s, "seq", p) for s, p in zip(slots[1:], along_x)]
    reaches = [reach_call(pos, query, r, z, sib, slots[0], 0)]
    xslots = slots
    (total,) = small_call(
        row_kernel, "row", pos, slots, [(MSG, D)], [(XS, MSG, D)], after=reaches[-1][0]
    )
    slots = [total] + [lax.ppermute(total, "seq", p) for p in along_y]
    yslots = slots
    reaches.append(reach_call(pos, query, r, z, sib, total, 1))
    (total,) = small_call(
        column_kernel, "column", pos, slots, [(MSG, D)], [(YS, MSG, D)], after=reaches[-1][0]
    )
    slots = [total] + [lax.ppermute(total, "seg", p) for p in along_z]
    path, start = small_call(
        path_kernel,
        "path",
        pos,
        [*xslots, *yslots, initial_state],
        [(XS, MSG, D), (HALF, D)],
        [(XS, MSG, D), (YS, MSG, D), (D, D)],
        after=total,
    )
    reaches.append(reach_call(pos, query, r, z, sib, path, 2))
    (lead,) = small_call(
        lead_kernel,
        "lead",
        pos,
        [*slots, start],
        [(HALF, D)],
        [(ZG, MSG, D)],
        after=reaches[-1][0],
    )
    early = lax.ppermute(lead, "seg", jump)
    (fused,) = small_call(
        fuse_kernel,
        "fuse",
        pos,
        [*slots, path],
        [(XS, MSG, D)],
        [(ZG, MSG, D)],
        after=lead,
    )
    reaches.append(reach_call(pos, query, r, z, sib, fused, 3))
    slots = small_call(
        entry_kernel,
        "entry",
        pos,
        [start, early, fused],
        [(HALF, D)] * XS,
        [(XS, HALF, D)],
        after=reaches[-1][0],
    )
    slots = [slots[0]] + [lax.ppermute(s, "seq", p) for s, p in zip(slots[1:], along_x)]
    mine = jnp.stack(slots)
    other = lax.ppermute(mine, "seq", swap)
    (out,) = small_call(
        read_kernel,
        "read",
        pos,
        [a for pair in reaches for a in pair] + [mine, other, out_gain],
        [(tokens * HEADS, D)],
        [(tokens * HEADS, D)],
        limit=8,
        out_dtype=bf16,
    )
    return out.reshape(1, tokens, HEADS, D)


def solution(mesh):
    return jax.shard_map(
        per_device,
        mesh=mesh,
        in_specs=(
            P("seg", "seq", None, None),
            P("seg", "seq", None, None, None),
            P("seg", "seq", None, None, None),
            P(),
            P(),
        ),
        out_specs=P("seg", "seq", None, None),
        check_vma=False,
    )
```

```python
import functools

import jax
import jax.numpy as jnp
from jax import lax
from jax.experimental import pallas as pl
from jax.experimental.pallas import tpu as pltpu
from jax.sharding import PartitionSpec as P

D = 128
HEADS = 4
REFL = 2
BLK = 128
XS = 4
YS = 4
CS = 2
ZG = 4
HALF = D // CS
MSG = D + HALF

f32 = jnp.float32
bf16 = jnp.bfloat16


def split(x):
    high = x.astype(bf16)
    low = (x - high.astype(f32)).astype(bf16)
    return high, low


def dot_nn(a, b):
    return lax.dot_general(a, b, (((1,), (0,)), ((), ())), preferred_element_type=f32)


def dot_nt(a, b):
    return lax.dot_general(a, b, (((1,), (1,)), ((), ())), preferred_element_type=f32)


def wide(x):
    high, low = split(x)
    return jnp.concatenate([high, low], axis=1)


def tall_wide(x):
    row = wide(x)
    return jnp.concatenate([row, row], axis=0)


def mm_pre(left_wide, right_tall):
    out = dot_nn(left_wide, right_tall)
    n = out.shape[1] // 2
    return out[:, :n] + out[:, n:]


def mm(a, b):
    return mm_pre(wide(a), tall_wide(b))


def mm_nt(a, b):
    ah, al = split(a)
    bh, bl = split(b)
    return dot_nt(ah, bh) + dot_nt(ah, bl) + dot_nt(al, bh)


def place_x():
    return lax.rem(lax.axis_index("seq") // CS, XS)


def place_y():
    return lax.axis_index("seq") // (CS * XS)


def place_core():
    return lax.rem(lax.axis_index("seq"), CS)


def place_seg():
    return lax.axis_index("seg")


def iota2(shape, dim):
    return lax.broadcasted_iota(jnp.int32, shape, dim)


def factor_kernel(k_hbm, v_hbm, m_ref, z_ref, r_ref, k_ref, v_ref, keys, values, sems):
    pieces = sems.shape[1]
    size = k_ref.shape[0] // pieces
    copies = [
        [
            pltpu.make_async_copy(
                src.at[pl.ds(i * size, size)], dst.at[pl.ds(i * size, size)], sems.at[j, i]
            )
            for i in range(pieces)
        ]
        for j, (src, dst) in enumerate(((k_hbm, k_ref), (v_hbm, v_ref)))
    ]
    for copy in copies[0]:
        copy.start()
    for i, copy in enumerate(copies[0]):
        copy.wait()
        keys[i * size : (i + 1) * size] = k_ref[i * size : (i + 1) * size].astype(f32)
    for copy in copies[1]:
        copy.start()
    nblk = r_ref.shape[1] // BLK
    row = iota2((BLK, BLK), 0)
    col = iota2((BLK, BLK), 1)
    eye = row == col
    pair = ((row >> 1) == (col >> 1)) & (row < col)
    quad = ((row >> 2) == (col >> 2)) & ((row >> 1) < (col >> 1))
    chains = [(h, b) for h in range(HEADS) for b in range(nblk)]
    rs, rts, vts, uppers, invs, ccols, crows = [], [], [], [], [], [], []
    for h, b in chains:
        rows = pl.ds(h + HEADS * BLK * b, BLK, stride=HEADS)
        r = keys[rows, :].astype(bf16)
        r_ref[h, b * BLK : (b + 1) * BLK, :] = r
        rt = r.T
        gram = dot_nn(r, rt)
        diag = jnp.where(eye, gram, 0.0)
        ccol = lax.rsqrt(jnp.sum(diag, axis=1, keepdims=True) + 1e-06)
        crow = lax.rsqrt(jnp.sum(diag, axis=0, keepdims=True) + 1e-06)
        upper = jnp.where(row < col, 2.0 * ccol * crow * gram, 0.0)
        near = jnp.where(pair, upper, 0.0)
        across = jnp.where(quad, upper, 0.0)
        erow = jnp.sum(near, axis=0, keepdims=True)
        fcol = jnp.sum(near, axis=1, keepdims=True)
        mid = across - pltpu.roll(across, 1, 1) * erow
        down = pltpu.roll(mid.reshape(BLK // 8, 8, BLK), 7, 1).reshape(BLK, BLK)
        inv = jnp.where(eye, 1.0, 0.0) - near - (mid - fcol * down)
        rs.append(r)
        rts.append(rt)
        uppers.append(upper)
        invs.append(inv)
        ccols.append(ccol)
        crows.append(crow)
    for level in range(2, 7):
        off = ((row >> (level + 1)) == (col >> (level + 1))) & (
            (row >> level) < (col >> level)
        )
        talls = [tall_wide(inv) for inv in invs]
        mids = [
            mm_pre(wide(jnp.where(off, upper, 0.0)), tall) for upper, tall in zip(uppers, talls)
        ]
        invs = [inv - mm(inv, mid) for inv, mid in zip(invs, mids)]
    for i, copy in enumerate(copies[1]):
        copy.wait()
        values[i * size : (i + 1) * size] = v_ref[i * size : (i + 1) * size].astype(f32)
    for h, b in chains:
        rows = pl.ds(h + HEADS * BLK * b, BLK, stride=HEADS)
        vts.append(values[rows, :].astype(bf16).T)
    pairs = []
    base = jnp.where(iota2((2 * D, D), 0) == iota2((2 * D, D), 1), 1.0, 0.0)
    sign = jnp.where(iota2((2 * D, D), 0) < D, -1.0, 1.0)
    for i, (h, b) in enumerate(chains):
        wh, wl = split(2.0 * ccols[i] * invs[i])
        uh, ul = split(2.0 * invs[i])
        wt = dot_nn(jnp.concatenate([rts[i], rts[i]], axis=1), jnp.concatenate([wh, wl], axis=0))
        ut = dot_nn(jnp.concatenate([vts[i], vts[i]], axis=1), jnp.concatenate([uh, ul], axis=0))
        z = jnp.concatenate([wt, ut], axis=0) * crows[i]
        z_ref[h, b] = z
        rr = jnp.concatenate([rs[i], rs[i]], axis=0)
        pairs.append(base + sign * dot_nn(wide(z), rr))
    for h in range(HEADS):
        own = pairs[h * nblk : (h + 1) * nblk]
        while len(own) > 1:
            own = [compose(own[i], own[i + 1]) for i in range(0, len(own), 2)]
        m_ref[h] = own[0]


def compose(first, second):
    moved = mm(first, second[:D])
    keep = jnp.concatenate([jnp.zeros((D, D), f32), second[D:]], axis=0)
    return moved + keep


def whole(*arrays):
    return [pl.BlockSpec(memory_space=pltpu.VMEM)] * len(arrays)


def factor_call(k, v):
    steps = k.shape[0] // HEADS
    nblk = steps // BLK
    return pl.pallas_call(
        factor_kernel,
        in_specs=[pl.BlockSpec(memory_space=pl.ANY)] * 2,
        out_specs=[pl.BlockSpec(memory_space=pltpu.VMEM)] * 3,
        out_shape=[
            jax.ShapeDtypeStruct((HEADS, 2 * D, D), f32),
            jax.ShapeDtypeStruct((HEADS, nblk, 2 * D, D), f32),
            jax.ShapeDtypeStruct((HEADS, steps, D), bf16),
        ],
        scratch_shapes=[pltpu.VMEM((HEADS * steps, D), bf16)] * 2
        + [pltpu.VMEM((HEADS * steps, D), f32)] * 2
        + [pltpu.SemaphoreType.DMA((2, 4))],
        compiler_params=pltpu.CompilerParams(vmem_limit_bytes=16 << 20),
        name="factor",
    )(k, v)


def chip_kernel(own_ref, sib_ref, *out_refs):
    x = place_x()
    core = place_core()
    half = pl.ds(pl.multiple_of(D + core * HALF, HALF), HALF)
    lower = core == 0
    for k in range(XS):
        head = lax.rem(x + k, HEADS)
        own_t, sib_t = own_ref[head, :D, :], sib_ref[head, :D, :]
        own_s, sib_s = own_ref[head, half, :], sib_ref[head, half, :]
        rows = jnp.concatenate(
            [jnp.where(lower, own_t, sib_t), jnp.where(lower, own_s, sib_s)], axis=0
        )
        moved = mm(rows, jnp.where(lower, sib_t, own_t))
        out_refs[k][:D, :] = moved[:D]
        out_refs[k][D:, :] = moved[D:] + jnp.where(lower, sib_s, own_s)


def ordered_cyclic(slots, place, scratch):
    n = len(slots)
    for k in range(n):
        scratch[lax.rem(place + n - k, n)] = slots[k][...]


def ordered_xor(slots, place, scratch):
    for k, slot in enumerate(slots):
        scratch[place ^ k] = slot[...]


def msg_compose(rows, second):
    moved = mm(rows, second[:D])
    return jnp.concatenate([moved[:D], moved[D:] + second[D:]], axis=0)


def advance(state, second):
    return mm(state, second[:D]) + second[D:]


def write_total(total_ref, hold):
    tail = msg_compose(hold[2], hold[3])
    total_ref[...] = msg_compose(msg_compose(hold[0], hold[1]), tail)


def row_kernel(s0, s1, s2, s3, after_ref, total_ref, hold):
    ordered_cyclic([s0, s1, s2, s3], place_x(), hold)
    write_total(total_ref, hold)


def column_kernel(s0, s1, s2, s3, after_ref, total_ref, hold):
    ordered_xor([s0, s1, s2, s3], place_y(), hold)
    write_total(total_ref, hold)


def place_prefix(place, hold):
    first = hold[0]
    second = msg_compose(first, hold[1])
    third = msg_compose(second, hold[2])
    out = jnp.where(iota2((MSG, D), 0) == iota2((MSG, D), 1), 1.0, 0.0)
    for i, prefix in enumerate((first, second, third)):
        out = jnp.where(place == i + 1, prefix, out)
    return out


def path_kernel(*refs):
    xslots, yslots = refs[:4], refs[4:8]
    init_ref, after_ref, path_ref, start_ref, xhold, yhold, turn = refs[8:]
    x = place_x()
    y = place_y()
    core = place_core()
    ordered_cyclic(xslots, x, xhold)
    ordered_xor(yslots, y, yhold)
    here = place_prefix(y, yhold)
    first = xhold[0]
    second = msg_compose(first, xhold[1])
    third = msg_compose(second, xhold[2])
    path_ref[0] = here
    left = wide(here)
    for i, prefix in enumerate((first, second, third)):
        moved = mm_pre(left, tall_wide(prefix[:D]))
        path_ref[i + 1, :D, :] = moved[:D]
        path_ref[i + 1, D:, :] = moved[D:] + prefix[D:]
    turn[...] = init_ref[x].T
    start_ref[...] = turn[pl.ds(pl.multiple_of(core * HALF, HALF), HALF), :]


def lead_kernel(s0, s1, s2, s3, start_ref, after_ref, lead_ref, hold):
    ordered_xor([s0, s1, s2, s3], lax.rem(place_seg(), ZG), hold)
    tail = msg_compose(hold[2], hold[3])
    state = advance(advance(start_ref[...], hold[0]), hold[1])
    lead_ref[...] = advance(state, tail)


def fuse_kernel(s0, s1, s2, s3, path_ref, after_ref, fuse_ref, hold):
    g = lax.rem(place_seg(), ZG)
    ordered_xor([s0, s1, s2, s3], g, hold)
    window = place_prefix(g, hold)
    left = wide(window)
    for i in range(XS):
        path = path_ref[i]
        moved = mm_pre(left, tall_wide(path[:D]))
        fuse_ref[i, :D, :] = moved[:D]
        fuse_ref[i, D:, :] = moved[D:] + path[D:]


def entry_kernel(start_ref, early_ref, fuse_ref, o0, o1, o2, o3, scratch):
    x = place_x()
    state = jnp.where(place_seg() >= ZG, early_ref[...], start_ref[...])
    left = wide(state)
    for i in range(XS):
        scratch[i] = mm_pre(left, tall_wide(fuse_ref[i, :D, :])) + fuse_ref[i, D:, :]
    for k, out in enumerate((o0, o1, o2, o3)):
        out[...] = scratch[lax.rem(x + k, XS)]


def reach_kernel(
    q_ref, r_ref, z_ref, sib_ref, after_ref, reach_ref, base_ref, rows, *, head
):
    tokens = reach_ref.shape[0]
    nblk = z_ref.shape[0]
    span = tokens // nblk
    rows[...] = q_ref[...].astype(f32)
    visible = iota2((span, BLK), 1) <= REFL * iota2((span, BLK), 0) + (REFL - 1)
    base = jnp.where(iota2((2 * D, D), 0) == iota2((2 * D, D), 1), 1.0, 0.0)
    sign = jnp.where(iota2((2 * D, D), 0) < D, -1.0, 1.0)
    prefixes = [jnp.where(place_core() == 1, sib_ref[...], base)]
    for b in range(nblk - 1):
        rr = jnp.concatenate([r_ref[b * BLK : (b + 1) * BLK, :]] * 2, axis=0)
        piece = base + sign * dot_nn(wide(z_ref[b]), rr)
        prefixes.append(compose(prefixes[b], piece))
    projects, locals_ = [], []
    for b in range(nblk):
        q = rows[pl.ds(head + HEADS * span * b, span, stride=HEADS), :]
        scores = dot_nt(q.astype(bf16), r_ref[b * BLK : (b + 1) * BLK, :])
        sz = mm_nt(jnp.where(visible, scores, 0.0), z_ref[b])
        projects.append(q - sz[:, :D])
        locals_.append(sz[:, D:])
    moves = [mm_nt(projects[b], prefixes[b]) for b in range(nblk)]
    for b in range(nblk):
        part = slice(b * span, (b + 1) * span)
        reach_ref[part, :] = wide(moves[b][:, :D])
        base_ref[part, :] = moves[b][:, D:] + locals_[b]


def reach_call(q, r, z, sib, after, head):
    tokens = q.shape[0] // HEADS

    def spec(array):
        rest = array.shape[1:]
        return pl.BlockSpec((None, *rest), lambda i: (head,) + (0,) * len(rest))

    return pl.pallas_call(
        functools.partial(reach_kernel, head=head),
        grid=(1,),
        in_specs=[
            pl.BlockSpec(q.shape, lambda i: (0, 0)),
            spec(r),
            spec(z),
            spec(sib),
            pl.BlockSpec(memory_space=pl.ANY),
        ],
        out_specs=[
            pl.BlockSpec((tokens, 2 * D), lambda i: (0, 0)),
            pl.BlockSpec((tokens, D), lambda i: (0, 0)),
        ],
        out_shape=[
            jax.ShapeDtypeStruct((tokens, 2 * D), bf16),
            jax.ShapeDtypeStruct((tokens, D), f32),
        ],
        scratch_shapes=[pltpu.VMEM(q.shape, f32)],
        compiler_params=pltpu.CompilerParams(vmem_limit_bytes=6 << 20),
        cost_estimate=pl.CostEstimate(
            flops=400_000_000, bytes_accessed=3_000_000, transcendentals=0
        ),
        name="reach",
    )(q, r, z, sib, after)


def read_kernel(*refs):
    reaches, bases = refs[: 2 * HEADS : 2], refs[1 : 2 * HEADS : 2]
    mine_ref, other_ref, gain_ref, out_hbm, rows, out, sems = refs[2 * HEADS :]
    x = place_x()
    lower = place_core() == 0
    rights = []
    for h in range(HEADS):
        slot = lax.rem(x + HEADS - h, HEADS)
        mine, other = mine_ref[slot], other_ref[slot]
        state = jnp.concatenate(
            [jnp.where(lower, mine, other), jnp.where(lower, other, mine)], axis=0
        )
        both = jnp.concatenate(split(state), axis=0)
        rights.append(jnp.concatenate([both, both], axis=1))
    pieces = sems.shape[0]
    span = reaches[0].shape[0] // pieces
    copies = []
    for i in range(pieces):
        part = slice(i * span, (i + 1) * span)
        for h in range(HEADS):
            moved = dot_nt(reaches[h][part, :], rights[h])
            read = moved[:, :D] + moved[:, D:] + bases[h][part, :]
            scale = lax.rsqrt(jnp.mean(read * read, axis=-1, keepdims=True) + 1e-06)
            rows[pl.ds(i * span * HEADS + h, span, stride=HEADS), :] = (
                read * scale * gain_ref[h : h + 1, :]
            )
        block = pl.ds(i * span * HEADS, span * HEADS)
        out[block, :] = rows[block, :].astype(bf16)
        copies.append(pltpu.make_async_copy(out.at[block], out_hbm.at[block], sems.at[i]))
        copies[-1].start()
    for copy in copies:
        copy.wait()


def read_call(arrays, tokens):
    shape = (tokens * HEADS, D)
    return pl.pallas_call(
        read_kernel,
        in_specs=whole(*arrays),
        out_specs=pl.BlockSpec(memory_space=pl.ANY),
        out_shape=jax.ShapeDtypeStruct(shape, bf16),
        scratch_shapes=[
            pltpu.VMEM(shape, f32),
            pltpu.VMEM(shape, bf16),
            pltpu.SemaphoreType.DMA((2,)),
        ],
        compiler_params=pltpu.CompilerParams(vmem_limit_bytes=8 << 20),
        name="read",
    )(*arrays)


def small_call(kernel, name, arrays, outs, scratch=(), after=None, limit=4, out_dtype=f32):
    extra = [] if after is None else [after]
    return pl.pallas_call(
        kernel,
        in_specs=whole(*arrays)
        + [pl.BlockSpec(memory_space=pl.ANY)] * len(extra),
        out_specs=whole(*outs),
        out_shape=[jax.ShapeDtypeStruct(s, out_dtype) for s in outs],
        scratch_shapes=[pltpu.VMEM(s, f32) for s in scratch],
        compiler_params=pltpu.CompilerParams(vmem_limit_bytes=limit << 20),
        name=name,
    )(*arrays, *extra)


def seq_perm(move):
    pairs = []
    for y in range(YS):
        for x in range(XS):
            for c in range(CS):
                ny, nx, nc = move(y, x, c)
                pairs.append(((y * XS + x) * CS + c, (ny * XS + nx) * CS + nc))
    return pairs


def per_device(query_rows, key_rows, value_rows, out_gain, initial_state):
    tokens = query_rows.shape[1]
    steps = tokens * REFL
    swap = seq_perm(lambda y, x, c: (y, x, 1 - c))
    along_x = [seq_perm(lambda y, x, c, k=k: (y, (x + k) % XS, c)) for k in range(1, XS)]
    along_y = [seq_perm(lambda y, x, c, k=k: (y ^ k, x, c)) for k in range(1, YS)]
    segs = 8
    along_z = [[(i, i ^ k) for i in range(segs)] for k in range(1, ZG)]
    jump = [(i, segs - 1 - i) for i in range(segs)]

    keys = key_rows.reshape(steps * HEADS, D)
    values = value_rows.reshape(steps * HEADS, D)
    query = query_rows.reshape(tokens * HEADS, D)
    keys = pltpu.with_memory_space_constraint(keys, pltpu.HBM)
    values = pltpu.with_memory_space_constraint(values, pltpu.HBM)
    pair, z, r = factor_call(keys, values)
    sib = lax.ppermute(pair, "seq", swap)
    slots = small_call(chip_kernel, "chip", [pair, sib], [(MSG, D)] * XS)
    slots = [slots[0]] + [lax.ppermute(s, "seq", p) for s, p in zip(slots[1:], along_x)]
    reaches = [reach_call(query, r, z, sib, slots[0], 0)]
    xslots = slots
    (total,) = small_call(
        row_kernel, "row", slots, [(MSG, D)], [(XS, MSG, D)], after=reaches[-1][0]
    )
    slots = [total] + [lax.ppermute(total, "seq", p) for p in along_y]
    yslots = slots
    reaches.append(reach_call(query, r, z, sib, total, 1))
    (total,) = small_call(
        column_kernel, "column", slots, [(MSG, D)], [(YS, MSG, D)], after=reaches[-1][0]
    )
    slots = [total] + [lax.ppermute(total, "seg", p) for p in along_z]
    path, start = small_call(
        path_kernel,
        "path",
        [*xslots, *yslots, initial_state],
        [(XS, MSG, D), (HALF, D)],
        [(XS, MSG, D), (YS, MSG, D), (D, D)],
        after=total,
    )
    reaches.append(reach_call(query, r, z, sib, path, 2))
    (lead,) = small_call(
        lead_kernel,
        "lead",
        [*slots, start],
        [(HALF, D)],
        [(ZG, MSG, D)],
        after=reaches[-1][0],
    )
    early = lax.ppermute(lead, "seg", jump)
    (fused,) = small_call(
        fuse_kernel,
        "fuse",
        [*slots, path],
        [(XS, MSG, D)],
        [(ZG, MSG, D)],
        after=lead,
    )
    slots = small_call(
        entry_kernel,
        "entry",
        [start, early, fused],
        [(HALF, D)] * XS,
        [(XS, HALF, D)],
    )
    slots = [slots[0]] + [lax.ppermute(s, "seq", p) for s, p in zip(slots[1:], along_x)]
    reaches.append(reach_call(query, r, z, sib, slots[0], 3))
    *slots, last = lax.optimization_barrier((*slots, reaches[-1][0]))
    reaches[-1] = (last, reaches[-1][1])
    mine = jnp.stack(slots)
    other = lax.ppermute(mine, "seq", swap)
    arrays = [a for pair in reaches for a in pair] + [mine, other, out_gain]
    out = read_call(arrays, tokens)
    return out.reshape(1, tokens, HEADS, D)


def solution(mesh):
    return jax.shard_map(
        per_device,
        mesh=mesh,
        in_specs=(
            P("seg", "seq", None, None),
            P("seg", "seq", None, None, None),
            P("seg", "seq", None, None, None),
            P(),
            P(),
        ),
        out_specs=P("seg", "seq", None, None),
        check_vma=False,
    )
```

```python
import functools

import jax
import jax.numpy as jnp
from jax import lax
from jax.experimental import pallas as pl
from jax.experimental.pallas import tpu as pltpu
from jax.sharding import PartitionSpec as P

D = 128
HEADS = 4
REFL = 2
BLK = 128
XS = 4
YS = 4
CS = 2
ZG = 4
MSG = 2 * D

f32 = jnp.float32
bf16 = jnp.bfloat16


def split(x):
    high = x.astype(bf16)
    low = (x - high.astype(f32)).astype(bf16)
    return high, low


def dot_nn(a, b):
    return lax.dot_general(a, b, (((1,), (0,)), ((), ())), preferred_element_type=f32)


def dot_nt(a, b):
    return lax.dot_general(a, b, (((1,), (1,)), ((), ())), preferred_element_type=f32)


def wide(x):
    high, low = split(x)
    return jnp.concatenate([high, low], axis=1)


def tall_wide(x):
    row = wide(x)
    return jnp.concatenate([row, row], axis=0)


def mm_pre(left_wide, right_tall):
    out = dot_nn(left_wide, right_tall)
    n = out.shape[1] // 2
    return out[:, :n] + out[:, n:]


def mm(a, b):
    return mm_pre(wide(a), tall_wide(b))


def mm_nt(a, b):
    ah, al = split(a)
    bh, bl = split(b)
    return dot_nt(ah, bh) + dot_nt(ah, bl) + dot_nt(al, bh)


def place_x():
    return lax.rem(lax.axis_index("seq") // CS, XS)


def place_y():
    return lax.axis_index("seq") // (CS * XS)


def place_core():
    return lax.rem(lax.axis_index("seq"), CS)


def place_seg():
    return lax.axis_index("seg")


def iota2(shape, dim):
    return lax.broadcasted_iota(jnp.int32, shape, dim)


def factor_kernel(k_hbm, v_hbm, m_ref, z_ref, r_ref, k_ref, v_ref, keys, values, sems):
    pieces = sems.shape[1]
    size = k_ref.shape[0] // pieces
    copies = [
        [
            pltpu.make_async_copy(
                src.at[pl.ds(i * size, size)], dst.at[pl.ds(i * size, size)], sems.at[j, i]
            )
            for i in range(pieces)
        ]
        for j, (src, dst) in enumerate(((k_hbm, k_ref), (v_hbm, v_ref)))
    ]
    for copy in copies[0]:
        copy.start()
    for i, copy in enumerate(copies[0]):
        copy.wait()
        keys[i * size : (i + 1) * size] = k_ref[i * size : (i + 1) * size].astype(f32)
    for copy in copies[1]:
        copy.start()
    nblk = r_ref.shape[1] // BLK
    row = iota2((BLK, BLK), 0)
    col = iota2((BLK, BLK), 1)
    eye = row == col
    pair = ((row >> 1) == (col >> 1)) & (row < col)
    quad = ((row >> 2) == (col >> 2)) & ((row >> 1) < (col >> 1))
    chains = [(h, b) for h in range(HEADS) for b in range(nblk)]
    rs, rts, vts, uppers, invs, ccols, crows = [], [], [], [], [], [], []
    for h, b in chains:
        rows = pl.ds(h + HEADS * BLK * b, BLK, stride=HEADS)
        r = keys[rows, :].astype(bf16)
        r_ref[h, b * BLK : (b + 1) * BLK, :] = r
        rt = r.T
        gram = dot_nn(r, rt)
        diag = jnp.where(eye, gram, 0.0)
        ccol = lax.rsqrt(jnp.sum(diag, axis=1, keepdims=True) + 1e-06)
        crow = lax.rsqrt(jnp.sum(diag, axis=0, keepdims=True) + 1e-06)
        upper = jnp.where(row < col, 2.0 * ccol * crow * gram, 0.0)
        near = jnp.where(pair, upper, 0.0)
        across = jnp.where(quad, upper, 0.0)
        erow = jnp.sum(near, axis=0, keepdims=True)
        fcol = jnp.sum(near, axis=1, keepdims=True)
        mid = across - pltpu.roll(across, 1, 1) * erow
        down = pltpu.roll(mid.reshape(BLK // 8, 8, BLK), 7, 1).reshape(BLK, BLK)
        inv = jnp.where(eye, 1.0, 0.0) - near - (mid - fcol * down)
        rs.append(r)
        rts.append(rt)
        uppers.append(upper)
        invs.append(inv)
        ccols.append(ccol)
        crows.append(crow)
    for level in range(2, 7):
        off = ((row >> (level + 1)) == (col >> (level + 1))) & (
            (row >> level) < (col >> level)
        )
        talls = [tall_wide(inv) for inv in invs]
        mids = [
            mm_pre(wide(jnp.where(off, upper, 0.0)), tall) for upper, tall in zip(uppers, talls)
        ]
        invs = [inv - mm(inv, mid) for inv, mid in zip(invs, mids)]
    for i, copy in enumerate(copies[1]):
        copy.wait()
        values[i * size : (i + 1) * size] = v_ref[i * size : (i + 1) * size].astype(f32)
    for h, b in chains:
        rows = pl.ds(h + HEADS * BLK * b, BLK, stride=HEADS)
        vts.append(values[rows, :].astype(bf16).T)
    pairs = []
    base = jnp.where(iota2((2 * D, D), 0) == iota2((2 * D, D), 1), 1.0, 0.0)
    sign = jnp.where(iota2((2 * D, D), 0) < D, -1.0, 1.0)
    for i, (h, b) in enumerate(chains):
        wh, wl = split(2.0 * ccols[i] * invs[i])
        uh, ul = split(2.0 * invs[i])
        wt = dot_nn(jnp.concatenate([rts[i], rts[i]], axis=1), jnp.concatenate([wh, wl], axis=0))
        ut = dot_nn(jnp.concatenate([vts[i], vts[i]], axis=1), jnp.concatenate([uh, ul], axis=0))
        z = jnp.concatenate([wt, ut], axis=0) * crows[i]
        z_ref[h, b] = z
        rr = jnp.concatenate([rs[i], rs[i]], axis=0)
        pairs.append(base + sign * dot_nn(wide(z), rr))
    for h in range(HEADS):
        own = pairs[h * nblk : (h + 1) * nblk]
        while len(own) > 1:
            own = [compose(own[i], own[i + 1]) for i in range(0, len(own), 2)]
        m_ref[h] = own[0]


def compose(first, second):
    moved = mm(first, second[:D])
    keep = jnp.concatenate([jnp.zeros((D, D), f32), second[D:]], axis=0)
    return moved + keep


def whole(*arrays):
    return [pl.BlockSpec(memory_space=pltpu.VMEM)] * len(arrays)


def factor_call(k, v):
    steps = k.shape[0] // HEADS
    nblk = steps // BLK
    return pl.pallas_call(
        factor_kernel,
        in_specs=[pl.BlockSpec(memory_space=pl.ANY)] * 2,
        out_specs=[pl.BlockSpec(memory_space=pltpu.VMEM)] * 3,
        out_shape=[
            jax.ShapeDtypeStruct((HEADS, 2 * D, D), f32),
            jax.ShapeDtypeStruct((HEADS, nblk, 2 * D, D), f32),
            jax.ShapeDtypeStruct((HEADS, steps, D), bf16),
        ],
        scratch_shapes=[pltpu.VMEM((HEADS * steps, D), bf16)] * 2
        + [pltpu.VMEM((HEADS * steps, D), f32)] * 2
        + [pltpu.SemaphoreType.DMA((2, 4))],
        compiler_params=pltpu.CompilerParams(vmem_limit_bytes=16 << 20),
        name="factor",
    )(k, v)


def chip_kernel(own_ref, sib_ref, *out_refs):
    x = place_x()
    for k in range(XS):
        head = lax.rem(x + k, HEADS)
        out_refs[k][...] = compose(sib_ref[head], own_ref[head])


def ordered_cyclic(slots, place, scratch):
    n = len(slots)
    for k in range(n):
        scratch[lax.rem(place + n - k, n)] = slots[k][...]


def ordered_xor(slots, place, scratch):
    for k, slot in enumerate(slots):
        scratch[place ^ k] = slot[...]


def msg_compose(rows, second):
    moved = mm(rows, second[:D])
    return jnp.concatenate([moved[:D], moved[D:] + second[D:]], axis=0)


def advance(state, second):
    return mm(state, second[:D]) + second[D:]


def write_total(total_ref, hold):
    tail = msg_compose(hold[2], hold[3])
    total_ref[...] = msg_compose(msg_compose(hold[0], hold[1]), tail)


def row_kernel(s0, s1, s2, s3, after_ref, total_ref, hold):
    ordered_cyclic([s0, s1, s2, s3], place_x(), hold)
    write_total(total_ref, hold)


def column_kernel(s0, s1, s2, s3, after_ref, total_ref, hold):
    ordered_xor([s0, s1, s2, s3], place_y(), hold)
    write_total(total_ref, hold)


def place_prefix(place, hold):
    first = hold[0]
    second = msg_compose(first, hold[1])
    third = msg_compose(second, hold[2])
    out = jnp.where(iota2((MSG, D), 0) == iota2((MSG, D), 1), 1.0, 0.0)
    for i, prefix in enumerate((first, second, third)):
        out = jnp.where(place == i + 1, prefix, out)
    return out


def path_kernel(*refs):
    xslots, yslots = refs[:4], refs[4:8]
    init_ref, after_ref, path_ref, start_ref, xhold, yhold = refs[8:]
    x = place_x()
    y = place_y()
    ordered_cyclic(xslots, x, xhold)
    ordered_xor(yslots, y, yhold)
    here = place_prefix(y, yhold)
    first = xhold[0]
    second = msg_compose(first, xhold[1])
    third = msg_compose(second, xhold[2])
    path_ref[0] = here
    left = wide(here)
    for i, prefix in enumerate((first, second, third)):
        moved = mm_pre(left, tall_wide(prefix[:D]))
        path_ref[i + 1, :D, :] = moved[:D]
        path_ref[i + 1, D:, :] = moved[D:] + prefix[D:]
    start_ref[...] = init_ref[x].T


def lead_kernel(s0, s1, s2, s3, start_ref, after_ref, lead_ref, hold):
    ordered_xor([s0, s1, s2, s3], lax.rem(place_seg(), ZG), hold)
    tail = msg_compose(hold[2], hold[3])
    state = advance(advance(start_ref[...], hold[0]), hold[1])
    lead_ref[...] = advance(state, tail)


def fuse_kernel(s0, s1, s2, s3, path_ref, after_ref, fuse_ref, hold):
    g = lax.rem(place_seg(), ZG)
    ordered_xor([s0, s1, s2, s3], g, hold)
    window = place_prefix(g, hold)
    left = wide(window)
    for i in range(XS):
        path = path_ref[i]
        moved = mm_pre(left, tall_wide(path[:D]))
        fuse_ref[i, :D, :] = moved[:D]
        fuse_ref[i, D:, :] = moved[D:] + path[D:]


def entry_kernel(start_ref, early_ref, fuse_ref, o0, o1, o2, o3, scratch):
    x = place_x()
    state = jnp.where(place_seg() >= ZG, early_ref[...], start_ref[...])
    left = wide(state)
    for i in range(XS):
        scratch[i] = mm_pre(left, tall_wide(fuse_ref[i, :D, :])) + fuse_ref[i, D:, :]
    for k, out in enumerate((o0, o1, o2, o3)):
        out[...] = scratch[lax.rem(x + k, XS)]


def reach_kernel(
    q_ref, r_ref, z_ref, sib_ref, after_ref, reach_ref, base_ref, rows, *, head
):
    tokens = reach_ref.shape[0]
    nblk = z_ref.shape[0]
    span = tokens // nblk
    rows[...] = q_ref[...].astype(f32)
    visible = iota2((span, BLK), 1) <= REFL * iota2((span, BLK), 0) + (REFL - 1)
    base = jnp.where(iota2((2 * D, D), 0) == iota2((2 * D, D), 1), 1.0, 0.0)
    sign = jnp.where(iota2((2 * D, D), 0) < D, -1.0, 1.0)
    prefixes = [jnp.where(place_core() == 1, sib_ref[...], base)]
    for b in range(nblk - 1):
        rr = jnp.concatenate([r_ref[b * BLK : (b + 1) * BLK, :]] * 2, axis=0)
        piece = base + sign * dot_nn(wide(z_ref[b]), rr)
        prefixes.append(compose(prefixes[b], piece))
    projects, locals_ = [], []
    for b in range(nblk):
        q = rows[pl.ds(head + HEADS * span * b, span, stride=HEADS), :]
        scores = dot_nt(q.astype(bf16), r_ref[b * BLK : (b + 1) * BLK, :])
        sz = mm_nt(jnp.where(visible, scores, 0.0), z_ref[b])
        projects.append(q - sz[:, :D])
        locals_.append(sz[:, D:])
    moves = [mm_nt(projects[b], prefixes[b]) for b in range(nblk)]
    for b in range(nblk):
        part = slice(b * span, (b + 1) * span)
        reach_ref[part, :] = wide(moves[b][:, :D])
        base_ref[part, :] = moves[b][:, D:] + locals_[b]


def reach_call(q, r, z, sib, after, head):
    tokens = q.shape[0] // HEADS

    def spec(array):
        rest = array.shape[1:]
        return pl.BlockSpec((None, *rest), lambda i: (head,) + (0,) * len(rest))

    return pl.pallas_call(
        functools.partial(reach_kernel, head=head),
        grid=(1,),
        in_specs=[
            pl.BlockSpec(q.shape, lambda i: (0, 0)),
            spec(r),
            spec(z),
            spec(sib),
            pl.BlockSpec(memory_space=pl.ANY),
        ],
        out_specs=[
            pl.BlockSpec((tokens, 2 * D), lambda i: (0, 0)),
            pl.BlockSpec((tokens, D), lambda i: (0, 0)),
        ],
        out_shape=[
            jax.ShapeDtypeStruct((tokens, 2 * D), bf16),
            jax.ShapeDtypeStruct((tokens, D), f32),
        ],
        scratch_shapes=[pltpu.VMEM(q.shape, f32)],
        compiler_params=pltpu.CompilerParams(vmem_limit_bytes=6 << 20),
        cost_estimate=pl.CostEstimate(
            flops=400_000_000, bytes_accessed=3_000_000, transcendentals=0
        ),
        name="reach",
    )(q, r, z, sib, after)


def read_kernel(*refs):
    reaches, bases = refs[: 2 * HEADS : 2], refs[1 : 2 * HEADS : 2]
    refs = refs[2 * HEADS :]
    mine, other = refs[:HEADS], refs[HEADS : 2 * HEADS]
    gain_ref, out_hbm, states, rows, out, sems = refs[2 * HEADS :]
    x = place_x()

    @pl.when(place_core() == 0)
    def _():
        ordered_cyclic(other, x, states)

    @pl.when(place_core() != 0)
    def _():
        ordered_cyclic(mine, x, states)

    rights = []
    for h in range(HEADS):
        both = jnp.concatenate(split(states[h]), axis=0)
        rights.append(jnp.concatenate([both, both], axis=1))
    pieces = sems.shape[0]
    span = reaches[0].shape[0] // pieces
    copies = []
    for i in range(pieces):
        part = slice(i * span, (i + 1) * span)
        for h in range(HEADS):
            moved = dot_nt(reaches[h][part, :], rights[h])
            read = moved[:, :D] + moved[:, D:] + bases[h][part, :]
            scale = lax.rsqrt(jnp.mean(read * read, axis=-1, keepdims=True) + 1e-06)
            rows[pl.ds(i * span * HEADS + h, span, stride=HEADS), :] = (
                read * scale * gain_ref[h : h + 1, :]
            )
        block = pl.ds(i * span * HEADS, span * HEADS)
        out[block, :] = rows[block, :].astype(bf16)
        copies.append(pltpu.make_async_copy(out.at[block], out_hbm.at[block], sems.at[i]))
        copies[-1].start()
    for copy in copies:
        copy.wait()


def read_call(arrays, tokens):
    shape = (tokens * HEADS, D)
    return pl.pallas_call(
        read_kernel,
        in_specs=whole(*arrays),
        out_specs=pl.BlockSpec(memory_space=pl.ANY),
        out_shape=jax.ShapeDtypeStruct(shape, bf16),
        scratch_shapes=[
            pltpu.VMEM((HEADS, D, D), f32),
            pltpu.VMEM(shape, f32),
            pltpu.VMEM(shape, bf16),
            pltpu.SemaphoreType.DMA((2,)),
        ],
        compiler_params=pltpu.CompilerParams(vmem_limit_bytes=8 << 20),
        name="read",
    )(*arrays)


def small_call(kernel, name, arrays, outs, scratch=(), after=None, limit=4, out_dtype=f32):
    extra = [] if after is None else [after]
    return pl.pallas_call(
        kernel,
        in_specs=whole(*arrays)
        + [pl.BlockSpec(memory_space=pl.ANY)] * len(extra),
        out_specs=whole(*outs),
        out_shape=[jax.ShapeDtypeStruct(s, out_dtype) for s in outs],
        scratch_shapes=[pltpu.VMEM(s, f32) for s in scratch],
        compiler_params=pltpu.CompilerParams(vmem_limit_bytes=limit << 20),
        name=name,
    )(*arrays, *extra)


def seat(y, x, c):
    return (y * XS + x) * CS + c


def plane_perm(move):
    last = CS - 1
    return [
        (seat(y, x, last), seat(*move(y, x), last)) for y in range(YS) for x in range(XS)
    ]


def depth_perm(segs, move):
    last = CS - 1
    return [
        (seat(y, x, last) * segs + g, seat(y, x, last) * segs + move(g))
        for y in range(YS)
        for x in range(XS)
        for g in range(segs)
    ]


def chip_perm(source):
    return [
        (seat(y, x, source), seat(y, x, 1 - source)) for y in range(YS) for x in range(XS)
    ]


def per_device(query_rows, key_rows, value_rows, out_gain, initial_state):
    tokens = query_rows.shape[1]
    steps = tokens * REFL
    up, down = chip_perm(0), chip_perm(1)
    along_x = [plane_perm(lambda y, x, k=k: (y, (x + k) % XS)) for k in range(1, XS)]
    along_y = [plane_perm(lambda y, x, k=k: (y ^ k, x)) for k in range(1, YS)]
    segs = lax.axis_size("seg")
    along_z = [depth_perm(segs, lambda g, k=k: g ^ k) for k in range(1, ZG)]
    jump = depth_perm(segs, lambda g: segs - 1 - g)

    keys = key_rows.reshape(steps * HEADS, D)
    values = value_rows.reshape(steps * HEADS, D)
    query = query_rows.reshape(tokens * HEADS, D)
    keys = pltpu.with_memory_space_constraint(keys, pltpu.HBM)
    values = pltpu.with_memory_space_constraint(values, pltpu.HBM)
    pair, z, r = factor_call(keys, values)
    sib = lax.ppermute(pair, "seq", up)
    slots = small_call(chip_kernel, "chip", [pair, sib], [(MSG, D)] * XS)
    slots = [slots[0]] + [lax.ppermute(s, "seq", p) for s, p in zip(slots[1:], along_x)]
    reaches = [reach_call(query, r, z, sib, slots[0], 0)]
    xslots = slots
    (total,) = small_call(
        row_kernel, "row", slots, [(MSG, D)], [(XS, MSG, D)], after=reaches[-1][0]
    )
    slots = [total] + [lax.ppermute(total, "seq", p) for p in along_y]
    yslots = slots
    reaches.append(reach_call(query, r, z, sib, total, 1))
    (total,) = small_call(
        column_kernel, "column", slots, [(MSG, D)], [(YS, MSG, D)], after=reaches[-1][0]
    )
    slots = [total] + [lax.ppermute(total, ("seq", "seg"), p) for p in along_z]
    path, start = small_call(
        path_kernel,
        "path",
        [*xslots, *yslots, initial_state],
        [(XS, MSG, D), (D, D)],
        [(XS, MSG, D), (YS, MSG, D)],
        after=total,
    )
    reaches.append(reach_call(query, r, z, sib, path, 2))
    (lead,) = small_call(
        lead_kernel,
        "lead",
        [*slots, start],
        [(D, D)],
        [(ZG, MSG, D)],
        after=reaches[-1][0],
    )
    early = lax.ppermute(lead, ("seq", "seg"), jump)
    (fused,) = small_call(
        fuse_kernel,
        "fuse",
        [*slots, path],
        [(XS, MSG, D)],
        [(ZG, MSG, D)],
        after=lead,
    )
    slots = small_call(
        entry_kernel,
        "entry",
        [start, early, fused],
        [(D, D)] * XS,
        [(XS, D, D)],
    )
    slots = [slots[0]] + [lax.ppermute(s, "seq", p) for s, p in zip(slots[1:], along_x)]
    reaches.append(reach_call(query, r, z, sib, slots[0], 3))
    last = reaches[-1][0]
    for k in range(1, XS):
        slots[k], last = lax.optimization_barrier((slots[k], last))
    reaches[-1] = (last, reaches[-1][1])
    others = [lax.ppermute(s, "seq", down) for s in slots]
    arrays = [a for pair in reaches for a in pair] + [*slots, *others, out_gain]
    out = read_call(arrays, tokens)
    return out.reshape(1, tokens, HEADS, D)


def solution(mesh):
    return jax.shard_map(
        per_device,
        mesh=mesh,
        in_specs=(
            P("seg", "seq", None, None),
            P("seg", "seq", None, None, None),
            P("seg", "seq", None, None, None),
            P(),
            P(),
        ),
        out_specs=P("seg", "seq", None, None),
        check_vma=False,
    )
```

```python
import functools

import jax
import jax.numpy as jnp
from jax import lax
from jax.experimental import pallas as pl
from jax.experimental.pallas import tpu as pltpu
from jax.sharding import PartitionSpec as P

D = 128
HEADS = 4
REFL = 2
BLK = 128
XS = 4
YS = 4
CS = 2
ZG = 4
MSG = 2 * D

f32 = jnp.float32
bf16 = jnp.bfloat16


def split(x):
    high = x.astype(bf16)
    low = (x - high.astype(f32)).astype(bf16)
    return high, low


def dot_nn(a, b):
    return lax.dot_general(a, b, (((1,), (0,)), ((), ())), preferred_element_type=f32)


def dot_nt(a, b):
    return lax.dot_general(a, b, (((1,), (1,)), ((), ())), preferred_element_type=f32)


def wide(x):
    high, low = split(x)
    return jnp.concatenate([high, low], axis=1)


def tall_wide(x):
    row = wide(x)
    return jnp.concatenate([row, row], axis=0)


def mm_pre(left_wide, right_tall):
    out = dot_nn(left_wide, right_tall)
    n = out.shape[1] // 2
    return out[:, :n] + out[:, n:]


def mm(a, b):
    return mm_pre(wide(a), tall_wide(b))


def mm_nt(a, b):
    ah, al = split(a)
    bh, bl = split(b)
    return dot_nt(ah, bh) + dot_nt(ah, bl) + dot_nt(al, bh)


def place_x():
    return lax.rem(lax.axis_index("seq") // CS, XS)


def place_y():
    return lax.axis_index("seq") // (CS * XS)


def place_core():
    return lax.rem(lax.axis_index("seq"), CS)


def place_seg():
    return lax.axis_index("seg")


def iota2(shape, dim):
    return lax.broadcasted_iota(jnp.int32, shape, dim)


def factor_kernel(k_hbm, v_hbm, m_ref, z_ref, r_ref, k_ref, v_ref, keys, values, sems):
    pieces = sems.shape[1]
    size = k_ref.shape[0] // pieces
    copies = [
        [
            pltpu.make_async_copy(
                src.at[pl.ds(i * size, size)], dst.at[pl.ds(i * size, size)], sems.at[j, i]
            )
            for i in range(pieces)
        ]
        for j, (src, dst) in enumerate(((k_hbm, k_ref), (v_hbm, v_ref)))
    ]
    for copy in copies[0]:
        copy.start()
    for i, copy in enumerate(copies[0]):
        copy.wait()
        keys[i * size : (i + 1) * size] = k_ref[i * size : (i + 1) * size].astype(f32)
    for copy in copies[1]:
        copy.start()
    nblk = r_ref.shape[1] // BLK
    row = iota2((BLK, BLK), 0)
    col = iota2((BLK, BLK), 1)
    eye = row == col
    pair = ((row >> 1) == (col >> 1)) & (row < col)
    quad = ((row >> 2) == (col >> 2)) & ((row >> 1) < (col >> 1))
    chains = [(h, b) for h in range(HEADS) for b in range(nblk)]
    rs, rts, vts, uppers, invs, ccols, crows = [], [], [], [], [], [], []
    for h, b in chains:
        rows = pl.ds(h + HEADS * BLK * b, BLK, stride=HEADS)
        r = keys[rows, :].astype(bf16)
        r_ref[h, b * BLK : (b + 1) * BLK, :] = r
        rt = r.T
        gram = dot_nn(r, rt)
        diag = jnp.where(eye, gram, 0.0)
        ccol = lax.rsqrt(jnp.sum(diag, axis=1, keepdims=True) + 1e-06)
        crow = lax.rsqrt(jnp.sum(diag, axis=0, keepdims=True) + 1e-06)
        upper = jnp.where(row < col, 2.0 * ccol * crow * gram, 0.0)
        near = jnp.where(pair, upper, 0.0)
        across = jnp.where(quad, upper, 0.0)
        erow = jnp.sum(near, axis=0, keepdims=True)
        fcol = jnp.sum(near, axis=1, keepdims=True)
        mid = across - pltpu.roll(across, 1, 1) * erow
        down = pltpu.roll(mid.reshape(BLK // 8, 8, BLK), 7, 1).reshape(BLK, BLK)
        inv = jnp.where(eye, 1.0, 0.0) - near - (mid - fcol * down)
        rs.append(r)
        rts.append(rt)
        uppers.append(upper)
        invs.append(inv)
        ccols.append(ccol)
        crows.append(crow)
    for level in range(2, 7):
        off = ((row >> (level + 1)) == (col >> (level + 1))) & (
            (row >> level) < (col >> level)
        )
        talls = [tall_wide(inv) for inv in invs]
        mids = [
            mm_pre(wide(jnp.where(off, upper, 0.0)), tall) for upper, tall in zip(uppers, talls)
        ]
        invs = [inv - mm(inv, mid) for inv, mid in zip(invs, mids)]
    for i, copy in enumerate(copies[1]):
        copy.wait()
        values[i * size : (i + 1) * size] = v_ref[i * size : (i + 1) * size].astype(f32)
    for h, b in chains:
        rows = pl.ds(h + HEADS * BLK * b, BLK, stride=HEADS)
        vts.append(values[rows, :].astype(bf16).T)
    pairs = []
    base = jnp.where(iota2((2 * D, D), 0) == iota2((2 * D, D), 1), 1.0, 0.0)
    sign = jnp.where(iota2((2 * D, D), 0) < D, -1.0, 1.0)
    for i, (h, b) in enumerate(chains):
        wh, wl = split(2.0 * ccols[i] * invs[i])
        uh, ul = split(2.0 * invs[i])
        wt = dot_nn(jnp.concatenate([rts[i], rts[i]], axis=1), jnp.concatenate([wh, wl], axis=0))
        ut = dot_nn(jnp.concatenate([vts[i], vts[i]], axis=1), jnp.concatenate([uh, ul], axis=0))
        z = jnp.concatenate([wt, ut], axis=0) * crows[i]
        z_ref[h, b] = z
        rr = jnp.concatenate([rs[i], rs[i]], axis=0)
        pairs.append(base + sign * dot_nn(wide(z), rr))
    for h in range(HEADS):
        own = pairs[h * nblk : (h + 1) * nblk]
        while len(own) > 1:
            own = [compose(own[i], own[i + 1]) for i in range(0, len(own), 2)]
        m_ref[h] = own[0]


def compose(first, second):
    moved = mm(first, second[:D])
    keep = jnp.concatenate([jnp.zeros((D, D), f32), second[D:]], axis=0)
    return moved + keep


def whole(*arrays):
    return [pl.BlockSpec(memory_space=pltpu.VMEM)] * len(arrays)


def factor_call(k, v):
    steps = k.shape[0] // HEADS
    nblk = steps // BLK
    return pl.pallas_call(
        factor_kernel,
        in_specs=[pl.BlockSpec(memory_space=pl.ANY)] * 2,
        out_specs=[pl.BlockSpec(memory_space=pltpu.VMEM)] * 3,
        out_shape=[
            jax.ShapeDtypeStruct((HEADS, 2 * D, D), f32),
            jax.ShapeDtypeStruct((HEADS, nblk, 2 * D, D), f32),
            jax.ShapeDtypeStruct((HEADS, steps, D), bf16),
        ],
        scratch_shapes=[pltpu.VMEM((HEADS * steps, D), bf16)] * 2
        + [pltpu.VMEM((HEADS * steps, D), f32)] * 2
        + [pltpu.SemaphoreType.DMA((2, 4))],
        compiler_params=pltpu.CompilerParams(vmem_limit_bytes=16 << 20),
        name="factor",
    )(k, v)


def chip_kernel(own_ref, sib_ref, *out_refs):
    x = place_x()
    for k in range(XS):
        head = lax.rem(x + k, HEADS)
        out_refs[k][...] = compose(sib_ref[head], own_ref[head])


def ordered_cyclic(slots, place, scratch):
    n = len(slots)
    for k in range(n):
        scratch[lax.rem(place + n - k, n)] = slots[k][...]


def ordered_xor(slots, place, scratch):
    for k, slot in enumerate(slots):
        scratch[place ^ k] = slot[...]


def msg_compose(rows, second):
    moved = mm(rows, second[:D])
    return jnp.concatenate([moved[:D], moved[D:] + second[D:]], axis=0)


def advance(state, second):
    return mm(state, second[:D]) + second[D:]


def write_total(total_ref, hold):
    tail = msg_compose(hold[2], hold[3])
    total_ref[...] = msg_compose(msg_compose(hold[0], hold[1]), tail)


def row_kernel(s0, s1, s2, s3, after_ref, total_ref, hold):
    ordered_cyclic([s0, s1, s2, s3], place_x(), hold)
    write_total(total_ref, hold)


def column_kernel(s0, s1, s2, s3, after_ref, total_ref, hold):
    ordered_xor([s0, s1, s2, s3], place_y(), hold)
    write_total(total_ref, hold)


def place_prefix(place, hold):
    first = hold[0]
    second = msg_compose(first, hold[1])
    third = msg_compose(second, hold[2])
    out = jnp.where(iota2((MSG, D), 0) == iota2((MSG, D), 1), 1.0, 0.0)
    for i, prefix in enumerate((first, second, third)):
        out = jnp.where(place == i + 1, prefix, out)
    return out


def path_kernel(*refs):
    xslots, yslots = refs[:4], refs[4:8]
    init_ref, after_ref, path_ref, start_ref, xhold, yhold = refs[8:]
    x = place_x()
    y = place_y()
    ordered_cyclic(xslots, x, xhold)
    ordered_xor(yslots, y, yhold)
    here = place_prefix(y, yhold)
    first = xhold[0]
    second = msg_compose(first, xhold[1])
    third = msg_compose(second, xhold[2])
    path_ref[0] = here
    left = wide(here)
    for i, prefix in enumerate((first, second, third)):
        moved = mm_pre(left, tall_wide(prefix[:D]))
        path_ref[i + 1, :D, :] = moved[:D]
        path_ref[i + 1, D:, :] = moved[D:] + prefix[D:]
    start_ref[...] = init_ref[x].T


def lead_kernel(s0, s1, s2, s3, start_ref, after_ref, lead_ref, hold):
    ordered_xor([s0, s1, s2, s3], lax.rem(place_seg(), ZG), hold)
    tail = msg_compose(hold[2], hold[3])
    state = advance(advance(start_ref[...], hold[0]), hold[1])
    lead_ref[...] = advance(state, tail)


def fuse_kernel(s0, s1, s2, s3, path_ref, after_ref, fuse_ref, hold):
    g = lax.rem(place_seg(), ZG)
    ordered_xor([s0, s1, s2, s3], g, hold)
    window = place_prefix(g, hold)
    left = wide(window)
    for i in range(XS):
        path = path_ref[i]
        moved = mm_pre(left, tall_wide(path[:D]))
        fuse_ref[i, :D, :] = moved[:D]
        fuse_ref[i, D:, :] = moved[D:] + path[D:]


def entry_kernel(start_ref, early_ref, fuse_ref, o0, o1, o2, o3, scratch):
    x = place_x()
    state = jnp.where(place_seg() >= ZG, early_ref[...], start_ref[...])
    left = wide(state)
    for i in range(XS):
        scratch[i] = mm_pre(left, tall_wide(fuse_ref[i, :D, :])) + fuse_ref[i, D:, :]
    for k, out in enumerate((o0, o1, o2, o3)):
        out[...] = scratch[lax.rem(x + k, XS)]


def reach_kernel(
    q_ref, r_ref, z_ref, sib_ref, after_ref, reach_ref, base_ref, rows, *, head
):
    tokens = reach_ref.shape[0]
    nblk = z_ref.shape[0]
    span = tokens // nblk
    rows[...] = q_ref[...].astype(f32)
    visible = iota2((span, BLK), 1) <= REFL * iota2((span, BLK), 0) + (REFL - 1)
    base = jnp.where(iota2((2 * D, D), 0) == iota2((2 * D, D), 1), 1.0, 0.0)
    sign = jnp.where(iota2((2 * D, D), 0) < D, -1.0, 1.0)
    prefixes = [jnp.where(place_core() == 1, sib_ref[...], base)]
    for b in range(nblk - 1):
        rr = jnp.concatenate([r_ref[b * BLK : (b + 1) * BLK, :]] * 2, axis=0)
        piece = base + sign * dot_nn(wide(z_ref[b]), rr)
        prefixes.append(compose(prefixes[b], piece))
    projects, locals_ = [], []
    for b in range(nblk):
        q = rows[pl.ds(head + HEADS * span * b, span, stride=HEADS), :]
        scores = dot_nt(q.astype(bf16), r_ref[b * BLK : (b + 1) * BLK, :])
        sz = mm_nt(jnp.where(visible, scores, 0.0), z_ref[b])
        projects.append(q - sz[:, :D])
        locals_.append(sz[:, D:])
    moves = [mm_nt(projects[b], prefixes[b]) for b in range(nblk)]
    for b in range(nblk):
        part = slice(b * span, (b + 1) * span)
        reach_ref[part, :] = wide(moves[b][:, :D])
        base_ref[part, :] = moves[b][:, D:] + locals_[b]


def reach_call(q, r, z, sib, after, head):
    tokens = q.shape[0] // HEADS

    def spec(array):
        rest = array.shape[1:]
        return pl.BlockSpec((None, *rest), lambda i: (head,) + (0,) * len(rest))

    return pl.pallas_call(
        functools.partial(reach_kernel, head=head),
        grid=(1,),
        in_specs=[
            pl.BlockSpec(q.shape, lambda i: (0, 0)),
            spec(r),
            spec(z),
            spec(sib),
            pl.BlockSpec(memory_space=pl.ANY),
        ],
        out_specs=[
            pl.BlockSpec((tokens, 2 * D), lambda i: (0, 0)),
            pl.BlockSpec((tokens, D), lambda i: (0, 0)),
        ],
        out_shape=[
            jax.ShapeDtypeStruct((tokens, 2 * D), bf16),
            jax.ShapeDtypeStruct((tokens, D), f32),
        ],
        scratch_shapes=[pltpu.VMEM(q.shape, f32)],
        compiler_params=pltpu.CompilerParams(vmem_limit_bytes=6 << 20),
        cost_estimate=pl.CostEstimate(
            flops=400_000_000, bytes_accessed=3_000_000, transcendentals=0
        ),
        name="reach",
    )(q, r, z, sib, after)


def read_kernel(*refs):
    reaches, bases = refs[: 2 * HEADS : 2], refs[1 : 2 * HEADS : 2]
    refs = refs[2 * HEADS :]
    mine, other = refs[:HEADS], refs[HEADS : 2 * HEADS]
    gain_ref, out_hbm, states, rows, out, sems = refs[2 * HEADS :]
    x = place_x()

    @pl.when(place_core() == 0)
    def _():
        ordered_cyclic(other, x, states)

    @pl.when(place_core() != 0)
    def _():
        ordered_cyclic(mine, x, states)

    rights = []
    for h in range(HEADS):
        both = jnp.concatenate(split(states[h]), axis=0)
        rights.append(jnp.concatenate([both, both], axis=1))
    pieces = sems.shape[0]
    span = reaches[0].shape[0] // pieces
    copies = []
    for i in range(pieces):
        part = slice(i * span, (i + 1) * span)
        for h in range(HEADS):
            moved = dot_nt(reaches[h][part, :], rights[h])
            read = moved[:, :D] + moved[:, D:] + bases[h][part, :]
            scale = lax.rsqrt(jnp.mean(read * read, axis=-1, keepdims=True) + 1e-06)
            rows[pl.ds(i * span * HEADS + h, span, stride=HEADS), :] = (
                read * scale * gain_ref[h : h + 1, :]
            )
        block = pl.ds(i * span * HEADS, span * HEADS)
        out[block, :] = rows[block, :].astype(bf16)
        copies.append(pltpu.make_async_copy(out.at[block], out_hbm.at[block], sems.at[i]))
        copies[-1].start()
    for copy in copies:
        copy.wait()


def read_call(arrays, tokens):
    shape = (tokens * HEADS, D)
    return pl.pallas_call(
        read_kernel,
        in_specs=whole(*arrays),
        out_specs=pl.BlockSpec(memory_space=pl.ANY),
        out_shape=jax.ShapeDtypeStruct(shape, bf16),
        scratch_shapes=[
            pltpu.VMEM((HEADS, D, D), f32),
            pltpu.VMEM(shape, f32),
            pltpu.VMEM(shape, bf16),
            pltpu.SemaphoreType.DMA((2,)),
        ],
        compiler_params=pltpu.CompilerParams(vmem_limit_bytes=8 << 20),
        name="read",
    )(*arrays)


def small_call(kernel, name, arrays, outs, scratch=(), after=None, limit=4, out_dtype=f32):
    extra = [] if after is None else [after]
    return pl.pallas_call(
        kernel,
        in_specs=whole(*arrays)
        + [pl.BlockSpec(memory_space=pl.ANY)] * len(extra),
        out_specs=whole(*outs),
        out_shape=[jax.ShapeDtypeStruct(s, out_dtype) for s in outs],
        scratch_shapes=[pltpu.VMEM(s, f32) for s in scratch],
        compiler_params=pltpu.CompilerParams(vmem_limit_bytes=limit << 20),
        name=name,
    )(*arrays, *extra)


def seat(y, x, c):
    return (y * XS + x) * CS + c


def plane_perm(move):
    pairs = []
    for y in range(YS):
        for x in range(XS):
            pairs.append((seat(y, x, 0), seat(y, x, 0)))
            pairs.append((seat(y, x, 1), seat(*move(y, x), 1)))
    return pairs


def depth_perm(segs, move):
    pairs = []
    for y in range(YS):
        for x in range(XS):
            for g in range(segs):
                for c in range(CS):
                    at = seat(y, x, c) * segs
                    pairs.append((at + g, at + (move(g) if c else g)))
    return pairs


def chip_perm():
    return [(seat(y, x, c), seat(y, x, 1 - c)) for y in range(YS) for x in range(XS) for c in range(CS)]


def per_device(query_rows, key_rows, value_rows, out_gain, initial_state):
    tokens = query_rows.shape[1]
    steps = tokens * REFL
    swap = chip_perm()
    along_x = [plane_perm(lambda y, x, k=k: (y, (x + k) % XS)) for k in range(1, XS)]
    along_y = [plane_perm(lambda y, x, k=k: (y ^ k, x)) for k in range(1, YS)]
    segs = lax.axis_size("seg")
    along_z = [depth_perm(segs, lambda g, k=k: g ^ k) for k in range(1, ZG)]
    jump = depth_perm(segs, lambda g: segs - 1 - g)

    keys = key_rows.reshape(steps * HEADS, D)
    values = value_rows.reshape(steps * HEADS, D)
    query = query_rows.reshape(tokens * HEADS, D)
    keys = pltpu.with_memory_space_constraint(keys, pltpu.HBM)
    values = pltpu.with_memory_space_constraint(values, pltpu.HBM)
    pair, z, r = factor_call(keys, values)
    sib = lax.ppermute(pair, "seq", swap)
    slots = small_call(chip_kernel, "chip", [pair, sib], [(MSG, D)] * XS)
    slots = [slots[0]] + [lax.ppermute(s, "seq", p) for s, p in zip(slots[1:], along_x)]
    reaches = [reach_call(query, r, z, sib, slots[0], 0)]
    xslots = slots
    (total,) = small_call(
        row_kernel, "row", slots, [(MSG, D)], [(XS, MSG, D)], after=reaches[-1][0]
    )
    slots = [total] + [lax.ppermute(total, "seq", p) for p in along_y]
    yslots = slots
    reaches.append(reach_call(query, r, z, sib, total, 1))
    (total,) = small_call(
        column_kernel, "column", slots, [(MSG, D)], [(YS, MSG, D)], after=reaches[-1][0]
    )
    slots = [total] + [lax.ppermute(total, ("seq", "seg"), p) for p in along_z]
    path, start = small_call(
        path_kernel,
        "path",
        [*xslots, *yslots, initial_state],
        [(XS, MSG, D), (D, D)],
        [(XS, MSG, D), (YS, MSG, D)],
        after=total,
    )
    reaches.append(reach_call(query, r, z, sib, path, 2))
    (lead,) = small_call(
        lead_kernel,
        "lead",
        [*slots, start],
        [(D, D)],
        [(ZG, MSG, D)],
        after=reaches[-1][0],
    )
    early = lax.ppermute(lead, ("seq", "seg"), jump)
    (fused,) = small_call(
        fuse_kernel,
        "fuse",
        [*slots, path],
        [(XS, MSG, D)],
        [(ZG, MSG, D)],
        after=lead,
    )
    slots = small_call(
        entry_kernel,
        "entry",
        [start, early, fused],
        [(D, D)] * XS,
        [(XS, D, D)],
    )
    slots = [slots[0]] + [lax.ppermute(s, "seq", p) for s, p in zip(slots[1:], along_x)]
    reaches.append(reach_call(query, r, z, sib, slots[0], 3))
    last = reaches[-1][0]
    for k in range(1, XS):
        slots[k], last = lax.optimization_barrier((slots[k], last))
    reaches[-1] = (last, reaches[-1][1])
    others = [lax.ppermute(s, "seq", swap) for s in slots]
    arrays = [a for pair in reaches for a in pair] + [*slots, *others, out_gain]
    out = read_call(arrays, tokens)
    return out.reshape(1, tokens, HEADS, D)


def solution(mesh):
    return jax.shard_map(
        per_device,
        mesh=mesh,
        in_specs=(
            P("seg", "seq", None, None),
            P("seg", "seq", None, None, None),
            P("seg", "seq", None, None, None),
            P(),
            P(),
        ),
        out_specs=P("seg", "seq", None, None),
        check_vma=False,
    )
```

```python
import functools

import jax
import jax.numpy as jnp
from jax import lax
from jax.experimental import pallas as pl
from jax.experimental.pallas import tpu as pltpu
from jax.sharding import PartitionSpec as P

D = 128
HEADS = 4
REFL = 2
BLK = 128
XS = 4
YS = 4
CS = 2
ZG = 4
MSG = 2 * D

f32 = jnp.float32
bf16 = jnp.bfloat16


def split(x):
    high = x.astype(bf16)
    low = (x - high.astype(f32)).astype(bf16)
    return high, low


def dot_nn(a, b):
    return lax.dot_general(a, b, (((1,), (0,)), ((), ())), preferred_element_type=f32)


def dot_nt(a, b):
    return lax.dot_general(a, b, (((1,), (1,)), ((), ())), preferred_element_type=f32)


def wide(x):
    high, low = split(x)
    return jnp.concatenate([high, low], axis=1)


def tall_wide(x):
    row = wide(x)
    return jnp.concatenate([row, row], axis=0)


def mm_pre(left_wide, right_tall):
    out = dot_nn(left_wide, right_tall)
    n = out.shape[1] // 2
    return out[:, :n] + out[:, n:]


def mm(a, b):
    return mm_pre(wide(a), tall_wide(b))


def mm_nt(a, b):
    ah, al = split(a)
    bh, bl = split(b)
    return dot_nt(ah, bh) + dot_nt(ah, bl) + dot_nt(al, bh)


def place_x():
    return lax.rem(lax.axis_index("seq") // CS, XS)


def place_y():
    return lax.axis_index("seq") // (CS * XS)


def place_core():
    return lax.rem(lax.axis_index("seq"), CS)


def place_seg():
    return lax.axis_index("seg")


def iota2(shape, dim):
    return lax.broadcasted_iota(jnp.int32, shape, dim)


def factor_kernel(k_hbm, v_hbm, m_ref, z_ref, r_ref, k_ref, v_ref, keys, values, sems):
    pieces = sems.shape[1]
    size = k_ref.shape[0] // pieces
    copies = [
        [
            pltpu.make_async_copy(
                src.at[pl.ds(i * size, size)], dst.at[pl.ds(i * size, size)], sems.at[j, i]
            )
            for i in range(pieces)
        ]
        for j, (src, dst) in enumerate(((k_hbm, k_ref), (v_hbm, v_ref)))
    ]
    for copy in copies[0]:
        copy.start()
    for i, copy in enumerate(copies[0]):
        copy.wait()
        keys[i * size : (i + 1) * size] = k_ref[i * size : (i + 1) * size].astype(f32)
    for copy in copies[1]:
        copy.start()
    nblk = r_ref.shape[1] // BLK
    row = iota2((BLK, BLK), 0)
    col = iota2((BLK, BLK), 1)
    eye = row == col
    pair = ((row >> 1) == (col >> 1)) & (row < col)
    quad = ((row >> 2) == (col >> 2)) & ((row >> 1) < (col >> 1))
    chains = [(h, b) for h in range(HEADS) for b in range(nblk)]
    rs, rts, vts, uppers, invs, ccols, crows = [], [], [], [], [], [], []
    for h, b in chains:
        rows = pl.ds(h + HEADS * BLK * b, BLK, stride=HEADS)
        r = keys[rows, :].astype(bf16)
        r_ref[h, b * BLK : (b + 1) * BLK, :] = r
        rt = r.T
        gram = dot_nn(r, rt)
        diag = jnp.where(eye, gram, 0.0)
        ccol = lax.rsqrt(jnp.sum(diag, axis=1, keepdims=True) + 1e-06)
        crow = lax.rsqrt(jnp.sum(diag, axis=0, keepdims=True) + 1e-06)
        upper = jnp.where(row < col, 2.0 * ccol * crow * gram, 0.0)
        near = jnp.where(pair, upper, 0.0)
        across = jnp.where(quad, upper, 0.0)
        erow = jnp.sum(near, axis=0, keepdims=True)
        fcol = jnp.sum(near, axis=1, keepdims=True)
        mid = across - pltpu.roll(across, 1, 1) * erow
        down = pltpu.roll(mid.reshape(BLK // 8, 8, BLK), 7, 1).reshape(BLK, BLK)
        inv = jnp.where(eye, 1.0, 0.0) - near - (mid - fcol * down)
        rs.append(r)
        rts.append(rt)
        uppers.append(upper)
        invs.append(inv)
        ccols.append(ccol)
        crows.append(crow)
    for level in range(2, 7):
        off = ((row >> (level + 1)) == (col >> (level + 1))) & (
            (row >> level) < (col >> level)
        )
        talls = [tall_wide(inv) for inv in invs]
        mids = [
            mm_pre(wide(jnp.where(off, upper, 0.0)), tall) for upper, tall in zip(uppers, talls)
        ]
        invs = [inv - mm(inv, mid) for inv, mid in zip(invs, mids)]
    for i, copy in enumerate(copies[1]):
        copy.wait()
        values[i * size : (i + 1) * size] = v_ref[i * size : (i + 1) * size].astype(f32)
    for h, b in chains:
        rows = pl.ds(h + HEADS * BLK * b, BLK, stride=HEADS)
        vts.append(values[rows, :].astype(bf16).T)
    pairs = []
    base = jnp.where(iota2((2 * D, D), 0) == iota2((2 * D, D), 1), 1.0, 0.0)
    sign = jnp.where(iota2((2 * D, D), 0) < D, -1.0, 1.0)
    for i, (h, b) in enumerate(chains):
        wh, wl = split(2.0 * ccols[i] * invs[i])
        uh, ul = split(2.0 * invs[i])
        wt = dot_nn(jnp.concatenate([rts[i], rts[i]], axis=1), jnp.concatenate([wh, wl], axis=0))
        ut = dot_nn(jnp.concatenate([vts[i], vts[i]], axis=1), jnp.concatenate([uh, ul], axis=0))
        z = jnp.concatenate([wt, ut], axis=0) * crows[i]
        z_ref[h, b] = z
        rr = jnp.concatenate([rs[i], rs[i]], axis=0)
        pairs.append(base + sign * dot_nn(wide(z), rr))
    for h in range(HEADS):
        own = pairs[h * nblk : (h + 1) * nblk]
        while len(own) > 1:
            own = [compose(own[i], own[i + 1]) for i in range(0, len(own), 2)]
        m_ref[h] = own[0]


def compose(first, second):
    moved = mm(first, second[:D])
    keep = jnp.concatenate([jnp.zeros((D, D), f32), second[D:]], axis=0)
    return moved + keep


def whole(*arrays):
    return [pl.BlockSpec(memory_space=pltpu.VMEM)] * len(arrays)


def factor_call(k, v):
    steps = k.shape[0] // HEADS
    nblk = steps // BLK
    return pl.pallas_call(
        factor_kernel,
        in_specs=[pl.BlockSpec(memory_space=pl.ANY)] * 2,
        out_specs=[pl.BlockSpec(memory_space=pltpu.VMEM)] * 3,
        out_shape=[
            jax.ShapeDtypeStruct((HEADS, 2 * D, D), f32),
            jax.ShapeDtypeStruct((HEADS, nblk, 2 * D, D), f32),
            jax.ShapeDtypeStruct((HEADS, steps, D), bf16),
        ],
        scratch_shapes=[pltpu.VMEM((HEADS * steps, D), bf16)] * 2
        + [pltpu.VMEM((HEADS * steps, D), f32)] * 2
        + [pltpu.SemaphoreType.DMA((2, 4))],
        compiler_params=pltpu.CompilerParams(vmem_limit_bytes=16 << 20),
        name="factor",
    )(k, v)


def chip_kernel(own_ref, sib_ref, *out_refs):
    x = place_x()
    for k in range(XS):
        head = lax.rem(x + k, HEADS)
        out_refs[k][...] = compose(sib_ref[head], own_ref[head])


def ordered_cyclic(slots, place, scratch):
    n = len(slots)
    for k in range(n):
        scratch[lax.rem(place + n - k, n)] = slots[k][...]


def ordered_xor(slots, place, scratch):
    for k, slot in enumerate(slots):
        scratch[place ^ k] = slot[...]


def msg_compose(rows, second):
    moved = mm(rows, second[:D])
    return jnp.concatenate([moved[:D], moved[D:] + second[D:]], axis=0)


def advance(state, second):
    return mm(state, second[:D]) + second[D:]


def write_total(total_ref, hold):
    tail = msg_compose(hold[2], hold[3])
    total_ref[...] = msg_compose(msg_compose(hold[0], hold[1]), tail)


def row_kernel(s0, s1, s2, s3, after_ref, total_ref, hold):
    ordered_cyclic([s0, s1, s2, s3], place_x(), hold)
    write_total(total_ref, hold)


def column_kernel(s0, s1, s2, s3, after_ref, total_ref, hold):
    ordered_xor([s0, s1, s2, s3], place_y(), hold)
    write_total(total_ref, hold)


def place_prefix(place, hold):
    first = hold[0]
    second = msg_compose(first, hold[1])
    third = msg_compose(second, hold[2])
    out = jnp.where(iota2((MSG, D), 0) == iota2((MSG, D), 1), 1.0, 0.0)
    for i, prefix in enumerate((first, second, third)):
        out = jnp.where(place == i + 1, prefix, out)
    return out


def path_kernel(*refs):
    xslots, yslots = refs[:4], refs[4:8]
    init_ref, after_ref, path_ref, start_ref, xhold, yhold = refs[8:]
    x = place_x()
    y = place_y()
    ordered_cyclic(xslots, x, xhold)
    ordered_xor(yslots, y, yhold)
    here = place_prefix(y, yhold)
    first = xhold[0]
    second = msg_compose(first, xhold[1])
    third = msg_compose(second, xhold[2])
    path_ref[0] = here
    left = wide(here)
    for i, prefix in enumerate((first, second, third)):
        moved = mm_pre(left, tall_wide(prefix[:D]))
        path_ref[i + 1, :D, :] = moved[:D]
        path_ref[i + 1, D:, :] = moved[D:] + prefix[D:]
    start_ref[...] = init_ref[x].T


def lead_kernel(s0, s1, s2, s3, start_ref, after_ref, lead_ref, hold):
    ordered_xor([s0, s1, s2, s3], lax.rem(place_seg(), ZG), hold)
    tail = msg_compose(hold[2], hold[3])
    state = advance(advance(start_ref[...], hold[0]), hold[1])
    lead_ref[...] = advance(state, tail)


def fuse_kernel(s0, s1, s2, s3, path_ref, after_ref, fuse_ref, hold):
    g = lax.rem(place_seg(), ZG)
    ordered_xor([s0, s1, s2, s3], g, hold)
    window = place_prefix(g, hold)
    left = wide(window)
    for i in range(XS):
        path = path_ref[i]
        moved = mm_pre(left, tall_wide(path[:D]))
        fuse_ref[i, :D, :] = moved[:D]
        fuse_ref[i, D:, :] = moved[D:] + path[D:]


def entry_kernel(start_ref, early_ref, fuse_ref, o0, o1, o2, o3, scratch):
    x = place_x()
    state = jnp.where(place_seg() >= ZG, early_ref[...], start_ref[...])
    left = wide(state)
    for i in range(XS):
        scratch[i] = mm_pre(left, tall_wide(fuse_ref[i, :D, :])) + fuse_ref[i, D:, :]
    for k, out in enumerate((o0, o1, o2, o3)):
        out[...] = scratch[lax.rem(x + k, XS)]


def reach_kernel(
    q_ref, r_ref, z_ref, sib_ref, after_ref, reach_ref, base_ref, rows, *, head
):
    tokens = reach_ref.shape[0]
    nblk = z_ref.shape[0]
    span = tokens // nblk
    rows[...] = q_ref[...].astype(f32)
    visible = iota2((span, BLK), 1) <= REFL * iota2((span, BLK), 0) + (REFL - 1)
    base = jnp.where(iota2((2 * D, D), 0) == iota2((2 * D, D), 1), 1.0, 0.0)
    sign = jnp.where(iota2((2 * D, D), 0) < D, -1.0, 1.0)
    prefixes = [jnp.where(place_core() == 1, sib_ref[...], base)]
    for b in range(nblk - 1):
        rr = jnp.concatenate([r_ref[b * BLK : (b + 1) * BLK, :]] * 2, axis=0)
        piece = base + sign * dot_nn(wide(z_ref[b]), rr)
        prefixes.append(compose(prefixes[b], piece))
    projects, locals_ = [], []
    for b in range(nblk):
        q = rows[pl.ds(head + HEADS * span * b, span, stride=HEADS), :]
        scores = dot_nt(q.astype(bf16), r_ref[b * BLK : (b + 1) * BLK, :])
        sz = mm_nt(jnp.where(visible, scores, 0.0), z_ref[b])
        projects.append(q - sz[:, :D])
        locals_.append(sz[:, D:])
    moves = [mm_nt(projects[b], prefixes[b]) for b in range(nblk)]
    for b in range(nblk):
        part = slice(b * span, (b + 1) * span)
        reach_ref[part, :] = wide(moves[b][:, :D])
        base_ref[part, :] = moves[b][:, D:] + locals_[b]


def reach_call(q, r, z, sib, after, head):
    tokens = q.shape[0] // HEADS

    def spec(array):
        rest = array.shape[1:]
        return pl.BlockSpec((None, *rest), lambda i: (head,) + (0,) * len(rest))

    return pl.pallas_call(
        functools.partial(reach_kernel, head=head),
        grid=(1,),
        in_specs=[
            pl.BlockSpec(q.shape, lambda i: (0, 0)),
            spec(r),
            spec(z),
            spec(sib),
            pl.BlockSpec(memory_space=pl.ANY),
        ],
        out_specs=[
            pl.BlockSpec((tokens, 2 * D), lambda i: (0, 0)),
            pl.BlockSpec((tokens, D), lambda i: (0, 0)),
        ],
        out_shape=[
            jax.ShapeDtypeStruct((tokens, 2 * D), bf16),
            jax.ShapeDtypeStruct((tokens, D), f32),
        ],
        scratch_shapes=[pltpu.VMEM(q.shape, f32)],
        compiler_params=pltpu.CompilerParams(vmem_limit_bytes=6 << 20),
        cost_estimate=pl.CostEstimate(
            flops=400_000_000, bytes_accessed=3_000_000, transcendentals=0
        ),
        name="reach",
    )(q, r, z, sib, after)


def read_kernel(*refs):
    reaches, bases = refs[: 2 * HEADS : 2], refs[1 : 2 * HEADS : 2]
    refs = refs[2 * HEADS :]
    mine, other = refs[:HEADS], refs[HEADS : 2 * HEADS]
    gain_ref, out_hbm, states, rows, out, sems = refs[2 * HEADS :]
    x = place_x()

    @pl.when(place_core() == 0)
    def _():
        ordered_cyclic(other, x, states)

    @pl.when(place_core() != 0)
    def _():
        ordered_cyclic(mine, x, states)

    rights = []
    for h in range(HEADS):
        both = jnp.concatenate(split(states[h]), axis=0)
        rights.append(jnp.concatenate([both, both], axis=1))
    pieces = sems.shape[0]
    span = reaches[0].shape[0] // pieces
    copies = []
    for i in range(pieces):
        part = slice(i * span, (i + 1) * span)
        for h in range(HEADS):
            moved = dot_nt(reaches[h][part, :], rights[h])
            read = moved[:, :D] + moved[:, D:] + bases[h][part, :]
            scale = lax.rsqrt(jnp.mean(read * read, axis=-1, keepdims=True) + 1e-06)
            rows[pl.ds(i * span * HEADS + h, span, stride=HEADS), :] = (
                read * scale * gain_ref[h : h + 1, :]
            )
        block = pl.ds(i * span * HEADS, span * HEADS)
        out[block, :] = rows[block, :].astype(bf16)
        copies.append(pltpu.make_async_copy(out.at[block], out_hbm.at[block], sems.at[i]))
        copies[-1].start()
    for copy in copies:
        copy.wait()


def read_call(arrays, tokens):
    shape = (tokens * HEADS, D)
    return pl.pallas_call(
        read_kernel,
        in_specs=whole(*arrays),
        out_specs=pl.BlockSpec(memory_space=pl.ANY),
        out_shape=jax.ShapeDtypeStruct(shape, bf16),
        scratch_shapes=[
            pltpu.VMEM((HEADS, D, D), f32),
            pltpu.VMEM(shape, f32),
            pltpu.VMEM(shape, bf16),
            pltpu.SemaphoreType.DMA((2,)),
        ],
        compiler_params=pltpu.CompilerParams(vmem_limit_bytes=8 << 20),
        name="read",
    )(*arrays)


def small_call(kernel, name, arrays, outs, scratch=(), after=None, limit=4, out_dtype=f32):
    extra = [] if after is None else [after]
    return pl.pallas_call(
        kernel,
        in_specs=whole(*arrays)
        + [pl.BlockSpec(memory_space=pl.ANY)] * len(extra),
        out_specs=whole(*outs),
        out_shape=[jax.ShapeDtypeStruct(s, out_dtype) for s in outs],
        scratch_shapes=[pltpu.VMEM(s, f32) for s in scratch],
        compiler_params=pltpu.CompilerParams(vmem_limit_bytes=limit << 20),
        name=name,
    )(*arrays, *extra)


def seat(y, x, c):
    return (y * XS + x) * CS + c


def plane_perm(move, spare):
    pairs = []
    for y in range(YS):
        for x in range(XS):
            pairs.append((seat(y, x, 0), seat(*spare(y, x), 0)))
            pairs.append((seat(y, x, 1), seat(*move(y, x), 1)))
    return pairs


def depth_perm(segs, move):
    pairs = []
    for y in range(YS):
        for x in range(XS):
            for g in range(segs):
                pairs.append((seat(y, x, 0) * segs + g, seat(y, x ^ 1, 0) * segs + g))
                at = seat(y, x, 1) * segs
                pairs.append((at + g, at + move(g)))
    return pairs


def chip_perm():
    return [(seat(y, x, c), seat(y, x, 1 - c)) for y in range(YS) for x in range(XS) for c in range(CS)]


def per_device(query_rows, key_rows, value_rows, out_gain, initial_state):
    tokens = query_rows.shape[1]
    steps = tokens * REFL
    swap = chip_perm()
    near_x = lambda y, x: (y, x ^ 1)
    near_y = lambda y, x: (y ^ 1, x)
    along_x = [
        plane_perm(lambda y, x, k=k: (y, (x + k) % XS), near_y) for k in range(1, XS)
    ]
    along_y = [plane_perm(lambda y, x, k=k: (y ^ k, x), near_x) for k in range(1, YS)]
    segs = lax.axis_size("seg")
    along_z = [depth_perm(segs, lambda g, k=k: g ^ k) for k in range(1, ZG)]
    jump = depth_perm(segs, lambda g: segs - 1 - g)

    keys = key_rows.reshape(steps * HEADS, D)
    values = value_rows.reshape(steps * HEADS, D)
    query = query_rows.reshape(tokens * HEADS, D)
    keys = pltpu.with_memory_space_constraint(keys, pltpu.HBM)
    values = pltpu.with_memory_space_constraint(values, pltpu.HBM)
    pair, z, r = factor_call(keys, values)
    sib = lax.ppermute(pair, "seq", swap)
    slots = small_call(chip_kernel, "chip", [pair, sib], [(MSG, D)] * XS)
    slots = [slots[0]] + [lax.ppermute(s, "seq", p) for s, p in zip(slots[1:], along_x)]
    reaches = [reach_call(query, r, z, sib, slots[0], 0)]
    xslots = slots
    (total,) = small_call(
        row_kernel, "row", slots, [(MSG, D)], [(XS, MSG, D)], after=reaches[-1][0]
    )
    slots = [total] + [lax.ppermute(total, "seq", p) for p in along_y]
    yslots = slots
    reaches.append(reach_call(query, r, z, sib, total, 1))
    (total,) = small_call(
        column_kernel, "column", slots, [(MSG, D)], [(YS, MSG, D)], after=reaches[-1][0]
    )
    slots = [total] + [lax.ppermute(total, ("seq", "seg"), p) for p in along_z]
    path, start = small_call(
        path_kernel,
        "path",
        [*xslots, *yslots, initial_state],
        [(XS, MSG, D), (D, D)],
        [(XS, MSG, D), (YS, MSG, D)],
        after=total,
    )
    reaches.append(reach_call(query, r, z, sib, path, 2))
    (lead,) = small_call(
        lead_kernel,
        "lead",
        [*slots, start],
        [(D, D)],
        [(ZG, MSG, D)],
        after=reaches[-1][0],
    )
    early = lax.ppermute(lead, ("seq", "seg"), jump)
    (fused,) = small_call(
        fuse_kernel,
        "fuse",
        [*slots, path],
        [(XS, MSG, D)],
        [(ZG, MSG, D)],
        after=lead,
    )
    slots = small_call(
        entry_kernel,
        "entry",
        [start, early, fused],
        [(D, D)] * XS,
        [(XS, D, D)],
    )
    slots = [slots[0]] + [lax.ppermute(s, "seq", p) for s, p in zip(slots[1:], along_x)]
    reaches.append(reach_call(query, r, z, sib, slots[0], 3))
    last = reaches[-1][0]
    for k in range(1, XS):
        slots[k], last = lax.optimization_barrier((slots[k], last))
    reaches[-1] = (last, reaches[-1][1])
    others = [lax.ppermute(s, "seq", swap) for s in slots]
    arrays = [a for pair in reaches for a in pair] + [*slots, *others, out_gain]
    out = read_call(arrays, tokens)
    return out.reshape(1, tokens, HEADS, D)


def solution(mesh):
    return jax.shard_map(
        per_device,
        mesh=mesh,
        in_specs=(
            P("seg", "seq", None, None),
            P("seg", "seq", None, None, None),
            P("seg", "seq", None, None, None),
            P(),
            P(),
        ),
        out_specs=P("seg", "seq", None, None),
        check_vma=False,
    )
```

```python
import functools

import jax
import jax.numpy as jnp
from jax import lax
from jax.experimental import pallas as pl
from jax.experimental.pallas import tpu as pltpu
from jax.sharding import PartitionSpec as P

D = 128
HEADS = 4
REFL = 2
BLK = 128
XS = 4
YS = 4
CS = 2
MSG = 2 * D

f32 = jnp.float32
bf16 = jnp.bfloat16


def split(x):
    high = x.astype(bf16)
    low = (x - high.astype(f32)).astype(bf16)
    return high, low


def dot_nn(a, b):
    return lax.dot_general(a, b, (((1,), (0,)), ((), ())), preferred_element_type=f32)


def dot_nt(a, b):
    return lax.dot_general(a, b, (((1,), (1,)), ((), ())), preferred_element_type=f32)


def wide(x):
    high, low = split(x)
    return jnp.concatenate([high, low], axis=1)


def tall_wide(x):
    row = wide(x)
    return jnp.concatenate([row, row], axis=0)


def mm_pre(left_wide, right_tall):
    out = dot_nn(left_wide, right_tall)
    n = out.shape[1] // 2
    return out[:, :n] + out[:, n:]


def mm(a, b):
    return mm_pre(wide(a), tall_wide(b))


def mm_nt(a, b):
    ah, al = split(a)
    bh, bl = split(b)
    return dot_nt(ah, bh) + dot_nt(ah, bl) + dot_nt(al, bh)


def place_x():
    return lax.rem(lax.axis_index("seq") // CS, XS)


def place_y():
    return lax.axis_index("seq") // (CS * XS)


def place_core():
    return lax.rem(lax.axis_index("seq"), CS)


def place_seg():
    return lax.axis_index("seg")


def iota2(shape, dim):
    return lax.broadcasted_iota(jnp.int32, shape, dim)


def factor_kernel(k_hbm, v_hbm, m_ref, z_ref, r_ref, k_ref, v_ref, keys, values, sems):
    pieces = sems.shape[1]
    size = k_ref.shape[0] // pieces
    copies = [
        [
            pltpu.make_async_copy(
                src.at[pl.ds(i * size, size)], dst.at[pl.ds(i * size, size)], sems.at[j, i]
            )
            for i in range(pieces)
        ]
        for j, (src, dst) in enumerate(((k_hbm, k_ref), (v_hbm, v_ref)))
    ]
    for copy in copies[0]:
        copy.start()
    for i, copy in enumerate(copies[0]):
        copy.wait()
        keys[i * size : (i + 1) * size] = k_ref[i * size : (i + 1) * size].astype(f32)
    for copy in copies[1]:
        copy.start()
    nblk = r_ref.shape[1] // BLK
    row = iota2((BLK, BLK), 0)
    col = iota2((BLK, BLK), 1)
    eye = row == col
    pair = ((row >> 1) == (col >> 1)) & (row < col)
    chains = [(h, b) for h in range(HEADS) for b in range(nblk)]
    rs, rts, vts, uppers, invs, ccols, crows = [], [], [], [], [], [], []
    for h, b in chains:
        rows = pl.ds(h + HEADS * BLK * b, BLK, stride=HEADS)
        r = keys[rows, :].astype(bf16)
        r_ref[h, b * BLK : (b + 1) * BLK, :] = r
        rt = r.T
        gram = dot_nn(r, rt)
        diag = jnp.where(eye, gram, 0.0)
        ccol = lax.rsqrt(jnp.sum(diag, axis=1, keepdims=True) + 1e-06)
        crow = lax.rsqrt(jnp.sum(diag, axis=0, keepdims=True) + 1e-06)
        upper = jnp.where(row < col, 2.0 * ccol * crow * gram, 0.0)
        inv = jnp.where(eye, 1.0, 0.0) - jnp.where(pair, upper, 0.0)
        rs.append(r)
        rts.append(rt)
        uppers.append(upper)
        invs.append(inv)
        ccols.append(ccol)
        crows.append(crow)
    for level in range(1, 7):
        off = ((row >> (level + 1)) == (col >> (level + 1))) & (
            (row >> level) < (col >> level)
        )
        talls = [tall_wide(inv) for inv in invs]
        mids = [
            mm_pre(wide(jnp.where(off, upper, 0.0)), tall) for upper, tall in zip(uppers, talls)
        ]
        invs = [inv - mm(inv, mid) for inv, mid in zip(invs, mids)]
    for i, copy in enumerate(copies[1]):
        copy.wait()
        values[i * size : (i + 1) * size] = v_ref[i * size : (i + 1) * size].astype(f32)
    for h, b in chains:
        rows = pl.ds(h + HEADS * BLK * b, BLK, stride=HEADS)
        vts.append(values[rows, :].astype(bf16).T)
    pairs = []
    base = jnp.where(iota2((2 * D, D), 0) == iota2((2 * D, D), 1), 1.0, 0.0)
    sign = jnp.where(iota2((2 * D, D), 0) < D, -1.0, 1.0)
    for i, (h, b) in enumerate(chains):
        wh, wl = split(2.0 * ccols[i] * invs[i])
        uh, ul = split(2.0 * invs[i])
        wt = dot_nn(jnp.concatenate([rts[i], rts[i]], axis=1), jnp.concatenate([wh, wl], axis=0))
        ut = dot_nn(jnp.concatenate([vts[i], vts[i]], axis=1), jnp.concatenate([uh, ul], axis=0))
        z = jnp.concatenate([wt, ut], axis=0) * crows[i]
        z_ref[h, b] = z
        rr = jnp.concatenate([rs[i], rs[i]], axis=0)
        pairs.append(base + sign * dot_nn(wide(z), rr))
    for h in range(HEADS):
        own = pairs[h * nblk : (h + 1) * nblk]
        while len(own) > 1:
            own = [compose(own[i], own[i + 1]) for i in range(0, len(own), 2)]
        m_ref[h] = own[0]


def compose(first, second):
    moved = mm(first, second[:D])
    keep = jnp.concatenate([jnp.zeros((D, D), f32), second[D:]], axis=0)
    return moved + keep


def whole(*arrays):
    return [pl.BlockSpec(memory_space=pltpu.VMEM)] * len(arrays)


def factor_call(k, v):
    steps = k.shape[0] // HEADS
    nblk = steps // BLK
    return pl.pallas_call(
        factor_kernel,
        in_specs=[pl.BlockSpec(memory_space=pl.ANY)] * 2,
        out_specs=[pl.BlockSpec(memory_space=pltpu.VMEM)] * 3,
        out_shape=[
            jax.ShapeDtypeStruct((HEADS, 2 * D, D), f32),
            jax.ShapeDtypeStruct((HEADS, nblk, 2 * D, D), f32),
            jax.ShapeDtypeStruct((HEADS, steps, D), bf16),
        ],
        scratch_shapes=[pltpu.VMEM((HEADS * steps, D), bf16)] * 2
        + [pltpu.VMEM((HEADS * steps, D), f32)] * 2
        + [pltpu.SemaphoreType.DMA((2, 4))],
        compiler_params=pltpu.CompilerParams(vmem_limit_bytes=16 << 20),
        name="factor",
    )(k, v)


def chip_kernel(own_ref, sib_ref, *out_refs):
    x = place_x()
    for k in range(XS):
        head = lax.rem(x + k, HEADS)
        out_refs[k][...] = compose(sib_ref[head], own_ref[head])


def ordered_cyclic(slots, place, scratch):
    n = len(slots)
    for k in range(n):
        scratch[lax.rem(place + n - k, n)] = slots[k][...]


def ordered_xor(slots, place, scratch):
    for k, slot in enumerate(slots):
        scratch[place ^ k] = slot[...]


def msg_compose(rows, second):
    moved = mm(rows, second[:D])
    return jnp.concatenate([moved[:D], moved[D:] + second[D:]], axis=0)


def advance(state, second):
    return mm(state, second[:D]) + second[D:]


def write_total(total_ref, hold):
    tail = msg_compose(hold[2], hold[3])
    total_ref[...] = msg_compose(msg_compose(hold[0], hold[1]), tail)


def row_kernel(s0, s1, s2, s3, after_ref, total_ref, hold):
    ordered_cyclic([s0, s1, s2, s3], place_x(), hold)
    write_total(total_ref, hold)


def column_kernel(s0, s1, s2, s3, after_ref, total_ref, hold):
    ordered_xor([s0, s1, s2, s3], place_y(), hold)
    write_total(total_ref, hold)


def place_prefix(place, hold):
    first = hold[0]
    second = msg_compose(first, hold[1])
    third = msg_compose(second, hold[2])
    out = jnp.where(iota2((MSG, D), 0) == iota2((MSG, D), 1), 1.0, 0.0)
    for i, prefix in enumerate((first, second, third)):
        out = jnp.where(place == i + 1, prefix, out)
    return out


def path_kernel(*refs):
    xslots, yslots = refs[:4], refs[4:8]
    init_ref, after_ref, path_ref, start_ref, xhold, yhold = refs[8:]
    x = place_x()
    y = place_y()
    ordered_cyclic(xslots, x, xhold)
    ordered_xor(yslots, y, yhold)
    here = place_prefix(y, yhold)
    first = xhold[0]
    second = msg_compose(first, xhold[1])
    third = msg_compose(second, xhold[2])
    path_ref[0] = here
    left = wide(here)
    for i, prefix in enumerate((first, second, third)):
        moved = mm_pre(left, tall_wide(prefix[:D]))
        path_ref[i + 1, :D, :] = moved[:D]
        path_ref[i + 1, D:, :] = moved[D:] + prefix[D:]
    start_ref[...] = init_ref[x].T


def pair_kernel(own_ref, near_ref, after_ref, total_ref):
    later = lax.rem(place_seg(), 2) == 1
    own, near = own_ref[...], near_ref[...]
    total_ref[...] = msg_compose(jnp.where(later, near, own), jnp.where(later, own, near))


def fuse_kernel(near_ref, path_ref, after_ref, fuse_ref):
    later = lax.rem(place_seg(), 2) == 1
    left = wide(near_ref[...])
    for i in range(XS):
        path = path_ref[i]
        moved = mm_pre(left, tall_wide(path[:D]))
        moved = jnp.concatenate([moved[:D], moved[D:] + path[D:]], axis=0)
        fuse_ref[i] = jnp.where(later, moved, path)


def entry_kernel(s0, s1, s2, s3, start_ref, fuse_ref, after_ref, o0, o1, o2, o3, hold, scratch):
    x = place_x()
    place = place_seg() // 2
    ordered_xor([s0, s1, s2, s3], place, hold)
    state = start_ref[...]
    for i in range(3):
        state = jnp.where(place > i, advance(state, hold[i]), state)
    left = wide(state)
    for i in range(XS):
        scratch[i] = mm_pre(left, tall_wide(fuse_ref[i, :D, :])) + fuse_ref[i, D:, :]
    for k, out in enumerate((o0, o1, o2, o3)):
        out[...] = scratch[lax.rem(x + k, XS)]


def reach_kernel(
    q_ref, r_ref, z_ref, sib_ref, after_ref, reach_ref, base_ref, rows, *, head
):
    tokens = reach_ref.shape[0]
    nblk = z_ref.shape[0]
    span = tokens // nblk
    rows[...] = q_ref[...].astype(f32)
    visible = iota2((span, BLK), 1) <= REFL * iota2((span, BLK), 0) + (REFL - 1)
    base = jnp.where(iota2((2 * D, D), 0) == iota2((2 * D, D), 1), 1.0, 0.0)
    sign = jnp.where(iota2((2 * D, D), 0) < D, -1.0, 1.0)
    prefixes = [jnp.where(place_core() == 1, sib_ref[...], base)]
    for b in range(nblk - 1):
        rr = jnp.concatenate([r_ref[b * BLK : (b + 1) * BLK, :]] * 2, axis=0)
        piece = base + sign * dot_nn(wide(z_ref[b]), rr)
        prefixes.append(compose(prefixes[b], piece))
    projects, locals_ = [], []
    for b in range(nblk):
        q = rows[pl.ds(head + HEADS * span * b, span, stride=HEADS), :]
        scores = dot_nt(q.astype(bf16), r_ref[b * BLK : (b + 1) * BLK, :])
        sz = mm_nt(jnp.where(visible, scores, 0.0), z_ref[b])
        projects.append(q - sz[:, :D])
        locals_.append(sz[:, D:])
    moves = [mm_nt(projects[b], prefixes[b]) for b in range(nblk)]
    for b in range(nblk):
        part = slice(b * span, (b + 1) * span)
        reach_ref[part, :] = wide(moves[b][:, :D])
        base_ref[part, :] = moves[b][:, D:] + locals_[b]


def reach_call(q, r, z, sib, after, head):
    tokens = q.shape[0] // HEADS

    def spec(array):
        rest = array.shape[1:]
        return pl.BlockSpec((None, *rest), lambda i: (head,) + (0,) * len(rest))

    return pl.pallas_call(
        functools.partial(reach_kernel, head=head),
        grid=(1,),
        in_specs=[
            pl.BlockSpec(q.shape, lambda i: (0, 0)),
            spec(r),
            spec(z),
            spec(sib),
            pl.BlockSpec(memory_space=pl.ANY),
        ],
        out_specs=[
            pl.BlockSpec((tokens, 2 * D), lambda i: (0, 0)),
            pl.BlockSpec((tokens, D), lambda i: (0, 0)),
        ],
        out_shape=[
            jax.ShapeDtypeStruct((tokens, 2 * D), bf16),
            jax.ShapeDtypeStruct((tokens, D), f32),
        ],
        scratch_shapes=[pltpu.VMEM(q.shape, f32)],
        compiler_params=pltpu.CompilerParams(vmem_limit_bytes=6 << 20),
        cost_estimate=pl.CostEstimate(
            flops=400_000_000, bytes_accessed=3_000_000, transcendentals=0
        ),
        name="reach",
    )(q, r, z, sib, after)


def read_kernel(*refs):
    reaches, bases = refs[: 2 * HEADS : 2], refs[1 : 2 * HEADS : 2]
    refs = refs[2 * HEADS :]
    mine, other = refs[:HEADS], refs[HEADS : 2 * HEADS]
    gain_ref, out_hbm, states, rows, out, sems = refs[2 * HEADS :]
    x = place_x()

    @pl.when(place_core() == 0)
    def _():
        ordered_cyclic(other, x, states)

    @pl.when(place_core() != 0)
    def _():
        ordered_cyclic(mine, x, states)

    rights = []
    for h in range(HEADS):
        both = jnp.concatenate(split(states[h]), axis=0)
        rights.append(jnp.concatenate([both, both], axis=1))
    pieces = sems.shape[0]
    span = reaches[0].shape[0] // pieces
    copies = []
    for i in range(pieces):
        part = slice(i * span, (i + 1) * span)
        for h in range(HEADS):
            moved = dot_nt(reaches[h][part, :], rights[h])
            read = moved[:, :D] + moved[:, D:] + bases[h][part, :]
            scale = lax.rsqrt(jnp.mean(read * read, axis=-1, keepdims=True) + 1e-06)
            rows[pl.ds(i * span * HEADS + h, span, stride=HEADS), :] = (
                read * scale * gain_ref[h : h + 1, :]
            )
        block = pl.ds(i * span * HEADS, span * HEADS)
        out[block, :] = rows[block, :].astype(bf16)
        copies.append(pltpu.make_async_copy(out.at[block], out_hbm.at[block], sems.at[i]))
        copies[-1].start()
    for copy in copies:
        copy.wait()


def read_call(arrays, tokens):
    shape = (tokens * HEADS, D)
    return pl.pallas_call(
        read_kernel,
        in_specs=whole(*arrays),
        out_specs=pl.BlockSpec(memory_space=pl.ANY),
        out_shape=jax.ShapeDtypeStruct(shape, bf16),
        scratch_shapes=[
            pltpu.VMEM((HEADS, D, D), f32),
            pltpu.VMEM(shape, f32),
            pltpu.VMEM(shape, bf16),
            pltpu.SemaphoreType.DMA((2,)),
        ],
        compiler_params=pltpu.CompilerParams(vmem_limit_bytes=8 << 20),
        name="read",
    )(*arrays)


def small_call(kernel, name, arrays, outs, scratch=(), after=None, limit=4, out_dtype=f32):
    extra = [] if after is None else [after]
    return pl.pallas_call(
        kernel,
        in_specs=whole(*arrays)
        + [pl.BlockSpec(memory_space=pl.ANY)] * len(extra),
        out_specs=whole(*outs),
        out_shape=[jax.ShapeDtypeStruct(s, out_dtype) for s in outs],
        scratch_shapes=[pltpu.VMEM(s, f32) for s in scratch],
        compiler_params=pltpu.CompilerParams(vmem_limit_bytes=limit << 20),
        name=name,
    )(*arrays, *extra)


def seat(y, x, c):
    return (y * XS + x) * CS + c


def plane_perm(move, spare):
    pairs = []
    for y in range(YS):
        for x in range(XS):
            pairs.append((seat(y, x, 0), seat(*spare(y, x), 0)))
            pairs.append((seat(y, x, 1), seat(*move(y, x), 1)))
    return pairs


def depth_perm(segs, move):
    pairs = []
    for y in range(YS):
        for x in range(XS):
            for g in range(segs):
                pairs.append((seat(y, x, 0) * segs + g, seat(y, x ^ 1, 0) * segs + g))
                at = seat(y, x, 1) * segs
                pairs.append((at + g, at + move(g)))
    return pairs


def chip_perm():
    return [(seat(y, x, c), seat(y, x, 1 - c)) for y in range(YS) for x in range(XS) for c in range(CS)]


def per_device(query_rows, key_rows, value_rows, out_gain, initial_state):
    tokens = query_rows.shape[1]
    steps = tokens * REFL
    swap = chip_perm()
    near_x = lambda y, x: (y, x ^ 1)
    near_y = lambda y, x: (y ^ 1, x)
    along_x = [
        plane_perm(lambda y, x, k=k: (y, (x + k) % XS), near_y) for k in range(1, XS)
    ]
    along_y = [plane_perm(lambda y, x, k=k: (y ^ k, x), near_x) for k in range(1, YS)]
    segs = lax.axis_size("seg")
    near_z, *along_z = [depth_perm(segs, lambda g, k=k: g ^ k) for k in (1, 2, 5, 6)]

    keys = key_rows.reshape(steps * HEADS, D)
    values = value_rows.reshape(steps * HEADS, D)
    query = query_rows.reshape(tokens * HEADS, D)
    keys = pltpu.with_memory_space_constraint(keys, pltpu.HBM)
    values = pltpu.with_memory_space_constraint(values, pltpu.HBM)
    pair, z, r = factor_call(keys, values)
    sib = lax.ppermute(pair, "seq", swap)
    slots = small_call(chip_kernel, "chip", [pair, sib], [(MSG, D)] * XS)
    slots = [slots[0]] + [lax.ppermute(s, "seq", p) for s, p in zip(slots[1:], along_x)]
    reaches = [reach_call(query, r, z, sib, slots[0], 0)]
    xslots = slots
    (total,) = small_call(
        row_kernel, "row", slots, [(MSG, D)], [(XS, MSG, D)], after=reaches[-1][0]
    )
    slots = [total] + [lax.ppermute(total, "seq", p) for p in along_y]
    yslots = slots
    reaches.append(reach_call(query, r, z, sib, total, 1))
    (total,) = small_call(
        column_kernel, "column", slots, [(MSG, D)], [(YS, MSG, D)], after=reaches[-1][0]
    )
    near = lax.ppermute(total, ("seq", "seg"), near_z)
    path, start = small_call(
        path_kernel,
        "path",
        [*xslots, *yslots, initial_state],
        [(XS, MSG, D), (D, D)],
        [(XS, MSG, D), (YS, MSG, D)],
        after=total,
    )
    (total,) = small_call(pair_kernel, "pair", [total, near], [(MSG, D)], after=path)
    slots = [total] + [lax.ppermute(total, ("seq", "seg"), p) for p in along_z]
    (fused,) = small_call(fuse_kernel, "fuse", [near, path], [(XS, MSG, D)], after=total)
    reaches.append(reach_call(query, r, z, sib, fused, 2))
    slots = small_call(
        entry_kernel,
        "entry",
        [*slots, start, fused],
        [(D, D)] * XS,
        [(XS, MSG, D), (XS, D, D)],
        after=reaches[-1][0],
    )
    slots = [slots[0]] + [lax.ppermute(s, "seq", p) for s, p in zip(slots[1:], along_x)]
    reaches.append(reach_call(query, r, z, sib, slots[0], 3))
    last = reaches[-1][0]
    for k in range(1, XS):
        slots[k], last = lax.optimization_barrier((slots[k], last))
    reaches[-1] = (last, reaches[-1][1])
    others = [lax.ppermute(s, "seq", swap) for s in slots]
    arrays = [a for pair in reaches for a in pair] + [*slots, *others, out_gain]
    out = read_call(arrays, tokens)
    return out.reshape(1, tokens, HEADS, D)


def solution(mesh):
    return jax.shard_map(
        per_device,
        mesh=mesh,
        in_specs=(
            P("seg", "seq", None, None),
            P("seg", "seq", None, None, None),
            P("seg", "seq", None, None, None),
            P(),
            P(),
        ),
        out_specs=P("seg", "seq", None, None),
        check_vma=False,
    )
```

```python
import functools

import jax
import jax.numpy as jnp
from jax import lax
from jax.experimental import pallas as pl
from jax.experimental.pallas import tpu as pltpu
from jax.sharding import PartitionSpec as P

D = 128
HEADS = 4
REFL = 2
BLK = 128
XS = 4
YS = 4
CS = 2
ZG = 4
MSG = 2 * D

f32 = jnp.float32
bf16 = jnp.bfloat16


def split(x):
    high = x.astype(bf16)
    low = (x - high.astype(f32)).astype(bf16)
    return high, low


def dot_nn(a, b):
    return lax.dot_general(a, b, (((1,), (0,)), ((), ())), preferred_element_type=f32)


def dot_nt(a, b):
    return lax.dot_general(a, b, (((1,), (1,)), ((), ())), preferred_element_type=f32)


def wide(x):
    high, low = split(x)
    return jnp.concatenate([high, low], axis=1)


def tall_wide(x):
    row = wide(x)
    return jnp.concatenate([row, row], axis=0)


def mm_pre(left_wide, right_tall):
    out = dot_nn(left_wide, right_tall)
    n = out.shape[1] // 2
    return out[:, :n] + out[:, n:]


def mm(a, b):
    return mm_pre(wide(a), tall_wide(b))


def mm_nt(a, b):
    ah, al = split(a)
    bh, bl = split(b)
    return dot_nt(ah, bh) + dot_nt(ah, bl) + dot_nt(al, bh)


def place_x():
    return lax.rem(lax.axis_index("seq") // CS, XS)


def place_y():
    return lax.axis_index("seq") // (CS * XS)


def place_core():
    return lax.rem(lax.axis_index("seq"), CS)


def place_seg():
    return lax.axis_index("seg")


def iota2(shape, dim):
    return lax.broadcasted_iota(jnp.int32, shape, dim)


def factor_kernel(k_hbm, v_hbm, m_ref, z_ref, r_ref, k_ref, v_ref, keys, values, sems):
    pieces = sems.shape[1]
    size = k_ref.shape[0] // pieces
    copies = [
        [
            pltpu.make_async_copy(
                src.at[pl.ds(i * size, size)], dst.at[pl.ds(i * size, size)], sems.at[j, i]
            )
            for i in range(pieces)
        ]
        for j, (src, dst) in enumerate(((k_hbm, k_ref), (v_hbm, v_ref)))
    ]
    for copy in copies[0]:
        copy.start()
    for i, copy in enumerate(copies[0]):
        copy.wait()
        keys[i * size : (i + 1) * size] = k_ref[i * size : (i + 1) * size].astype(f32)
    for copy in copies[1]:
        copy.start()
    nblk = r_ref.shape[1] // BLK
    row = iota2((BLK, BLK), 0)
    col = iota2((BLK, BLK), 1)
    eye = row == col
    pair = ((row >> 1) == (col >> 1)) & (row < col)
    chains = [(h, b) for h in range(HEADS) for b in range(nblk)]
    rs, rts, vts, uppers, invs, ccols, crows = [], [], [], [], [], [], []
    for h, b in chains:
        rows = pl.ds(h + HEADS * BLK * b, BLK, stride=HEADS)
        r = keys[rows, :].astype(bf16)
        r_ref[h, b * BLK : (b + 1) * BLK, :] = r
        rt = r.T
        gram = dot_nn(r, rt)
        diag = jnp.where(eye, gram, 0.0)
        ccol = lax.rsqrt(jnp.sum(diag, axis=1, keepdims=True) + 1e-06)
        crow = lax.rsqrt(jnp.sum(diag, axis=0, keepdims=True) + 1e-06)
        upper = jnp.where(row < col, 2.0 * ccol * crow * gram, 0.0)
        inv = jnp.where(eye, 1.0, 0.0) - jnp.where(pair, upper, 0.0)
        rs.append(r)
        rts.append(rt)
        uppers.append(upper)
        invs.append(inv)
        ccols.append(ccol)
        crows.append(crow)
    for level in range(1, 7):
        off = ((row >> (level + 1)) == (col >> (level + 1))) & (
            (row >> level) < (col >> level)
        )
        talls = [tall_wide(inv) for inv in invs]
        mids = [
            mm_pre(wide(jnp.where(off, upper, 0.0)), tall) for upper, tall in zip(uppers, talls)
        ]
        invs = [inv - mm(inv, mid) for inv, mid in zip(invs, mids)]
    for i, copy in enumerate(copies[1]):
        copy.wait()
        values[i * size : (i + 1) * size] = v_ref[i * size : (i + 1) * size].astype(f32)
    for h, b in chains:
        rows = pl.ds(h + HEADS * BLK * b, BLK, stride=HEADS)
        vts.append(values[rows, :].astype(bf16).T)
    pairs = []
    base = jnp.where(iota2((2 * D, D), 0) == iota2((2 * D, D), 1), 1.0, 0.0)
    sign = jnp.where(iota2((2 * D, D), 0) < D, -1.0, 1.0)
    for i, (h, b) in enumerate(chains):
        wh, wl = split(2.0 * ccols[i] * invs[i])
        uh, ul = split(2.0 * invs[i])
        wt = dot_nn(jnp.concatenate([rts[i], rts[i]], axis=1), jnp.concatenate([wh, wl], axis=0))
        ut = dot_nn(jnp.concatenate([vts[i], vts[i]], axis=1), jnp.concatenate([uh, ul], axis=0))
        z = jnp.concatenate([wt, ut], axis=0) * crows[i]
        z_ref[h, b] = z
        rr = jnp.concatenate([rs[i], rs[i]], axis=0)
        pairs.append(base + sign * dot_nn(wide(z), rr))
    for h in range(HEADS):
        own = pairs[h * nblk : (h + 1) * nblk]
        while len(own) > 1:
            own = [compose(own[i], own[i + 1]) for i in range(0, len(own), 2)]
        m_ref[h] = own[0]


def compose(first, second):
    moved = mm(first, second[:D])
    keep = jnp.concatenate([jnp.zeros((D, D), f32), second[D:]], axis=0)
    return moved + keep


def whole(*arrays):
    return [pl.BlockSpec(memory_space=pltpu.VMEM)] * len(arrays)


def factor_call(k, v):
    steps = k.shape[0] // HEADS
    nblk = steps // BLK
    return pl.pallas_call(
        factor_kernel,
        in_specs=[pl.BlockSpec(memory_space=pl.ANY)] * 2,
        out_specs=[pl.BlockSpec(memory_space=pltpu.VMEM)] * 3,
        out_shape=[
            jax.ShapeDtypeStruct((HEADS, 2 * D, D), f32),
            jax.ShapeDtypeStruct((HEADS, nblk, 2 * D, D), f32),
            jax.ShapeDtypeStruct((HEADS, steps, D), bf16),
        ],
        scratch_shapes=[pltpu.VMEM((HEADS * steps, D), bf16)] * 2
        + [pltpu.VMEM((HEADS * steps, D), f32)] * 2
        + [pltpu.SemaphoreType.DMA((2, 4))],
        compiler_params=pltpu.CompilerParams(vmem_limit_bytes=16 << 20),
        name="factor",
    )(k, v)


def chip_kernel(own_ref, sib_ref, *out_refs):
    x = place_x()
    for k in range(XS):
        head = lax.rem(x + k, HEADS)
        out_refs[k][...] = compose(sib_ref[head], own_ref[head])


def ordered_cyclic(slots, place, scratch):
    n = len(slots)
    for k in range(n):
        scratch[lax.rem(place + n - k, n)] = slots[k][...]


def ordered_xor(slots, place, scratch):
    for k, slot in enumerate(slots):
        scratch[place ^ k] = slot[...]


def msg_compose(rows, second):
    moved = mm(rows, second[:D])
    return jnp.concatenate([moved[:D], moved[D:] + second[D:]], axis=0)


def advance(state, second):
    return mm(state, second[:D]) + second[D:]


def write_total(total_ref, hold):
    tail = msg_compose(hold[2], hold[3])
    total_ref[...] = msg_compose(msg_compose(hold[0], hold[1]), tail)


def row_kernel(s0, s2, s1, s3, after_ref, total_ref, hold):
    ordered_cyclic([s0, s1, s2, s3], place_x(), hold)
    write_total(total_ref, hold)


def column_kernel(s0, s1, s3, s2, after_ref, total_ref, hold):
    ordered_xor([s0, s1, s2, s3], place_y(), hold)
    write_total(total_ref, hold)


def place_prefix(place, hold):
    first = hold[0]
    second = msg_compose(first, hold[1])
    third = msg_compose(second, hold[2])
    out = jnp.where(iota2((MSG, D), 0) == iota2((MSG, D), 1), 1.0, 0.0)
    for i, prefix in enumerate((first, second, third)):
        out = jnp.where(place == i + 1, prefix, out)
    return out


def path_kernel(*refs):
    xslots, yslots = refs[:4], refs[4:8]
    init_ref, after_ref, path_ref, start_ref, xhold, yhold = refs[8:]
    x = place_x()
    y = place_y()
    ordered_cyclic(xslots, x, xhold)
    ordered_xor(yslots, y, yhold)
    here = place_prefix(y, yhold)
    first = xhold[0]
    second = msg_compose(first, xhold[1])
    third = msg_compose(second, xhold[2])
    path_ref[0] = here
    left = wide(here)
    for i, prefix in enumerate((first, second, third)):
        moved = mm_pre(left, tall_wide(prefix[:D]))
        path_ref[i + 1, :D, :] = moved[:D]
        path_ref[i + 1, D:, :] = moved[D:] + prefix[D:]
    start_ref[...] = init_ref[x].T


def lead_kernel(s0, s1, s2, s3, start_ref, after_ref, lead_ref, hold):
    ordered_xor([s0, s1, s2, s3], lax.rem(place_seg(), ZG), hold)
    tail = msg_compose(hold[2], hold[3])
    state = advance(advance(start_ref[...], hold[0]), hold[1])
    lead_ref[...] = advance(state, tail)


def fuse_kernel(s0, s1, s2, s3, path_ref, after_ref, fuse_ref, hold):
    g = lax.rem(place_seg(), ZG)
    ordered_xor([s0, s1, s2, s3], g, hold)
    window = place_prefix(g, hold)
    left = wide(window)
    for i in range(XS):
        path = path_ref[i]
        moved = mm_pre(left, tall_wide(path[:D]))
        fuse_ref[i, :D, :] = moved[:D]
        fuse_ref[i, D:, :] = moved[D:] + path[D:]


def entry_kernel(start_ref, early_ref, fuse_ref, o0, o1, o2, o3, scratch):
    x = place_x()
    state = jnp.where(place_seg() >= ZG, early_ref[...], start_ref[...])
    left = wide(state)
    for i in range(XS):
        scratch[i] = mm_pre(left, tall_wide(fuse_ref[i, :D, :])) + fuse_ref[i, D:, :]
    for k, out in enumerate((o0, o1, o2, o3)):
        out[...] = scratch[lax.rem(x + k, XS)]


def reach_kernel(
    q_ref, r_ref, z_ref, sib_ref, after_ref, reach_ref, base_ref, rows, *, head
):
    tokens = reach_ref.shape[0]
    nblk = z_ref.shape[0]
    span = tokens // nblk
    rows[...] = q_ref[...].astype(f32)
    visible = iota2((span, BLK), 1) <= REFL * iota2((span, BLK), 0) + (REFL - 1)
    base = jnp.where(iota2((2 * D, D), 0) == iota2((2 * D, D), 1), 1.0, 0.0)
    sign = jnp.where(iota2((2 * D, D), 0) < D, -1.0, 1.0)
    prefixes = [jnp.where(place_core() == 1, sib_ref[...], base)]
    for b in range(nblk - 1):
        rr = jnp.concatenate([r_ref[b * BLK : (b + 1) * BLK, :]] * 2, axis=0)
        piece = base + sign * dot_nn(wide(z_ref[b]), rr)
        prefixes.append(compose(prefixes[b], piece))
    projects, locals_ = [], []
    for b in range(nblk):
        q = rows[pl.ds(head + HEADS * span * b, span, stride=HEADS), :]
        scores = dot_nt(q.astype(bf16), r_ref[b * BLK : (b + 1) * BLK, :])
        sz = mm_nt(jnp.where(visible, scores, 0.0), z_ref[b])
        projects.append(q - sz[:, :D])
        locals_.append(sz[:, D:])
    moves = [mm_nt(projects[b], prefixes[b]) for b in range(nblk)]
    for b in range(nblk):
        part = slice(b * span, (b + 1) * span)
        reach_ref[part, :] = wide(moves[b][:, :D])
        base_ref[part, :] = moves[b][:, D:] + locals_[b]


def reach_call(q, r, z, sib, after, head):
    tokens = q.shape[0] // HEADS

    def spec(array):
        rest = array.shape[1:]
        return pl.BlockSpec((None, *rest), lambda i: (head,) + (0,) * len(rest))

    return pl.pallas_call(
        functools.partial(reach_kernel, head=head),
        grid=(1,),
        in_specs=[
            pl.BlockSpec(q.shape, lambda i: (0, 0)),
            spec(r),
            spec(z),
            spec(sib),
            pl.BlockSpec(memory_space=pl.ANY),
        ],
        out_specs=[
            pl.BlockSpec((tokens, 2 * D), lambda i: (0, 0)),
            pl.BlockSpec((tokens, D), lambda i: (0, 0)),
        ],
        out_shape=[
            jax.ShapeDtypeStruct((tokens, 2 * D), bf16),
            jax.ShapeDtypeStruct((tokens, D), f32),
        ],
        scratch_shapes=[pltpu.VMEM(q.shape, f32)],
        compiler_params=pltpu.CompilerParams(vmem_limit_bytes=6 << 20),
        cost_estimate=pl.CostEstimate(
            flops=400_000_000, bytes_accessed=3_000_000, transcendentals=0
        ),
        name="reach",
    )(q, r, z, sib, after)


def read_kernel(*refs):
    reaches, bases = refs[: 2 * HEADS : 2], refs[1 : 2 * HEADS : 2]
    refs = refs[2 * HEADS :]
    mine, other = refs[:HEADS], refs[HEADS : 2 * HEADS]
    gain_ref, out_hbm, states, rows, out, sems = refs[2 * HEADS :]
    x = place_x()

    @pl.when(place_core() == 0)
    def _():
        ordered_cyclic(other, x, states)

    @pl.when(place_core() != 0)
    def _():
        ordered_cyclic(mine, x, states)

    rights = []
    for h in range(HEADS):
        both = jnp.concatenate(split(states[h]), axis=0)
        rights.append(jnp.concatenate([both, both], axis=1))
    pieces = sems.shape[0]
    span = reaches[0].shape[0] // pieces
    copies = []
    for i in range(pieces):
        part = slice(i * span, (i + 1) * span)
        for h in range(HEADS):
            moved = dot_nt(reaches[h][part, :], rights[h])
            read = moved[:, :D] + moved[:, D:] + bases[h][part, :]
            scale = lax.rsqrt(jnp.mean(read * read, axis=-1, keepdims=True) + 1e-06)
            rows[pl.ds(i * span * HEADS + h, span, stride=HEADS), :] = (
                read * scale * gain_ref[h : h + 1, :]
            )
        block = pl.ds(i * span * HEADS, span * HEADS)
        out[block, :] = rows[block, :].astype(bf16)
        copies.append(pltpu.make_async_copy(out.at[block], out_hbm.at[block], sems.at[i]))
        copies[-1].start()
    for copy in copies:
        copy.wait()


def read_call(arrays, tokens):
    shape = (tokens * HEADS, D)
    return pl.pallas_call(
        read_kernel,
        in_specs=whole(*arrays),
        out_specs=pl.BlockSpec(memory_space=pl.ANY),
        out_shape=jax.ShapeDtypeStruct(shape, bf16),
        scratch_shapes=[
            pltpu.VMEM((HEADS, D, D), f32),
            pltpu.VMEM(shape, f32),
            pltpu.VMEM(shape, bf16),
            pltpu.SemaphoreType.DMA((2,)),
        ],
        compiler_params=pltpu.CompilerParams(vmem_limit_bytes=8 << 20),
        name="read",
    )(*arrays)


def small_call(kernel, name, arrays, outs, scratch=(), after=None, limit=4, out_dtype=f32):
    extra = [] if after is None else [after]
    return pl.pallas_call(
        kernel,
        in_specs=whole(*arrays)
        + [pl.BlockSpec(memory_space=pl.ANY)] * len(extra),
        out_specs=whole(*outs),
        out_shape=[jax.ShapeDtypeStruct(s, out_dtype) for s in outs],
        scratch_shapes=[pltpu.VMEM(s, f32) for s in scratch],
        compiler_params=pltpu.CompilerParams(vmem_limit_bytes=limit << 20),
        name=name,
    )(*arrays, *extra)


def seat(y, x, c):
    return (y * XS + x) * CS + c


def plane_perm(move, spare):
    pairs = []
    for y in range(YS):
        for x in range(XS):
            pairs.append((seat(y, x, 0), seat(*spare(y, x), 0)))
            pairs.append((seat(y, x, 1), seat(*move(y, x), 1)))
    return pairs


def depth_perm(segs, move):
    pairs = []
    for y in range(YS):
        for x in range(XS):
            for g in range(segs):
                pairs.append((seat(y, x, 0) * segs + g, seat(y, x ^ 1, 0) * segs + g))
                at = seat(y, x, 1) * segs
                pairs.append((at + g, at + move(g)))
    return pairs


def chip_perm():
    return [(seat(y, x, c), seat(y, x, 1 - c)) for y in range(YS) for x in range(XS) for c in range(CS)]


def exchange(slots, axis, perms, order):
    out = list(slots)
    for k in order:
        out[k] = lax.ppermute(slots[k], axis, perms[k - 1])
    return out


def per_device(query_rows, key_rows, value_rows, out_gain, initial_state):
    tokens = query_rows.shape[1]
    steps = tokens * REFL
    swap = chip_perm()
    near_x = lambda y, x: (y, x ^ 1)
    near_y = lambda y, x: (y ^ 1, x)
    along_x = [
        plane_perm(lambda y, x, k=k: (y, (x + k) % XS), near_y) for k in range(1, XS)
    ]
    along_y = [plane_perm(lambda y, x, k=k: (y ^ k, x), near_x) for k in range(1, YS)]
    segs = lax.axis_size("seg")
    along_z = [depth_perm(segs, lambda g, k=k: g ^ k) for k in range(1, ZG)]
    jump = depth_perm(segs, lambda g: segs - 1 - g)

    keys = key_rows.reshape(steps * HEADS, D)
    values = value_rows.reshape(steps * HEADS, D)
    query = query_rows.reshape(tokens * HEADS, D)
    keys = pltpu.with_memory_space_constraint(keys, pltpu.HBM)
    values = pltpu.with_memory_space_constraint(values, pltpu.HBM)
    pair, z, r = factor_call(keys, values)
    sib = lax.ppermute(pair, "seq", swap)
    slots = small_call(chip_kernel, "chip", [pair, sib], [(MSG, D)] * XS)
    slots = exchange(slots, "seq", along_x, (2, 1, 3))
    reaches = [reach_call(query, r, z, sib, slots[0], 0)]
    xslots = slots
    (total,) = small_call(
        row_kernel, "row", [slots[i] for i in (0, 2, 1, 3)], [(MSG, D)], [(XS, MSG, D)], after=reaches[-1][0]
    )
    slots = exchange([total] * YS, "seq", along_y, (1, 3, 2))
    yslots = slots
    reaches.append(reach_call(query, r, z, sib, total, 1))
    (total,) = small_call(
        column_kernel, "column", [slots[i] for i in (0, 1, 3, 2)], [(MSG, D)], [(YS, MSG, D)], after=reaches[-1][0]
    )
    slots = exchange([total] * ZG, ("seq", "seg"), along_z, (1, 2, 3))
    path, start = small_call(
        path_kernel,
        "path",
        [*xslots, *yslots, initial_state],
        [(XS, MSG, D), (D, D)],
        [(XS, MSG, D), (YS, MSG, D)],
        after=total,
    )
    reaches.append(reach_call(query, r, z, sib, path, 2))
    (lead,) = small_call(
        lead_kernel,
        "lead",
        [*slots, start],
        [(D, D)],
        [(ZG, MSG, D)],
        after=reaches[-1][0],
    )
    early = lax.ppermute(lead, ("seq", "seg"), jump)
    (fused,) = small_call(
        fuse_kernel,
        "fuse",
        [*slots, path],
        [(XS, MSG, D)],
        [(ZG, MSG, D)],
        after=lead,
    )
    slots = small_call(
        entry_kernel,
        "entry",
        [start, early, fused],
        [(D, D)] * XS,
        [(XS, D, D)],
    )
    slots = exchange(slots, "seq", along_x, (2, 1, 3))
    reaches.append(reach_call(query, r, z, sib, slots[0], 3))
    last = reaches[-1][0]
    for k in range(1, XS):
        slots[k], last = lax.optimization_barrier((slots[k], last))
    reaches[-1] = (last, reaches[-1][1])
    others = [lax.ppermute(s, "seq", swap) for s in slots]
    arrays = [a for pair in reaches for a in pair] + [*slots, *others, out_gain]
    out = read_call(arrays, tokens)
    return out.reshape(1, tokens, HEADS, D)


def solution(mesh):
    return jax.shard_map(
        per_device,
        mesh=mesh,
        in_specs=(
            P("seg", "seq", None, None),
            P("seg", "seq", None, None, None),
            P("seg", "seq", None, None, None),
            P(),
            P(),
        ),
        out_specs=P("seg", "seq", None, None),
        check_vma=False,
    )
```

```python
import functools

import jax
import jax.numpy as jnp
from jax import lax
from jax.experimental import pallas as pl
from jax.experimental.pallas import tpu as pltpu
from jax.sharding import PartitionSpec as P

D = 128
HEADS = 4
REFL = 2
BLK = 128
XS = 4
YS = 4
CS = 2
ZG = 4
MSG = 2 * D

f32 = jnp.float32
bf16 = jnp.bfloat16


def split(x):
    high = x.astype(bf16)
    low = (x - high.astype(f32)).astype(bf16)
    return high, low


def dot_nn(a, b):
    return lax.dot_general(a, b, (((1,), (0,)), ((), ())), preferred_element_type=f32)


def dot_nt(a, b):
    return lax.dot_general(a, b, (((1,), (1,)), ((), ())), preferred_element_type=f32)


def wide(x):
    high, low = split(x)
    return jnp.concatenate([high, low], axis=1)


def tall_wide(x):
    row = wide(x)
    return jnp.concatenate([row, row], axis=0)


def mm_pre(left_wide, right_tall):
    out = dot_nn(left_wide, right_tall)
    n = out.shape[1] // 2
    return out[:, :n] + out[:, n:]


def mm(a, b):
    return mm_pre(wide(a), tall_wide(b))


def mm_nt(a, b):
    ah, al = split(a)
    bh, bl = split(b)
    return dot_nt(ah, bh) + dot_nt(ah, bl) + dot_nt(al, bh)


def place_x():
    return lax.rem(lax.axis_index("seq") // CS, XS)


def place_y():
    return lax.axis_index("seq") // (CS * XS)


def place_core():
    return lax.rem(lax.axis_index("seq"), CS)


def place_seg():
    return lax.axis_index("seg")


def iota2(shape, dim):
    return lax.broadcasted_iota(jnp.int32, shape, dim)


def factor_kernel(k_hbm, v_hbm, m_ref, z_ref, r_ref, k_ref, v_ref, keys, values, sems):
    pieces = sems.shape[1]
    size = k_ref.shape[0] // pieces
    copies = [
        [
            pltpu.make_async_copy(
                src.at[pl.ds(i * size, size)], dst.at[pl.ds(i * size, size)], sems.at[j, i]
            )
            for i in range(pieces)
        ]
        for j, (src, dst) in enumerate(((k_hbm, k_ref), (v_hbm, v_ref)))
    ]
    for copy in copies[0]:
        copy.start()
    for i, copy in enumerate(copies[0]):
        copy.wait()
        keys[i * size : (i + 1) * size] = k_ref[i * size : (i + 1) * size].astype(f32)
    for copy in copies[1]:
        copy.start()
    nblk = r_ref.shape[1] // BLK
    row = iota2((BLK, BLK), 0)
    col = iota2((BLK, BLK), 1)
    eye = row == col
    pair = ((row >> 1) == (col >> 1)) & (row < col)
    chains = [(h, b) for h in range(HEADS) for b in range(nblk)]
    rs, rts, vts, uppers, invs, ccols, crows = [], [], [], [], [], [], []
    for h, b in chains:
        rows = pl.ds(h + HEADS * BLK * b, BLK, stride=HEADS)
        r = keys[rows, :].astype(bf16)
        r_ref[h, b * BLK : (b + 1) * BLK, :] = r
        rt = r.T
        gram = dot_nn(r, rt)
        diag = jnp.where(eye, gram, 0.0)
        ccol = lax.rsqrt(jnp.sum(diag, axis=1, keepdims=True) + 1e-06)
        crow = lax.rsqrt(jnp.sum(diag, axis=0, keepdims=True) + 1e-06)
        upper = jnp.where(row < col, 2.0 * ccol * crow * gram, 0.0)
        inv = jnp.where(eye, 1.0, 0.0) - jnp.where(pair, upper, 0.0)
        rs.append(r)
        rts.append(rt)
        uppers.append(upper)
        invs.append(inv)
        ccols.append(ccol)
        crows.append(crow)
    for level in range(1, 7):
        off = ((row >> (level + 1)) == (col >> (level + 1))) & (
            (row >> level) < (col >> level)
        )
        talls = [tall_wide(inv) for inv in invs]
        mids = [
            mm_pre(wide(jnp.where(off, upper, 0.0)), tall) for upper, tall in zip(uppers, talls)
        ]
        invs = [inv - mm(inv, mid) for inv, mid in zip(invs, mids)]
    for i, copy in enumerate(copies[1]):
        copy.wait()
        values[i * size : (i + 1) * size] = v_ref[i * size : (i + 1) * size].astype(f32)
    for h, b in chains:
        rows = pl.ds(h + HEADS * BLK * b, BLK, stride=HEADS)
        vts.append(values[rows, :].astype(bf16).T)
    pairs = []
    base = jnp.where(iota2((2 * D, D), 0) == iota2((2 * D, D), 1), 1.0, 0.0)
    sign = jnp.where(iota2((2 * D, D), 0) < D, -1.0, 1.0)
    for i, (h, b) in enumerate(chains):
        wh, wl = split(2.0 * ccols[i] * invs[i])
        uh, ul = split(2.0 * invs[i])
        wt = dot_nn(jnp.concatenate([rts[i], rts[i]], axis=1), jnp.concatenate([wh, wl], axis=0))
        ut = dot_nn(jnp.concatenate([vts[i], vts[i]], axis=1), jnp.concatenate([uh, ul], axis=0))
        z = jnp.concatenate([wt, ut], axis=0) * crows[i]
        z_ref[h, b] = z
        rr = jnp.concatenate([rs[i], rs[i]], axis=0)
        pairs.append(base + sign * dot_nn(wide(z), rr))
    for h in range(HEADS):
        own = pairs[h * nblk : (h + 1) * nblk]
        while len(own) > 1:
            own = [compose(own[i], own[i + 1]) for i in range(0, len(own), 2)]
        m_ref[h] = own[0]


def compose(first, second):
    moved = mm(first, second[:D])
    keep = jnp.concatenate([jnp.zeros((D, D), f32), second[D:]], axis=0)
    return moved + keep


def whole(*arrays):
    return [pl.BlockSpec(memory_space=pltpu.VMEM)] * len(arrays)


def factor_call(k, v):
    steps = k.shape[0] // HEADS
    nblk = steps // BLK
    return pl.pallas_call(
        factor_kernel,
        in_specs=[pl.BlockSpec(memory_space=pl.ANY)] * 2,
        out_specs=[pl.BlockSpec(memory_space=pltpu.VMEM)] * 3,
        out_shape=[
            jax.ShapeDtypeStruct((HEADS, 2 * D, D), f32),
            jax.ShapeDtypeStruct((HEADS, nblk, 2 * D, D), f32),
            jax.ShapeDtypeStruct((HEADS, steps, D), bf16),
        ],
        scratch_shapes=[pltpu.VMEM((HEADS * steps, D), bf16)] * 2
        + [pltpu.VMEM((HEADS * steps, D), f32)] * 2
        + [pltpu.SemaphoreType.DMA((2, 4))],
        compiler_params=pltpu.CompilerParams(vmem_limit_bytes=16 << 20),
        name="factor",
    )(k, v)


def chip_kernel(own_ref, sib_ref, *out_refs):
    x = place_x()
    for k in range(XS):
        head = lax.rem(x + k, HEADS)
        out_refs[k][...] = compose(sib_ref[head], own_ref[head])


def ordered_cyclic(slots, place, scratch):
    n = len(slots)
    for k in range(n):
        scratch[lax.rem(place + n - k, n)] = slots[k][...]


def ordered_xor(slots, place, scratch):
    for k, slot in enumerate(slots):
        scratch[place ^ k] = slot[...]


def msg_compose(rows, second):
    moved = mm(rows, second[:D])
    return jnp.concatenate([moved[:D], moved[D:] + second[D:]], axis=0)


def advance(state, second):
    return mm(state, second[:D]) + second[D:]


def write_total(total_ref, hold):
    tail = msg_compose(hold[2], hold[3])
    total_ref[...] = msg_compose(msg_compose(hold[0], hold[1]), tail)


def row_kernel(s0, s2, s1, s3, after_ref, total_ref, hold):
    ordered_cyclic([s0, s1, s2, s3], place_x(), hold)
    write_total(total_ref, hold)


def column_kernel(s0, s1, s3, s2, after_ref, total_ref, hold):
    ordered_xor([s0, s1, s2, s3], place_y(), hold)
    write_total(total_ref, hold)


def place_prefix(place, hold):
    first = hold[0]
    second = msg_compose(first, hold[1])
    third = msg_compose(second, hold[2])
    out = jnp.where(iota2((MSG, D), 0) == iota2((MSG, D), 1), 1.0, 0.0)
    for i, prefix in enumerate((first, second, third)):
        out = jnp.where(place == i + 1, prefix, out)
    return out


def path_kernel(*refs):
    xslots, yslots = refs[:4], [refs[i] for i in (4, 5, 7, 6)]
    init_ref, after_ref, path_ref, start_ref, xhold, yhold = refs[8:]
    x = place_x()
    y = place_y()
    ordered_cyclic(xslots, x, xhold)
    ordered_xor(yslots, y, yhold)
    here = place_prefix(y, yhold)
    first = xhold[0]
    second = msg_compose(first, xhold[1])
    third = msg_compose(second, xhold[2])
    path_ref[0] = here
    left = wide(here)
    for i, prefix in enumerate((first, second, third)):
        moved = mm_pre(left, tall_wide(prefix[:D]))
        path_ref[i + 1, :D, :] = moved[:D]
        path_ref[i + 1, D:, :] = moved[D:] + prefix[D:]
    start_ref[...] = init_ref[x].T


def lead_kernel(s0, s1, s2, s3, start_ref, after_ref, lead_ref, hold):
    ordered_xor([s0, s1, s2, s3], lax.rem(place_seg(), ZG), hold)
    tail = msg_compose(hold[2], hold[3])
    state = advance(advance(start_ref[...], hold[0]), hold[1])
    lead_ref[...] = advance(state, tail)


def fuse_kernel(s0, s1, s2, s3, path_ref, after_ref, fuse_ref, hold):
    g = lax.rem(place_seg(), ZG)
    ordered_xor([s0, s1, s2, s3], g, hold)
    window = place_prefix(g, hold)
    left = wide(window)
    for i in range(XS):
        path = path_ref[i]
        moved = mm_pre(left, tall_wide(path[:D]))
        fuse_ref[i, :D, :] = moved[:D]
        fuse_ref[i, D:, :] = moved[D:] + path[D:]


def entry_kernel(start_ref, early_ref, fuse_ref, o0, o1, o2, o3, scratch):
    x = place_x()
    state = jnp.where(place_seg() >= ZG, early_ref[...], start_ref[...])
    left = wide(state)
    for i in range(XS):
        scratch[i] = mm_pre(left, tall_wide(fuse_ref[i, :D, :])) + fuse_ref[i, D:, :]
    for k, out in enumerate((o0, o1, o2, o3)):
        out[...] = scratch[lax.rem(x + k, XS)]


def reach_kernel(
    q_ref, r_ref, z_ref, sib_ref, after_ref, reach_ref, base_ref, rows, *, head
):
    tokens = reach_ref.shape[0]
    nblk = z_ref.shape[0]
    span = tokens // nblk
    rows[...] = q_ref[...].astype(f32)
    visible = iota2((span, BLK), 1) <= REFL * iota2((span, BLK), 0) + (REFL - 1)
    base = jnp.where(iota2((2 * D, D), 0) == iota2((2 * D, D), 1), 1.0, 0.0)
    sign = jnp.where(iota2((2 * D, D), 0) < D, -1.0, 1.0)
    prefixes = [jnp.where(place_core() == 1, sib_ref[...], base)]
    for b in range(nblk - 1):
        rr = jnp.concatenate([r_ref[b * BLK : (b + 1) * BLK, :]] * 2, axis=0)
        piece = base + sign * dot_nn(wide(z_ref[b]), rr)
        prefixes.append(compose(prefixes[b], piece))
    projects, locals_ = [], []
    for b in range(nblk):
        q = rows[pl.ds(head + HEADS * span * b, span, stride=HEADS), :]
        scores = dot_nt(q.astype(bf16), r_ref[b * BLK : (b + 1) * BLK, :])
        sz = mm_nt(jnp.where(visible, scores, 0.0), z_ref[b])
        projects.append(q - sz[:, :D])
        locals_.append(sz[:, D:])
    moves = [mm_nt(projects[b], prefixes[b]) for b in range(nblk)]
    for b in range(nblk):
        part = slice(b * span, (b + 1) * span)
        reach_ref[part, :] = wide(moves[b][:, :D])
        base_ref[part, :] = moves[b][:, D:] + locals_[b]


def reach_call(q, r, z, sib, after, head):
    tokens = q.shape[0] // HEADS

    def spec(array):
        rest = array.shape[1:]
        return pl.BlockSpec((None, *rest), lambda i: (head,) + (0,) * len(rest))

    return pl.pallas_call(
        functools.partial(reach_kernel, head=head),
        grid=(1,),
        in_specs=[
            pl.BlockSpec(q.shape, lambda i: (0, 0)),
            spec(r),
            spec(z),
            spec(sib),
            pl.BlockSpec(memory_space=pl.ANY),
        ],
        out_specs=[
            pl.BlockSpec((tokens, 2 * D), lambda i: (0, 0)),
            pl.BlockSpec((tokens, D), lambda i: (0, 0)),
        ],
        out_shape=[
            jax.ShapeDtypeStruct((tokens, 2 * D), bf16),
            jax.ShapeDtypeStruct((tokens, D), f32),
        ],
        scratch_shapes=[pltpu.VMEM(q.shape, f32)],
        compiler_params=pltpu.CompilerParams(vmem_limit_bytes=6 << 20),
        cost_estimate=pl.CostEstimate(
            flops=400_000_000, bytes_accessed=3_000_000, transcendentals=0
        ),
        name="reach",
    )(q, r, z, sib, after)


def read_kernel(*refs):
    reaches, bases = refs[: 2 * HEADS : 2], refs[1 : 2 * HEADS : 2]
    refs = refs[2 * HEADS :]
    mine, other = refs[:HEADS], refs[HEADS : 2 * HEADS]
    mine, other = ([part[i] for i in (0, 2, 1, 3)] for part in (mine, other))
    gain_ref, out_hbm, states, rows, out, sems = refs[2 * HEADS :]
    x = place_x()

    @pl.when(place_core() == 0)
    def _():
        ordered_cyclic(other, x, states)

    @pl.when(place_core() != 0)
    def _():
        ordered_cyclic(mine, x, states)

    rights = []
    for h in range(HEADS):
        both = jnp.concatenate(split(states[h]), axis=0)
        rights.append(jnp.concatenate([both, both], axis=1))
    pieces = sems.shape[0]
    span = reaches[0].shape[0] // pieces
    copies = []
    for i in range(pieces):
        part = slice(i * span, (i + 1) * span)
        for h in range(HEADS):
            moved = dot_nt(reaches[h][part, :], rights[h])
            read = moved[:, :D] + moved[:, D:] + bases[h][part, :]
            scale = lax.rsqrt(jnp.mean(read * read, axis=-1, keepdims=True) + 1e-06)
            rows[pl.ds(i * span * HEADS + h, span, stride=HEADS), :] = (
                read * scale * gain_ref[h : h + 1, :]
            )
        block = pl.ds(i * span * HEADS, span * HEADS)
        out[block, :] = rows[block, :].astype(bf16)
        copies.append(pltpu.make_async_copy(out.at[block], out_hbm.at[block], sems.at[i]))
        copies[-1].start()
    for copy in copies:
        copy.wait()


def read_call(arrays, tokens):
    shape = (tokens * HEADS, D)
    return pl.pallas_call(
        read_kernel,
        in_specs=whole(*arrays),
        out_specs=pl.BlockSpec(memory_space=pl.ANY),
        out_shape=jax.ShapeDtypeStruct(shape, bf16),
        scratch_shapes=[
            pltpu.VMEM((HEADS, D, D), f32),
            pltpu.VMEM(shape, f32),
            pltpu.VMEM(shape, bf16),
            pltpu.SemaphoreType.DMA((2,)),
        ],
        compiler_params=pltpu.CompilerParams(vmem_limit_bytes=8 << 20),
        name="read",
    )(*arrays)


def small_call(kernel, name, arrays, outs, scratch=(), after=None, limit=4, out_dtype=f32):
    extra = [] if after is None else [after]
    return pl.pallas_call(
        kernel,
        in_specs=whole(*arrays)
        + [pl.BlockSpec(memory_space=pl.ANY)] * len(extra),
        out_specs=whole(*outs),
        out_shape=[jax.ShapeDtypeStruct(s, out_dtype) for s in outs],
        scratch_shapes=[pltpu.VMEM(s, f32) for s in scratch],
        compiler_params=pltpu.CompilerParams(vmem_limit_bytes=limit << 20),
        name=name,
    )(*arrays, *extra)


def seat(y, x, c):
    return (y * XS + x) * CS + c


def plane_perm(move, spare):
    pairs = []
    for y in range(YS):
        for x in range(XS):
            pairs.append((seat(y, x, 0), seat(*spare(y, x), 0)))
            pairs.append((seat(y, x, 1), seat(*move(y, x), 1)))
    return pairs


def depth_perm(segs, move):
    pairs = []
    for y in range(YS):
        for x in range(XS):
            for g in range(segs):
                pairs.append((seat(y, x, 0) * segs + g, seat(y, x ^ 1, 0) * segs + g))
                at = seat(y, x, 1) * segs
                pairs.append((at + g, at + move(g)))
    return pairs


def chip_perm():
    return [(seat(y, x, c), seat(y, x, 1 - c)) for y in range(YS) for x in range(XS) for c in range(CS)]


def exchange(slots, axis, perms, order):
    out = list(slots)
    for k in order:
        out[k] = lax.ppermute(slots[k], axis, perms[k - 1])
    return out


def per_device(query_rows, key_rows, value_rows, out_gain, initial_state):
    tokens = query_rows.shape[1]
    steps = tokens * REFL
    swap = chip_perm()
    near_x = lambda y, x: (y, x ^ 1)
    near_y = lambda y, x: (y ^ 1, x)
    along_x = [
        plane_perm(lambda y, x, k=k: (y, (x + k) % XS), near_y) for k in range(1, XS)
    ]
    along_y = [plane_perm(lambda y, x, k=k: (y ^ k, x), near_x) for k in range(1, YS)]
    segs = lax.axis_size("seg")
    along_z = [depth_perm(segs, lambda g, k=k: g ^ k) for k in range(1, ZG)]
    jump = depth_perm(segs, lambda g: segs - 1 - g)

    keys = key_rows.reshape(steps * HEADS, D)
    values = value_rows.reshape(steps * HEADS, D)
    query = query_rows.reshape(tokens * HEADS, D)
    keys = pltpu.with_memory_space_constraint(keys, pltpu.HBM)
    values = pltpu.with_memory_space_constraint(values, pltpu.HBM)
    pair, z, r = factor_call(keys, values)
    sib = lax.ppermute(pair, "seq", swap)
    slots = small_call(chip_kernel, "chip", [pair, sib], [(MSG, D)] * XS)
    slots = exchange(slots, "seq", along_x, (2, 1, 3))
    reaches = [reach_call(query, r, z, sib, slots[0], 0)]
    xslots = slots
    (total,) = small_call(
        row_kernel, "row", [slots[i] for i in (0, 2, 1, 3)], [(MSG, D)], [(XS, MSG, D)], after=reaches[-1][0]
    )
    slots = exchange([total] * YS, "seq", along_y, (1, 3, 2))
    yslots = slots
    reaches.append(reach_call(query, r, z, sib, total, 1))
    (total,) = small_call(
        column_kernel, "column", [slots[i] for i in (0, 1, 3, 2)], [(MSG, D)], [(YS, MSG, D)], after=reaches[-1][0]
    )
    slots = exchange([total] * ZG, ("seq", "seg"), along_z, (1, 2, 3))
    path, start = small_call(
        path_kernel,
        "path",
        [*xslots, *(yslots[i] for i in (0, 1, 3, 2)), initial_state],
        [(XS, MSG, D), (D, D)],
        [(XS, MSG, D), (YS, MSG, D)],
        after=total,
    )
    reaches.append(reach_call(query, r, z, sib, path, 2))
    (lead,) = small_call(
        lead_kernel,
        "lead",
        [*slots, start],
        [(D, D)],
        [(ZG, MSG, D)],
        after=reaches[-1][0],
    )
    early = lax.ppermute(lead, ("seq", "seg"), jump)
    (fused,) = small_call(
        fuse_kernel,
        "fuse",
        [*slots, path],
        [(XS, MSG, D)],
        [(ZG, MSG, D)],
        after=lead,
    )
    slots = small_call(
        entry_kernel,
        "entry",
        [start, early, fused],
        [(D, D)] * XS,
        [(XS, D, D)],
    )
    slots = exchange(slots, "seq", along_x, (2, 1, 3))
    reaches.append(reach_call(query, r, z, sib, slots[0], 3))
    last = reaches[-1][0]
    for k in (2, 1, 3):
        slots[k], last = lax.optimization_barrier((slots[k], last))
    reaches[-1] = (last, reaches[-1][1])
    others = exchange(slots, "seq", [swap] * XS, (2, 1, 3))
    others[0] = lax.ppermute(slots[0], "seq", swap)
    arrays = [a for pair in reaches for a in pair] + [part[i] for part in (slots, others) for i in (0, 2, 1, 3)] + [out_gain]
    out = read_call(arrays, tokens)
    return out.reshape(1, tokens, HEADS, D)


def solution(mesh):
    return jax.shard_map(
        per_device,
        mesh=mesh,
        in_specs=(
            P("seg", "seq", None, None),
            P("seg", "seq", None, None, None),
            P("seg", "seq", None, None, None),
            P(),
            P(),
        ),
        out_specs=P("seg", "seq", None, None),
        check_vma=False,
    )
```

```python
import functools

import jax
import jax.numpy as jnp
from jax import lax
from jax.experimental import pallas as pl
from jax.experimental.pallas import tpu as pltpu
from jax.sharding import PartitionSpec as P

D = 128
HEADS = 4
REFL = 2
BLK = 128
XS = 4
YS = 4
CS = 2
ZG = 4
MSG = 2 * D

f32 = jnp.float32
bf16 = jnp.bfloat16


def split(x):
    high = x.astype(bf16)
    low = (x - high.astype(f32)).astype(bf16)
    return high, low


def dot_nn(a, b):
    return lax.dot_general(a, b, (((1,), (0,)), ((), ())), preferred_element_type=f32)


def dot_nt(a, b):
    return lax.dot_general(a, b, (((1,), (1,)), ((), ())), preferred_element_type=f32)


def wide(x):
    high, low = split(x)
    return jnp.concatenate([high, low], axis=1)


def tall_wide(x):
    row = wide(x)
    return jnp.concatenate([row, row], axis=0)


def mm_pre(left_wide, right_tall):
    out = dot_nn(left_wide, right_tall)
    n = out.shape[1] // 2
    return out[:, :n] + out[:, n:]


def mm(a, b):
    return mm_pre(wide(a), tall_wide(b))


def mm_nt(a, b):
    ah, al = split(a)
    bh, bl = split(b)
    return dot_nt(ah, bh) + dot_nt(ah, bl) + dot_nt(al, bh)


def place_x():
    return lax.rem(lax.axis_index("seq") // CS, XS)


def place_y():
    return lax.axis_index("seq") // (CS * XS)


def place_core():
    return lax.rem(lax.axis_index("seq"), CS)


def place_seg():
    return lax.axis_index("seg")


def iota2(shape, dim):
    return lax.broadcasted_iota(jnp.int32, shape, dim)


def factor_kernel(k_hbm, v_hbm, m_ref, z_ref, r_ref, k_ref, v_ref, keys, values, sems):
    pieces = sems.shape[1]
    size = k_ref.shape[0] // pieces
    copies = [
        [
            pltpu.make_async_copy(
                src.at[pl.ds(i * size, size)], dst.at[pl.ds(i * size, size)], sems.at[j, i]
            )
            for i in range(pieces)
        ]
        for j, (src, dst) in enumerate(((k_hbm, k_ref), (v_hbm, v_ref)))
    ]
    for copy in copies[0]:
        copy.start()
    for i, copy in enumerate(copies[0]):
        copy.wait()
        keys[i * size : (i + 1) * size] = k_ref[i * size : (i + 1) * size].astype(f32)
    for copy in copies[1]:
        copy.start()
    nblk = r_ref.shape[1] // BLK
    row = iota2((BLK, BLK), 0)
    col = iota2((BLK, BLK), 1)
    eye = row == col
    pair = ((row >> 1) == (col >> 1)) & (row < col)
    chains = [(h, b) for h in range(HEADS) for b in range(nblk)]
    rs, rts, vts, uppers, invs, ccols, crows = [], [], [], [], [], [], []
    for h, b in chains:
        rows = pl.ds(h + HEADS * BLK * b, BLK, stride=HEADS)
        r = keys[rows, :].astype(bf16)
        r_ref[h, b * BLK : (b + 1) * BLK, :] = r
        rt = r.T
        gram = dot_nn(r, rt)
        diag = jnp.where(eye, gram, 0.0)
        ccol = lax.rsqrt(jnp.sum(diag, axis=1, keepdims=True) + 1e-06)
        crow = lax.rsqrt(jnp.sum(diag, axis=0, keepdims=True) + 1e-06)
        upper = jnp.where(row < col, 2.0 * ccol * crow * gram, 0.0)
        inv = jnp.where(eye, 1.0, 0.0) - jnp.where(pair, upper, 0.0)
        rs.append(r)
        rts.append(rt)
        uppers.append(upper)
        invs.append(inv)
        ccols.append(ccol)
        crows.append(crow)
    for level in range(1, 7):
        off = ((row >> (level + 1)) == (col >> (level + 1))) & (
            (row >> level) < (col >> level)
        )
        talls = [tall_wide(inv) for inv in invs]
        mids = [
            mm_pre(wide(jnp.where(off, upper, 0.0)), tall) for upper, tall in zip(uppers, talls)
        ]
        invs = [inv - mm(inv, mid) for inv, mid in zip(invs, mids)]
    for i, copy in enumerate(copies[1]):
        copy.wait()
        values[i * size : (i + 1) * size] = v_ref[i * size : (i + 1) * size].astype(f32)
    for h, b in chains:
        rows = pl.ds(h + HEADS * BLK * b, BLK, stride=HEADS)
        vts.append(values[rows, :].astype(bf16).T)
    pairs = []
    base = jnp.where(iota2((2 * D, D), 0) == iota2((2 * D, D), 1), 1.0, 0.0)
    sign = jnp.where(iota2((2 * D, D), 0) < D, -1.0, 1.0)
    for i, (h, b) in enumerate(chains):
        wh, wl = split(2.0 * ccols[i] * invs[i])
        uh, ul = split(2.0 * invs[i])
        wt = dot_nn(jnp.concatenate([rts[i], rts[i]], axis=1), jnp.concatenate([wh, wl], axis=0))
        ut = dot_nn(jnp.concatenate([vts[i], vts[i]], axis=1), jnp.concatenate([uh, ul], axis=0))
        z = jnp.concatenate([wt, ut], axis=0) * crows[i]
        z_ref[h, b] = z
        rr = jnp.concatenate([rs[i], rs[i]], axis=0)
        pairs.append(base + sign * dot_nn(wide(z), rr))
    for h in range(HEADS):
        own = pairs[h * nblk : (h + 1) * nblk]
        while len(own) > 1:
            own = [compose(own[i], own[i + 1]) for i in range(0, len(own), 2)]
        m_ref[h] = own[0]


def compose(first, second):
    moved = mm(first, second[:D])
    keep = jnp.concatenate([jnp.zeros((D, D), f32), second[D:]], axis=0)
    return moved + keep


def whole(*arrays):
    return [pl.BlockSpec(memory_space=pltpu.VMEM)] * len(arrays)


def factor_call(k, v):
    steps = k.shape[0] // HEADS
    nblk = steps // BLK
    return pl.pallas_call(
        factor_kernel,
        in_specs=[pl.BlockSpec(memory_space=pl.ANY)] * 2,
        out_specs=[pl.BlockSpec(memory_space=pltpu.VMEM)] * 3,
        out_shape=[
            jax.ShapeDtypeStruct((HEADS, 2 * D, D), f32),
            jax.ShapeDtypeStruct((HEADS, nblk, 2 * D, D), f32),
            jax.ShapeDtypeStruct((HEADS, steps, D), bf16),
        ],
        scratch_shapes=[pltpu.VMEM((HEADS * steps, D), bf16)] * 2
        + [pltpu.VMEM((HEADS * steps, D), f32)] * 2
        + [pltpu.SemaphoreType.DMA((2, 4))],
        compiler_params=pltpu.CompilerParams(vmem_limit_bytes=16 << 20),
        name="factor",
    )(k, v)


def chip_kernel(own_ref, sib_ref, *out_refs):
    x = place_x()
    for k in range(XS):
        head = x ^ k
        out_refs[k][...] = compose(sib_ref[head], own_ref[head])


def ordered_xor(slots, place, scratch):
    for k, slot in enumerate(slots):
        scratch[place ^ k] = slot[...]


def msg_compose(rows, second):
    moved = mm(rows, second[:D])
    return jnp.concatenate([moved[:D], moved[D:] + second[D:]], axis=0)


def advance(state, second):
    return mm(state, second[:D]) + second[D:]


def write_total(total_ref, hold):
    tail = msg_compose(hold[2], hold[3])
    total_ref[...] = msg_compose(msg_compose(hold[0], hold[1]), tail)


def row_kernel(s0, s2, s1, s3, after_ref, total_ref, hold):
    ordered_xor([s0, s1, s2, s3], place_x(), hold)
    write_total(total_ref, hold)


def column_kernel(s0, s1, s3, s2, after_ref, total_ref, hold):
    ordered_xor([s0, s1, s2, s3], place_y(), hold)
    write_total(total_ref, hold)


def place_prefix(place, hold):
    first = hold[0]
    second = msg_compose(first, hold[1])
    third = msg_compose(second, hold[2])
    out = jnp.where(iota2((MSG, D), 0) == iota2((MSG, D), 1), 1.0, 0.0)
    for i, prefix in enumerate((first, second, third)):
        out = jnp.where(place == i + 1, prefix, out)
    return out


def path_kernel(*refs):
    xslots, yslots = refs[:4], [refs[i] for i in (4, 5, 7, 6)]
    init_ref, after_ref, path_ref, start_ref, xhold, yhold = refs[8:]
    x = place_x()
    y = place_y()
    ordered_xor(xslots, x, xhold)
    ordered_xor(yslots, y, yhold)
    here = place_prefix(y, yhold)
    first = xhold[0]
    second = msg_compose(first, xhold[1])
    third = msg_compose(second, xhold[2])
    path_ref[0] = here
    left = wide(here)
    for i, prefix in enumerate((first, second, third)):
        moved = mm_pre(left, tall_wide(prefix[:D]))
        path_ref[i + 1, :D, :] = moved[:D]
        path_ref[i + 1, D:, :] = moved[D:] + prefix[D:]
    start_ref[...] = init_ref[x].T


def lead_kernel(s0, s1, s2, s3, start_ref, after_ref, lead_ref, hold):
    ordered_xor([s0, s1, s2, s3], lax.rem(place_seg(), ZG), hold)
    tail = msg_compose(hold[2], hold[3])
    state = advance(advance(start_ref[...], hold[0]), hold[1])
    lead_ref[...] = advance(state, tail)


def fuse_kernel(s0, s1, s2, s3, path_ref, after_ref, fuse_ref, hold):
    g = lax.rem(place_seg(), ZG)
    ordered_xor([s0, s1, s2, s3], g, hold)
    window = place_prefix(g, hold)
    left = wide(window)
    for i in range(XS):
        path = path_ref[i]
        moved = mm_pre(left, tall_wide(path[:D]))
        fuse_ref[i, :D, :] = moved[:D]
        fuse_ref[i, D:, :] = moved[D:] + path[D:]


def entry_kernel(start_ref, early_ref, fuse_ref, o0, o1, o2, o3, scratch):
    x = place_x()
    state = jnp.where(place_seg() >= ZG, early_ref[...], start_ref[...])
    left = wide(state)
    for i in range(XS):
        scratch[i] = mm_pre(left, tall_wide(fuse_ref[i, :D, :])) + fuse_ref[i, D:, :]
    for k, out in enumerate((o0, o1, o2, o3)):
        out[...] = scratch[x ^ k]


def reach_kernel(
    q_ref, r_ref, z_ref, sib_ref, after_ref, reach_ref, base_ref, rows, *, head
):
    tokens = reach_ref.shape[0]
    nblk = z_ref.shape[0]
    span = tokens // nblk
    rows[...] = q_ref[...].astype(f32)
    visible = iota2((span, BLK), 1) <= REFL * iota2((span, BLK), 0) + (REFL - 1)
    base = jnp.where(iota2((2 * D, D), 0) == iota2((2 * D, D), 1), 1.0, 0.0)
    sign = jnp.where(iota2((2 * D, D), 0) < D, -1.0, 1.0)
    prefixes = [jnp.where(place_core() == 1, sib_ref[...], base)]
    for b in range(nblk - 1):
        rr = jnp.concatenate([r_ref[b * BLK : (b + 1) * BLK, :]] * 2, axis=0)
        piece = base + sign * dot_nn(wide(z_ref[b]), rr)
        prefixes.append(compose(prefixes[b], piece))
    projects, locals_ = [], []
    for b in range(nblk):
        q = rows[pl.ds(head + HEADS * span * b, span, stride=HEADS), :]
        scores = dot_nt(q.astype(bf16), r_ref[b * BLK : (b + 1) * BLK, :])
        sz = mm_nt(jnp.where(visible, scores, 0.0), z_ref[b])
        projects.append(q - sz[:, :D])
        locals_.append(sz[:, D:])
    moves = [mm_nt(projects[b], prefixes[b]) for b in range(nblk)]
    for b in range(nblk):
        part = slice(b * span, (b + 1) * span)
        reach_ref[part, :] = wide(moves[b][:, :D])
        base_ref[part, :] = moves[b][:, D:] + locals_[b]


def reach_call(q, r, z, sib, after, head):
    tokens = q.shape[0] // HEADS

    def spec(array):
        rest = array.shape[1:]
        return pl.BlockSpec((None, *rest), lambda i: (head,) + (0,) * len(rest))

    return pl.pallas_call(
        functools.partial(reach_kernel, head=head),
        grid=(1,),
        in_specs=[
            pl.BlockSpec(q.shape, lambda i: (0, 0)),
            spec(r),
            spec(z),
            spec(sib),
            pl.BlockSpec(memory_space=pl.ANY),
        ],
        out_specs=[
            pl.BlockSpec((tokens, 2 * D), lambda i: (0, 0)),
            pl.BlockSpec((tokens, D), lambda i: (0, 0)),
        ],
        out_shape=[
            jax.ShapeDtypeStruct((tokens, 2 * D), bf16),
            jax.ShapeDtypeStruct((tokens, D), f32),
        ],
        scratch_shapes=[pltpu.VMEM(q.shape, f32)],
        compiler_params=pltpu.CompilerParams(vmem_limit_bytes=6 << 20),
        cost_estimate=pl.CostEstimate(
            flops=400_000_000, bytes_accessed=3_000_000, transcendentals=0
        ),
        name="reach",
    )(q, r, z, sib, after)


def read_kernel(*refs):
    reaches, bases = refs[: 2 * HEADS : 2], refs[1 : 2 * HEADS : 2]
    refs = refs[2 * HEADS :]
    mine, other = refs[:HEADS], refs[HEADS : 2 * HEADS]
    mine, other = ([part[i] for i in (0, 2, 1, 3)] for part in (mine, other))
    gain_ref, out_hbm, states, rows, out, sems = refs[2 * HEADS :]
    x = place_x()

    @pl.when(place_core() == 0)
    def _():
        ordered_xor(other, x, states)

    @pl.when(place_core() != 0)
    def _():
        ordered_xor(mine, x, states)

    rights = []
    for h in range(HEADS):
        both = jnp.concatenate(split(states[h]), axis=0)
        rights.append(jnp.concatenate([both, both], axis=1))
    pieces = sems.shape[0]
    span = reaches[0].shape[0] // pieces
    copies = []
    for i in range(pieces):
        part = slice(i * span, (i + 1) * span)
        for h in range(HEADS):
            moved = dot_nt(reaches[h][part, :], rights[h])
            read = moved[:, :D] + moved[:, D:] + bases[h][part, :]
            scale = lax.rsqrt(jnp.mean(read * read, axis=-1, keepdims=True) + 1e-06)
            rows[pl.ds(i * span * HEADS + h, span, stride=HEADS), :] = (
                read * scale * gain_ref[h : h + 1, :]
            )
        block = pl.ds(i * span * HEADS, span * HEADS)
        out[block, :] = rows[block, :].astype(bf16)
        copies.append(pltpu.make_async_copy(out.at[block], out_hbm.at[block], sems.at[i]))
        copies[-1].start()
    for copy in copies:
        copy.wait()


def read_call(arrays, tokens):
    shape = (tokens * HEADS, D)
    return pl.pallas_call(
        read_kernel,
        in_specs=whole(*arrays),
        out_specs=pl.BlockSpec(memory_space=pl.ANY),
        out_shape=jax.ShapeDtypeStruct(shape, bf16),
        scratch_shapes=[
            pltpu.VMEM((HEADS, D, D), f32),
            pltpu.VMEM(shape, f32),
            pltpu.VMEM(shape, bf16),
            pltpu.SemaphoreType.DMA((2,)),
        ],
        compiler_params=pltpu.CompilerParams(vmem_limit_bytes=8 << 20),
        name="read",
    )(*arrays)


def small_call(kernel, name, arrays, outs, scratch=(), after=None, limit=4, out_dtype=f32):
    extra = [] if after is None else [after]
    return pl.pallas_call(
        kernel,
        in_specs=whole(*arrays)
        + [pl.BlockSpec(memory_space=pl.ANY)] * len(extra),
        out_specs=whole(*outs),
        out_shape=[jax.ShapeDtypeStruct(s, out_dtype) for s in outs],
        scratch_shapes=[pltpu.VMEM(s, f32) for s in scratch],
        compiler_params=pltpu.CompilerParams(vmem_limit_bytes=limit << 20),
        name=name,
    )(*arrays, *extra)


def seat(y, x, c):
    return (y * XS + x) * CS + c


def plane_perm(move, spare):
    pairs = []
    for y in range(YS):
        for x in range(XS):
            pairs.append((seat(y, x, 0), seat(*spare(y, x), 0)))
            pairs.append((seat(y, x, 1), seat(*move(y, x), 1)))
    return pairs


def depth_perm(segs, move):
    pairs = []
    for y in range(YS):
        for x in range(XS):
            for g in range(segs):
                pairs.append((seat(y, x, 0) * segs + g, seat(y, x ^ 1, 0) * segs + g))
                at = seat(y, x, 1) * segs
                pairs.append((at + g, at + move(g)))
    return pairs


def chip_perm():
    return [(seat(y, x, c), seat(y, x, 1 - c)) for y in range(YS) for x in range(XS) for c in range(CS)]


def exchange(slots, axis, perms, order):
    out = list(slots)
    for k in order:
        out[k] = lax.ppermute(slots[k], axis, perms[k - 1])
    return out


def per_device(query_rows, key_rows, value_rows, out_gain, initial_state):
    tokens = query_rows.shape[1]
    steps = tokens * REFL
    swap = chip_perm()
    near_x = lambda y, x: (y, x ^ 1)
    near_y = lambda y, x: (y ^ 1, x)
    along_x = [
        plane_perm(lambda y, x, k=k: (y, x ^ k), near_y) for k in range(1, XS)
    ]
    along_y = [plane_perm(lambda y, x, k=k: (y ^ k, x), near_x) for k in range(1, YS)]
    segs = lax.axis_size("seg")
    along_z = [depth_perm(segs, lambda g, k=k: g ^ k) for k in range(1, ZG)]
    jump = depth_perm(segs, lambda g: segs - 1 - g)

    keys = key_rows.reshape(steps * HEADS, D)
    values = value_rows.reshape(steps * HEADS, D)
    query = query_rows.reshape(tokens * HEADS, D)
    keys = pltpu.with_memory_space_constraint(keys, pltpu.HBM)
    values = pltpu.with_memory_space_constraint(values, pltpu.HBM)
    pair, z, r = factor_call(keys, values)
    sib = lax.ppermute(pair, "seq", swap)
    slots = small_call(chip_kernel, "chip", [pair, sib], [(MSG, D)] * XS)
    slots = exchange(slots, "seq", along_x, (2, 1, 3))
    reaches = [reach_call(query, r, z, sib, slots[0], 0)]
    xslots = slots
    (total,) = small_call(
        row_kernel, "row", [slots[i] for i in (0, 2, 1, 3)], [(MSG, D)], [(XS, MSG, D)], after=reaches[-1][0]
    )
    slots = exchange([total] * YS, "seq", along_y, (1, 3, 2))
    yslots = slots
    reaches.append(reach_call(query, r, z, sib, total, 1))
    (total,) = small_call(
        column_kernel, "column", [slots[i] for i in (0, 1, 3, 2)], [(MSG, D)], [(YS, MSG, D)], after=reaches[-1][0]
    )
    slots = exchange([total] * ZG, ("seq", "seg"), along_z, (1, 2, 3))
    path, start = small_call(
        path_kernel,
        "path",
        [*xslots, *(yslots[i] for i in (0, 1, 3, 2)), initial_state],
        [(XS, MSG, D), (D, D)],
        [(XS, MSG, D), (YS, MSG, D)],
        after=total,
    )
    reaches.append(reach_call(query, r, z, sib, path, 2))
    (lead,) = small_call(
        lead_kernel,
        "lead",
        [*slots, start],
        [(D, D)],
        [(ZG, MSG, D)],
        after=reaches[-1][0],
    )
    early = lax.ppermute(lead, ("seq", "seg"), jump)
    (fused,) = small_call(
        fuse_kernel,
        "fuse",
        [*slots, path],
        [(XS, MSG, D)],
        [(ZG, MSG, D)],
        after=lead,
    )
    slots = small_call(
        entry_kernel,
        "entry",
        [start, early, fused],
        [(D, D)] * XS,
        [(XS, D, D)],
    )
    slots = exchange(slots, "seq", along_x, (2, 1, 3))
    reaches.append(reach_call(query, r, z, sib, slots[0], 3))
    last = reaches[-1][0]
    for k in (2, 1, 3):
        slots[k], last = lax.optimization_barrier((slots[k], last))
    reaches[-1] = (last, reaches[-1][1])
    others = exchange(slots, "seq", [swap] * XS, (2, 1, 3))
    others[0] = lax.ppermute(slots[0], "seq", swap)
    arrays = [a for pair in reaches for a in pair] + [part[i] for part in (slots, others) for i in (0, 2, 1, 3)] + [out_gain]
    out = read_call(arrays, tokens)
    return out.reshape(1, tokens, HEADS, D)


def solution(mesh):
    return jax.shard_map(
        per_device,
        mesh=mesh,
        in_specs=(
            P("seg", "seq", None, None),
            P("seg", "seq", None, None, None),
            P("seg", "seq", None, None, None),
            P(),
            P(),
        ),
        out_specs=P("seg", "seq", None, None),
        check_vma=False,
    )
```

```python
import functools

import jax
import jax.numpy as jnp
from jax import lax
from jax.experimental import pallas as pl
from jax.experimental.pallas import tpu as pltpu
from jax.sharding import PartitionSpec as P

D = 128
HEADS = 4
REFL = 2
BLK = 128
XS = 4
YS = 4
CS = 2
ZG = 4
MSG = 2 * D

f32 = jnp.float32
bf16 = jnp.bfloat16


def split(x):
    high = x.astype(bf16)
    low = (x - high.astype(f32)).astype(bf16)
    return high, low


def dot_nn(a, b):
    return lax.dot_general(a, b, (((1,), (0,)), ((), ())), preferred_element_type=f32)


def dot_nt(a, b):
    return lax.dot_general(a, b, (((1,), (1,)), ((), ())), preferred_element_type=f32)


def wide(x):
    high, low = split(x)
    return jnp.concatenate([high, low], axis=1)


def tall_wide(x):
    row = wide(x)
    return jnp.concatenate([row, row], axis=0)


def mm_pre(left_wide, right_tall):
    out = dot_nn(left_wide, right_tall)
    n = out.shape[1] // 2
    return out[:, :n] + out[:, n:]


def mm(a, b):
    return mm_pre(wide(a), tall_wide(b))


def mm_nt(a, b):
    ah, al = split(a)
    bh, bl = split(b)
    return dot_nt(ah, bh) + dot_nt(ah, bl) + dot_nt(al, bh)


def place_x():
    return lax.rem(lax.axis_index("seq") // CS, XS)


def place_y():
    return lax.axis_index("seq") // (CS * XS)


def place_core():
    return lax.rem(lax.axis_index("seq"), CS)


def place_seg():
    return lax.axis_index("seg")


def iota2(shape, dim):
    return lax.broadcasted_iota(jnp.int32, shape, dim)


def factor_kernel(k_hbm, v_hbm, m_ref, z_ref, r_ref, k_ref, v_ref, keys, values, sems):
    pieces = sems.shape[1]
    size = k_ref.shape[0] // pieces
    copies = [
        [
            pltpu.make_async_copy(
                src.at[pl.ds(i * size, size)], dst.at[pl.ds(i * size, size)], sems.at[j, i]
            )
            for i in range(pieces)
        ]
        for j, (src, dst) in enumerate(((k_hbm, k_ref), (v_hbm, v_ref)))
    ]
    for copy in copies[0]:
        copy.start()
    for i, copy in enumerate(copies[0]):
        copy.wait()
        keys[i * size : (i + 1) * size] = k_ref[i * size : (i + 1) * size].astype(f32)
    for copy in copies[1]:
        copy.start()
    nblk = r_ref.shape[1] // BLK
    row = iota2((BLK, BLK), 0)
    col = iota2((BLK, BLK), 1)
    eye = row == col
    pair = ((row >> 1) == (col >> 1)) & (row < col)
    chains = [(h, b) for h in range(HEADS) for b in range(nblk)]
    rs, rts, vts, uppers, invs, ccols, crows = [], [], [], [], [], [], []
    for h, b in chains:
        rows = pl.ds(h + HEADS * BLK * b, BLK, stride=HEADS)
        r = keys[rows, :].astype(bf16)
        r_ref[h, b * BLK : (b + 1) * BLK, :] = r
        rt = r.T
        gram = dot_nn(r, rt)
        diag = jnp.where(eye, gram, 0.0)
        ccol = lax.rsqrt(jnp.sum(diag, axis=1, keepdims=True) + 1e-06)
        crow = lax.rsqrt(jnp.sum(diag, axis=0, keepdims=True) + 1e-06)
        upper = jnp.where(row < col, 2.0 * ccol * crow * gram, 0.0)
        inv = jnp.where(eye, 1.0, 0.0) - jnp.where(pair, upper, 0.0)
        rs.append(r)
        rts.append(rt)
        uppers.append(upper)
        invs.append(inv)
        ccols.append(ccol)
        crows.append(crow)
    for level in range(1, 7):
        off = ((row >> (level + 1)) == (col >> (level + 1))) & (
            (row >> level) < (col >> level)
        )
        talls = [tall_wide(inv) for inv in invs]
        mids = [
            mm_pre(wide(jnp.where(off, upper, 0.0)), tall) for upper, tall in zip(uppers, talls)
        ]
        invs = [inv - mm(inv, mid) for inv, mid in zip(invs, mids)]
    for i, copy in enumerate(copies[1]):
        copy.wait()
        values[i * size : (i + 1) * size] = v_ref[i * size : (i + 1) * size].astype(f32)
    for h, b in chains:
        rows = pl.ds(h + HEADS * BLK * b, BLK, stride=HEADS)
        vts.append(values[rows, :].astype(bf16).T)
    pairs = []
    base = jnp.where(iota2((2 * D, D), 0) == iota2((2 * D, D), 1), 1.0, 0.0)
    sign = jnp.where(iota2((2 * D, D), 0) < D, -1.0, 1.0)
    for i, (h, b) in enumerate(chains):
        wh, wl = split(2.0 * ccols[i] * invs[i])
        uh, ul = split(2.0 * invs[i])
        wt = dot_nn(jnp.concatenate([rts[i], rts[i]], axis=1), jnp.concatenate([wh, wl], axis=0))
        ut = dot_nn(jnp.concatenate([vts[i], vts[i]], axis=1), jnp.concatenate([uh, ul], axis=0))
        z = jnp.concatenate([wt, ut], axis=0) * crows[i]
        z_ref[h, b] = z
        rr = jnp.concatenate([rs[i], rs[i]], axis=0)
        pairs.append(base + sign * dot_nn(wide(z), rr))
    for h in range(HEADS):
        own = pairs[h * nblk : (h + 1) * nblk]
        while len(own) > 1:
            own = [compose(own[i], own[i + 1]) for i in range(0, len(own), 2)]
        m_ref[h] = own[0]


def compose(first, second):
    moved = mm(first, second[:D])
    keep = jnp.concatenate([jnp.zeros((D, D), f32), second[D:]], axis=0)
    return moved + keep


def whole(*arrays):
    return [pl.BlockSpec(memory_space=pltpu.VMEM)] * len(arrays)


def factor_call(k, v):
    steps = k.shape[0] // HEADS
    nblk = steps // BLK
    return pl.pallas_call(
        factor_kernel,
        in_specs=[pl.BlockSpec(memory_space=pl.ANY)] * 2,
        out_specs=[pl.BlockSpec(memory_space=pltpu.VMEM)] * 3,
        out_shape=[
            jax.ShapeDtypeStruct((HEADS, 2 * D, D), f32),
            jax.ShapeDtypeStruct((HEADS, nblk, 2 * D, D), f32),
            jax.ShapeDtypeStruct((HEADS, steps, D), bf16),
        ],
        scratch_shapes=[pltpu.VMEM((HEADS * steps, D), bf16)] * 2
        + [pltpu.VMEM((HEADS * steps, D), f32)] * 2
        + [pltpu.SemaphoreType.DMA((2, 4))],
        compiler_params=pltpu.CompilerParams(vmem_limit_bytes=16 << 20),
        name="factor",
    )(k, v)


def chip_kernel(own_ref, sib_ref, *out_refs):
    x = place_x()
    for k in range(XS):
        head = x ^ k
        out_refs[k][...] = compose(sib_ref[head], own_ref[head])


def ordered_xor(slots, place, scratch):
    for k, slot in enumerate(slots):
        scratch[place ^ k] = slot[...]


def msg_compose(rows, second):
    moved = mm(rows, second[:D])
    return jnp.concatenate([moved[:D], moved[D:] + second[D:]], axis=0)


def advance(state, second):
    return mm(state, second[:D]) + second[D:]


def write_total(total_ref, hold):
    tail = msg_compose(hold[2], hold[3])
    total_ref[...] = msg_compose(msg_compose(hold[0], hold[1]), tail)


def row_kernel(s0, s2, s1, s3, after_ref, total_ref, hold):
    ordered_xor([s0, s1, s2, s3], place_x(), hold)
    write_total(total_ref, hold)


def column_kernel(s0, s1, s3, s2, after_ref, total_ref, hold):
    ordered_xor([s0, s1, s2, s3], place_y(), hold)
    write_total(total_ref, hold)


def place_prefix(place, hold):
    first = hold[0]
    second = msg_compose(first, hold[1])
    third = msg_compose(second, hold[2])
    out = jnp.where(iota2((MSG, D), 0) == iota2((MSG, D), 1), 1.0, 0.0)
    for i, prefix in enumerate((first, second, third)):
        out = jnp.where(place == i + 1, prefix, out)
    return out


def path_kernel(*refs):
    xslots, yslots = refs[:4], [refs[i] for i in (4, 5, 7, 6)]
    init_ref, after_ref, path_ref, start_ref, xhold, yhold = refs[8:]
    x = place_x()
    y = place_y()
    ordered_xor(xslots, x, xhold)
    ordered_xor(yslots, y, yhold)
    here = place_prefix(y, yhold)
    first = xhold[0]
    second = msg_compose(first, xhold[1])
    third = msg_compose(second, xhold[2])
    path_ref[0] = here
    left = wide(here)
    for i, prefix in enumerate((first, second, third)):
        moved = mm_pre(left, tall_wide(prefix[:D]))
        path_ref[i + 1, :D, :] = moved[:D]
        path_ref[i + 1, D:, :] = moved[D:] + prefix[D:]
    start_ref[...] = init_ref[x].T


def lead_kernel(s0, s1, s3, s2, start_ref, after_ref, lead_ref, hold):
    ordered_xor([s0, s1, s2, s3], lax.rem(place_seg(), ZG), hold)
    tail = msg_compose(hold[2], hold[3])
    state = advance(advance(start_ref[...], hold[0]), hold[1])
    lead_ref[...] = advance(state, tail)


def fuse_kernel(s0, s1, s2, s3, path_ref, after_ref, fuse_ref, hold):
    g = lax.rem(place_seg(), ZG)
    ordered_xor([s0, s1, s2, s3], g, hold)
    window = place_prefix(g, hold)
    left = wide(window)
    for i in range(XS):
        path = path_ref[i]
        moved = mm_pre(left, tall_wide(path[:D]))
        fuse_ref[i, :D, :] = moved[:D]
        fuse_ref[i, D:, :] = moved[D:] + path[D:]


def entry_kernel(start_ref, early_ref, fuse_ref, o0, o1, o2, o3, scratch):
    x = place_x()
    state = jnp.where(place_seg() >= ZG, early_ref[...], start_ref[...])
    left = wide(state)
    for i in range(XS):
        scratch[i] = mm_pre(left, tall_wide(fuse_ref[i, :D, :])) + fuse_ref[i, D:, :]
    for k, out in enumerate((o0, o1, o2, o3)):
        out[...] = scratch[x ^ k]


def reach_kernel(
    q_ref, r_ref, z_ref, sib_ref, after_ref, reach_ref, base_ref, rows, *, head
):
    tokens = reach_ref.shape[0]
    nblk = z_ref.shape[0]
    span = tokens // nblk
    rows[...] = q_ref[...].astype(f32)
    visible = iota2((span, BLK), 1) <= REFL * iota2((span, BLK), 0) + (REFL - 1)
    base = jnp.where(iota2((2 * D, D), 0) == iota2((2 * D, D), 1), 1.0, 0.0)
    sign = jnp.where(iota2((2 * D, D), 0) < D, -1.0, 1.0)
    prefixes = [jnp.where(place_core() == 1, sib_ref[...], base)]
    for b in range(nblk - 1):
        rr = jnp.concatenate([r_ref[b * BLK : (b + 1) * BLK, :]] * 2, axis=0)
        piece = base + sign * dot_nn(wide(z_ref[b]), rr)
        prefixes.append(compose(prefixes[b], piece))
    projects, locals_ = [], []
    for b in range(nblk):
        q = rows[pl.ds(head + HEADS * span * b, span, stride=HEADS), :]
        scores = dot_nt(q.astype(bf16), r_ref[b * BLK : (b + 1) * BLK, :])
        sz = mm_nt(jnp.where(visible, scores, 0.0), z_ref[b])
        projects.append(q - sz[:, :D])
        locals_.append(sz[:, D:])
    moves = [mm_nt(projects[b], prefixes[b]) for b in range(nblk)]
    for b in range(nblk):
        part = slice(b * span, (b + 1) * span)
        reach_ref[part, :] = wide(moves[b][:, :D])
        base_ref[part, :] = moves[b][:, D:] + locals_[b]


def reach_call(q, r, z, sib, after, head):
    tokens = q.shape[0] // HEADS

    def spec(array):
        rest = array.shape[1:]
        return pl.BlockSpec((None, *rest), lambda i: (head,) + (0,) * len(rest))

    return pl.pallas_call(
        functools.partial(reach_kernel, head=head),
        grid=(1,),
        in_specs=[
            pl.BlockSpec(q.shape, lambda i: (0, 0)),
            spec(r),
            spec(z),
            spec(sib),
            pl.BlockSpec(memory_space=pl.ANY),
        ],
        out_specs=[
            pl.BlockSpec((tokens, 2 * D), lambda i: (0, 0)),
            pl.BlockSpec((tokens, D), lambda i: (0, 0)),
        ],
        out_shape=[
            jax.ShapeDtypeStruct((tokens, 2 * D), bf16),
            jax.ShapeDtypeStruct((tokens, D), f32),
        ],
        scratch_shapes=[pltpu.VMEM(q.shape, f32)],
        compiler_params=pltpu.CompilerParams(vmem_limit_bytes=6 << 20),
        cost_estimate=pl.CostEstimate(
            flops=400_000_000, bytes_accessed=3_000_000, transcendentals=0
        ),
        name="reach",
    )(q, r, z, sib, after)


def read_kernel(*refs):
    reaches, bases = refs[: 2 * HEADS : 2], refs[1 : 2 * HEADS : 2]
    refs = refs[2 * HEADS :]
    mine, other = refs[:HEADS], refs[HEADS : 2 * HEADS]
    mine, other = ([part[i] for i in (0, 2, 1, 3)] for part in (mine, other))
    gain_ref, out_hbm, states, rows, out, sems = refs[2 * HEADS :]
    x = place_x()

    @pl.when(place_core() == 0)
    def _():
        ordered_xor(other, x, states)

    @pl.when(place_core() != 0)
    def _():
        ordered_xor(mine, x, states)

    rights = []
    for h in range(HEADS):
        both = jnp.concatenate(split(states[h]), axis=0)
        rights.append(jnp.concatenate([both, both], axis=1))
    pieces = sems.shape[0]
    span = reaches[0].shape[0] // pieces
    copies = []
    for i in range(pieces):
        part = slice(i * span, (i + 1) * span)
        for h in range(HEADS):
            moved = dot_nt(reaches[h][part, :], rights[h])
            read = moved[:, :D] + moved[:, D:] + bases[h][part, :]
            scale = lax.rsqrt(jnp.mean(read * read, axis=-1, keepdims=True) + 1e-06)
            rows[pl.ds(i * span * HEADS + h, span, stride=HEADS), :] = (
                read * scale * gain_ref[h : h + 1, :]
            )
        block = pl.ds(i * span * HEADS, span * HEADS)
        out[block, :] = rows[block, :].astype(bf16)
        copies.append(pltpu.make_async_copy(out.at[block], out_hbm.at[block], sems.at[i]))
        copies[-1].start()
    for copy in copies:
        copy.wait()


def read_call(arrays, tokens):
    shape = (tokens * HEADS, D)
    return pl.pallas_call(
        read_kernel,
        in_specs=whole(*arrays),
        out_specs=pl.BlockSpec(memory_space=pl.ANY),
        out_shape=jax.ShapeDtypeStruct(shape, bf16),
        scratch_shapes=[
            pltpu.VMEM((HEADS, D, D), f32),
            pltpu.VMEM(shape, f32),
            pltpu.VMEM(shape, bf16),
            pltpu.SemaphoreType.DMA((2,)),
        ],
        compiler_params=pltpu.CompilerParams(vmem_limit_bytes=8 << 20),
        name="read",
    )(*arrays)


def small_call(kernel, name, arrays, outs, scratch=(), after=None, limit=4, out_dtype=f32):
    extra = [] if after is None else [after]
    return pl.pallas_call(
        kernel,
        in_specs=whole(*arrays)
        + [pl.BlockSpec(memory_space=pl.ANY)] * len(extra),
        out_specs=whole(*outs),
        out_shape=[jax.ShapeDtypeStruct(s, out_dtype) for s in outs],
        scratch_shapes=[pltpu.VMEM(s, f32) for s in scratch],
        compiler_params=pltpu.CompilerParams(vmem_limit_bytes=limit << 20),
        name=name,
    )(*arrays, *extra)


def seat(y, x, c):
    return (y * XS + x) * CS + c


def plane_perm(move, spare):
    pairs = []
    for y in range(YS):
        for x in range(XS):
            pairs.append((seat(y, x, 0), seat(*spare(y, x), 0)))
            pairs.append((seat(y, x, 1), seat(*move(y, x), 1)))
    return pairs


def depth_perm(segs, move):
    pairs = []
    for y in range(YS):
        for x in range(XS):
            for g in range(segs):
                pairs.append((seat(y, x, 0) * segs + g, seat(y, x ^ 1, 0) * segs + g))
                at = seat(y, x, 1) * segs
                pairs.append((at + g, at + move(g)))
    return pairs


def chip_perm():
    return [(seat(y, x, c), seat(y, x, 1 - c)) for y in range(YS) for x in range(XS) for c in range(CS)]


def exchange(slots, axis, perms, order):
    out = list(slots)
    for k in order:
        out[k] = lax.ppermute(slots[k], axis, perms[k - 1])
    return out


def per_device(query_rows, key_rows, value_rows, out_gain, initial_state):
    tokens = query_rows.shape[1]
    steps = tokens * REFL
    swap = chip_perm()
    near_x = lambda y, x: (y, x ^ 1)
    near_y = lambda y, x: (y ^ 1, x)
    along_x = [
        plane_perm(lambda y, x, k=k: (y, x ^ k), near_y) for k in range(1, XS)
    ]
    along_y = [plane_perm(lambda y, x, k=k: (y ^ k, x), near_x) for k in range(1, YS)]
    segs = lax.axis_size("seg")
    along_z = [depth_perm(segs, lambda g, k=k: g ^ k) for k in range(1, ZG)]
    jump = depth_perm(segs, lambda g: segs - 1 - g)

    keys = key_rows.reshape(steps * HEADS, D)
    values = value_rows.reshape(steps * HEADS, D)
    query = query_rows.reshape(tokens * HEADS, D)
    keys = pltpu.with_memory_space_constraint(keys, pltpu.HBM)
    values = pltpu.with_memory_space_constraint(values, pltpu.HBM)
    pair, z, r = factor_call(keys, values)
    sib = lax.ppermute(pair, "seq", swap)
    slots = small_call(chip_kernel, "chip", [pair, sib], [(MSG, D)] * XS)
    slots = exchange(slots, "seq", along_x, (2, 1, 3))
    reaches = [reach_call(query, r, z, sib, slots[0], 0)]
    xslots = slots
    (total,) = small_call(
        row_kernel, "row", [slots[i] for i in (0, 2, 1, 3)], [(MSG, D)], [(XS, MSG, D)], after=reaches[-1][0]
    )
    slots = exchange([total] * YS, "seq", along_y, (1, 3, 2))
    yslots = slots
    reaches.append(reach_call(query, r, z, sib, total, 1))
    (total,) = small_call(
        column_kernel, "column", [slots[i] for i in (0, 1, 3, 2)], [(MSG, D)], [(YS, MSG, D)], after=reaches[-1][0]
    )
    slots = exchange([total] * ZG, ("seq", "seg"), along_z, (1, 2, 3))
    path, start = small_call(
        path_kernel,
        "path",
        [*xslots, *(yslots[i] for i in (0, 1, 3, 2)), initial_state],
        [(XS, MSG, D), (D, D)],
        [(XS, MSG, D), (YS, MSG, D)],
        after=total,
    )
    reaches.append(reach_call(query, r, z, sib, path, 2))
    (lead,) = small_call(
        lead_kernel,
        "lead",
        [*(slots[i] for i in (0, 1, 3, 2)), start],
        [(D, D)],
        [(ZG, MSG, D)],
        after=reaches[-1][0],
    )
    early = lax.ppermute(lead, ("seq", "seg"), jump)
    (fused,) = small_call(
        fuse_kernel,
        "fuse",
        [*slots, path],
        [(XS, MSG, D)],
        [(ZG, MSG, D)],
        after=lead,
    )
    slots = small_call(
        entry_kernel,
        "entry",
        [start, early, fused],
        [(D, D)] * XS,
        [(XS, D, D)],
    )
    slots = exchange(slots, "seq", along_x, (2, 1, 3))
    reaches.append(reach_call(query, r, z, sib, slots[0], 3))
    last = reaches[-1][0]
    for k in (2, 1, 3):
        slots[k], last = lax.optimization_barrier((slots[k], last))
    reaches[-1] = (last, reaches[-1][1])
    others = exchange(slots, "seq", [swap] * XS, (2, 1, 3))
    others[0] = lax.ppermute(slots[0], "seq", swap)
    arrays = [a for pair in reaches for a in pair] + [part[i] for part in (slots, others) for i in (0, 2, 1, 3)] + [out_gain]
    out = read_call(arrays, tokens)
    return out.reshape(1, tokens, HEADS, D)


def solution(mesh):
    return jax.shard_map(
        per_device,
        mesh=mesh,
        in_specs=(
            P("seg", "seq", None, None),
            P("seg", "seq", None, None, None),
            P("seg", "seq", None, None, None),
            P(),
            P(),
        ),
        out_specs=P("seg", "seq", None, None),
        check_vma=False,
    )
```

```python
import functools

import jax
import jax.numpy as jnp
from jax import lax
from jax.experimental import pallas as pl
from jax.experimental.pallas import tpu as pltpu
from jax.sharding import PartitionSpec as P

D = 128
HEADS = 4
REFL = 2
BLK = 128
XS = 4
YS = 4
CS = 2
ZG = 4
MSG = 2 * D

f32 = jnp.float32
bf16 = jnp.bfloat16


def split(x):
    high = x.astype(bf16)
    low = (x - high.astype(f32)).astype(bf16)
    return high, low


def dot_nn(a, b):
    return lax.dot_general(a, b, (((1,), (0,)), ((), ())), preferred_element_type=f32)


def dot_nt(a, b):
    return lax.dot_general(a, b, (((1,), (1,)), ((), ())), preferred_element_type=f32)


def wide(x):
    high, low = split(x)
    return jnp.concatenate([high, low], axis=1)


def tall_wide(x):
    row = wide(x)
    return jnp.concatenate([row, row], axis=0)


def mm_pre(left_wide, right_tall):
    out = dot_nn(left_wide, right_tall)
    n = out.shape[1] // 2
    return out[:, :n] + out[:, n:]


def mm(a, b):
    return mm_pre(wide(a), tall_wide(b))


def mm_nt(a, b):
    ah, al = split(a)
    bh, bl = split(b)
    return dot_nt(ah, bh) + dot_nt(ah, bl) + dot_nt(al, bh)


def place_x():
    return lax.rem(lax.axis_index("seq") // CS, XS)


def place_y():
    return lax.axis_index("seq") // (CS * XS)


def place_core():
    return lax.rem(lax.axis_index("seq"), CS)


def place_seg():
    return lax.axis_index("seg")


def iota2(shape, dim):
    return lax.broadcasted_iota(jnp.int32, shape, dim)


def factor_kernel(k_hbm, v_hbm, m_ref, z_ref, r_ref, k_ref, v_ref, keys, values, sems):
    pieces = sems.shape[1]
    size = k_ref.shape[0] // pieces
    copies = [
        [
            pltpu.make_async_copy(
                src.at[pl.ds(i * size, size)], dst.at[pl.ds(i * size, size)], sems.at[j, i]
            )
            for i in range(pieces)
        ]
        for j, (src, dst) in enumerate(((k_hbm, k_ref), (v_hbm, v_ref)))
    ]
    for copy in copies[0]:
        copy.start()
    for i, copy in enumerate(copies[0]):
        copy.wait()
        keys[i * size : (i + 1) * size] = k_ref[i * size : (i + 1) * size].astype(f32)
    for copy in copies[1]:
        copy.start()
    nblk = r_ref.shape[1] // BLK
    row = iota2((BLK, BLK), 0)
    col = iota2((BLK, BLK), 1)
    eye = row == col
    unit = jnp.where(eye, 1.0, 0.0).astype(bf16)
    pair = ((row >> 1) == (col >> 1)) & (row < col)
    chains = [(h, b) for h in range(HEADS) for b in range(nblk)]
    rs, rts, vts, uppers, invs, ccols, crows = [], [], [], [], [], [], []
    for h, b in chains:
        rows = pl.ds(h + HEADS * BLK * b, BLK, stride=HEADS)
        r = keys[rows, :].astype(bf16)
        r_ref[h, b * BLK : (b + 1) * BLK, :] = r
        both = dot_nt(jnp.concatenate([r, unit], axis=0), r)
        gram, rt = both[:BLK], both[BLK:].astype(bf16)
        diag = jnp.where(eye, gram, 0.0)
        ccol = lax.rsqrt(jnp.sum(diag, axis=1, keepdims=True) + 1e-06)
        crow = lax.rsqrt(jnp.sum(diag, axis=0, keepdims=True) + 1e-06)
        upper = jnp.where(row < col, 2.0 * ccol * crow * gram, 0.0)
        inv = jnp.where(eye, 1.0, 0.0) - jnp.where(pair, upper, 0.0)
        rs.append(r)
        rts.append(rt)
        uppers.append(upper)
        invs.append(inv)
        ccols.append(ccol)
        crows.append(crow)
    for level in range(1, 7):
        off = ((row >> (level + 1)) == (col >> (level + 1))) & (
            (row >> level) < (col >> level)
        )
        talls = [tall_wide(inv) for inv in invs]
        mids = [
            mm_pre(wide(jnp.where(off, upper, 0.0)), tall) for upper, tall in zip(uppers, talls)
        ]
        invs = [inv - mm(inv, mid) for inv, mid in zip(invs, mids)]
    for i, copy in enumerate(copies[1]):
        copy.wait()
        values[i * size : (i + 1) * size] = v_ref[i * size : (i + 1) * size].astype(f32)
    for h, b in chains:
        rows = pl.ds(h + HEADS * BLK * b, BLK, stride=HEADS)
        vts.append(values[rows, :].astype(bf16).T)
    pairs = []
    base = jnp.where(iota2((2 * D, D), 0) == iota2((2 * D, D), 1), 1.0, 0.0)
    sign = jnp.where(iota2((2 * D, D), 0) < D, -1.0, 1.0)
    for i, (h, b) in enumerate(chains):
        wh, wl = split(2.0 * ccols[i] * invs[i])
        uh, ul = split(2.0 * invs[i])
        wt = dot_nn(jnp.concatenate([rts[i], rts[i]], axis=1), jnp.concatenate([wh, wl], axis=0))
        ut = dot_nn(jnp.concatenate([vts[i], vts[i]], axis=1), jnp.concatenate([uh, ul], axis=0))
        z = jnp.concatenate([wt, ut], axis=0) * crows[i]
        z_ref[h, b] = z
        rr = jnp.concatenate([rs[i], rs[i]], axis=0)
        pairs.append(base + sign * dot_nn(wide(z), rr))
    for h in range(HEADS):
        own = pairs[h * nblk : (h + 1) * nblk]
        while len(own) > 1:
            own = [compose(own[i], own[i + 1]) for i in range(0, len(own), 2)]
        m_ref[h] = own[0]


def compose(first, second):
    moved = mm(first, second[:D])
    keep = jnp.concatenate([jnp.zeros((D, D), f32), second[D:]], axis=0)
    return moved + keep


def whole(*arrays):
    return [pl.BlockSpec(memory_space=pltpu.VMEM)] * len(arrays)


def factor_call(k, v):
    steps = k.shape[0] // HEADS
    nblk = steps // BLK
    return pl.pallas_call(
        factor_kernel,
        in_specs=[pl.BlockSpec(memory_space=pl.ANY)] * 2,
        out_specs=[pl.BlockSpec(memory_space=pltpu.VMEM)] * 3,
        out_shape=[
            jax.ShapeDtypeStruct((HEADS, 2 * D, D), f32),
            jax.ShapeDtypeStruct((HEADS, nblk, 2 * D, D), f32),
            jax.ShapeDtypeStruct((HEADS, steps, D), bf16),
        ],
        scratch_shapes=[pltpu.VMEM((HEADS * steps, D), bf16)] * 2
        + [pltpu.VMEM((HEADS * steps, D), f32)] * 2
        + [pltpu.SemaphoreType.DMA((2, 4))],
        compiler_params=pltpu.CompilerParams(vmem_limit_bytes=16 << 20),
        name="factor",
    )(k, v)


def chip_kernel(own_ref, sib_ref, *out_refs):
    x = place_x()
    for k in range(XS):
        head = x ^ k
        out_refs[k][...] = compose(sib_ref[head], own_ref[head])


def ordered_xor(slots, place, scratch):
    for k, slot in enumerate(slots):
        scratch[place ^ k] = slot[...]


def msg_compose(rows, second):
    moved = mm(rows, second[:D])
    return jnp.concatenate([moved[:D], moved[D:] + second[D:]], axis=0)


def advance(state, second):
    return mm(state, second[:D]) + second[D:]


def write_total(total_ref, hold):
    tail = msg_compose(hold[2], hold[3])
    total_ref[...] = msg_compose(msg_compose(hold[0], hold[1]), tail)


def row_kernel(s0, s2, s1, s3, after_ref, total_ref, hold):
    ordered_xor([s0, s1, s2, s3], place_x(), hold)
    write_total(total_ref, hold)


def column_kernel(s0, s1, s3, s2, after_ref, total_ref, hold):
    ordered_xor([s0, s1, s2, s3], place_y(), hold)
    write_total(total_ref, hold)


def place_prefix(place, hold):
    first = hold[0]
    second = msg_compose(first, hold[1])
    third = msg_compose(second, hold[2])
    out = jnp.where(iota2((MSG, D), 0) == iota2((MSG, D), 1), 1.0, 0.0)
    for i, prefix in enumerate((first, second, third)):
        out = jnp.where(place == i + 1, prefix, out)
    return out


def path_kernel(*refs):
    xslots, yslots = refs[:4], [refs[i] for i in (4, 5, 7, 6)]
    init_ref, after_ref, path_ref, start_ref, xhold, yhold = refs[8:]
    x = place_x()
    y = place_y()
    ordered_xor(xslots, x, xhold)
    ordered_xor(yslots, y, yhold)
    here = place_prefix(y, yhold)
    first = xhold[0]
    second = msg_compose(first, xhold[1])
    third = msg_compose(second, xhold[2])
    path_ref[0] = here
    left = wide(here)
    for i, prefix in enumerate((first, second, third)):
        moved = mm_pre(left, tall_wide(prefix[:D]))
        path_ref[i + 1, :D, :] = moved[:D]
        path_ref[i + 1, D:, :] = moved[D:] + prefix[D:]
    start_ref[...] = init_ref[x].T


def lead_kernel(s0, s1, s2, s3, start_ref, after_ref, lead_ref, hold):
    ordered_xor([s0, s1, s2, s3], lax.rem(place_seg(), ZG), hold)
    tail = msg_compose(hold[2], hold[3])
    state = advance(advance(start_ref[...], hold[0]), hold[1])
    lead_ref[...] = advance(state, tail)


def fuse_kernel(s0, s1, s2, s3, path_ref, after_ref, fuse_ref, hold):
    g = lax.rem(place_seg(), ZG)
    ordered_xor([s0, s1, s2, s3], g, hold)
    window = place_prefix(g, hold)
    left = wide(window)
    for i in range(XS):
        path = path_ref[i]
        moved = mm_pre(left, tall_wide(path[:D]))
        fuse_ref[i, :D, :] = moved[:D]
        fuse_ref[i, D:, :] = moved[D:] + path[D:]


def entry_kernel(start_ref, early_ref, fuse_ref, o0, o1, o2, o3, scratch):
    x = place_x()
    state = jnp.where(place_seg() >= ZG, early_ref[...], start_ref[...])
    left = wide(state)
    for i in range(XS):
        scratch[i] = mm_pre(left, tall_wide(fuse_ref[i, :D, :])) + fuse_ref[i, D:, :]
    for k, out in enumerate((o0, o1, o2, o3)):
        out[...] = scratch[x ^ k]


def reach_kernel(
    q_ref, r_ref, z_ref, sib_ref, after_ref, reach_ref, base_ref, rows, *, head
):
    tokens = reach_ref.shape[0]
    nblk = z_ref.shape[0]
    span = tokens // nblk
    rows[...] = q_ref[...].astype(f32)
    visible = iota2((span, BLK), 1) <= REFL * iota2((span, BLK), 0) + (REFL - 1)
    base = jnp.where(iota2((2 * D, D), 0) == iota2((2 * D, D), 1), 1.0, 0.0)
    sign = jnp.where(iota2((2 * D, D), 0) < D, -1.0, 1.0)
    prefixes = [jnp.where(place_core() == 1, sib_ref[...], base)]
    for b in range(nblk - 1):
        rr = jnp.concatenate([r_ref[b * BLK : (b + 1) * BLK, :]] * 2, axis=0)
        piece = base + sign * dot_nn(wide(z_ref[b]), rr)
        prefixes.append(compose(prefixes[b], piece))
    projects, locals_ = [], []
    for b in range(nblk):
        q = rows[pl.ds(head + HEADS * span * b, span, stride=HEADS), :]
        scores = dot_nt(q.astype(bf16), r_ref[b * BLK : (b + 1) * BLK, :])
        sz = mm_nt(jnp.where(visible, scores, 0.0), z_ref[b])
        projects.append(q - sz[:, :D])
        locals_.append(sz[:, D:])
    moves = [mm_nt(projects[b], prefixes[b]) for b in range(nblk)]
    for b in range(nblk):
        part = slice(b * span, (b + 1) * span)
        reach_ref[part, :] = wide(moves[b][:, :D])
        base_ref[part, :] = moves[b][:, D:] + locals_[b]


def reach_call(q, r, z, sib, after, head):
    tokens = q.shape[0] // HEADS

    def spec(array):
        rest = array.shape[1:]
        return pl.BlockSpec((None, *rest), lambda i: (head,) + (0,) * len(rest))

    return pl.pallas_call(
        functools.partial(reach_kernel, head=head),
        grid=(1,),
        in_specs=[
            pl.BlockSpec(q.shape, lambda i: (0, 0)),
            spec(r),
            spec(z),
            spec(sib),
            pl.BlockSpec(memory_space=pl.ANY),
        ],
        out_specs=[
            pl.BlockSpec((tokens, 2 * D), lambda i: (0, 0)),
            pl.BlockSpec((tokens, D), lambda i: (0, 0)),
        ],
        out_shape=[
            jax.ShapeDtypeStruct((tokens, 2 * D), bf16),
            jax.ShapeDtypeStruct((tokens, D), f32),
        ],
        scratch_shapes=[pltpu.VMEM(q.shape, f32)],
        compiler_params=pltpu.CompilerParams(vmem_limit_bytes=6 << 20),
        cost_estimate=pl.CostEstimate(
            flops=400_000_000, bytes_accessed=3_000_000, transcendentals=0
        ),
        name="reach",
    )(q, r, z, sib, after)


def read_kernel(*refs):
    reaches, bases = refs[: 2 * HEADS : 2], refs[1 : 2 * HEADS : 2]
    refs = refs[2 * HEADS :]
    mine, other = refs[:HEADS], refs[HEADS : 2 * HEADS]
    mine, other = ([part[i] for i in (0, 2, 1, 3)] for part in (mine, other))
    gain_ref, out_hbm, states, rows, out, sems = refs[2 * HEADS :]
    x = place_x()

    @pl.when(place_core() == 0)
    def _():
        ordered_xor(other, x, states)

    @pl.when(place_core() != 0)
    def _():
        ordered_xor(mine, x, states)

    rights = []
    for h in range(HEADS):
        both = jnp.concatenate(split(states[h]), axis=0)
        rights.append(jnp.concatenate([both, both], axis=1))
    pieces = sems.shape[0]
    span = reaches[0].shape[0] // pieces
    copies = []
    for i in range(pieces):
        part = slice(i * span, (i + 1) * span)
        for h in range(HEADS):
            moved = dot_nt(reaches[h][part, :], rights[h])
            read = moved[:, :D] + moved[:, D:] + bases[h][part, :]
            scale = lax.rsqrt(jnp.mean(read * read, axis=-1, keepdims=True) + 1e-06)
            rows[pl.ds(i * span * HEADS + h, span, stride=HEADS), :] = (
                read * scale * gain_ref[h : h + 1, :]
            )
        block = pl.ds(i * span * HEADS, span * HEADS)
        out[block, :] = rows[block, :].astype(bf16)
        copies.append(pltpu.make_async_copy(out.at[block], out_hbm.at[block], sems.at[i]))
        copies[-1].start()
    for copy in copies:
        copy.wait()


def read_call(arrays, tokens):
    shape = (tokens * HEADS, D)
    return pl.pallas_call(
        read_kernel,
        in_specs=whole(*arrays),
        out_specs=pl.BlockSpec(memory_space=pl.ANY),
        out_shape=jax.ShapeDtypeStruct(shape, bf16),
        scratch_shapes=[
            pltpu.VMEM((HEADS, D, D), f32),
            pltpu.VMEM(shape, f32),
            pltpu.VMEM(shape, bf16),
            pltpu.SemaphoreType.DMA((2,)),
        ],
        compiler_params=pltpu.CompilerParams(vmem_limit_bytes=8 << 20),
        name="read",
    )(*arrays)


def small_call(kernel, name, arrays, outs, scratch=(), after=None, limit=4, out_dtype=f32):
    extra = [] if after is None else [after]
    return pl.pallas_call(
        kernel,
        in_specs=whole(*arrays)
        + [pl.BlockSpec(memory_space=pl.ANY)] * len(extra),
        out_specs=whole(*outs),
        out_shape=[jax.ShapeDtypeStruct(s, out_dtype) for s in outs],
        scratch_shapes=[pltpu.VMEM(s, f32) for s in scratch],
        compiler_params=pltpu.CompilerParams(vmem_limit_bytes=limit << 20),
        name=name,
    )(*arrays, *extra)


def seat(y, x, c):
    return (y * XS + x) * CS + c


def plane_perm(move, spare):
    pairs = []
    for y in range(YS):
        for x in range(XS):
            pairs.append((seat(y, x, 0), seat(*spare(y, x), 0)))
            pairs.append((seat(y, x, 1), seat(*move(y, x), 1)))
    return pairs


def depth_perm(segs, move):
    pairs = []
    for y in range(YS):
        for x in range(XS):
            for g in range(segs):
                pairs.append((seat(y, x, 0) * segs + g, seat(y, x ^ 1, 0) * segs + g))
                at = seat(y, x, 1) * segs
                pairs.append((at + g, at + move(g)))
    return pairs


def chip_perm():
    return [(seat(y, x, c), seat(y, x, 1 - c)) for y in range(YS) for x in range(XS) for c in range(CS)]


def exchange(slots, axis, perms, order):
    out = list(slots)
    for k in order:
        out[k] = lax.ppermute(slots[k], axis, perms[k - 1])
    return out


def per_device(query_rows, key_rows, value_rows, out_gain, initial_state):
    tokens = query_rows.shape[1]
    steps = tokens * REFL
    swap = chip_perm()
    near_x = lambda y, x: (y, x ^ 1)
    near_y = lambda y, x: (y ^ 1, x)
    along_x = [
        plane_perm(lambda y, x, k=k: (y, x ^ k), near_y) for k in range(1, XS)
    ]
    along_y = [plane_perm(lambda y, x, k=k: (y ^ k, x), near_x) for k in range(1, YS)]
    segs = lax.axis_size("seg")
    along_z = [depth_perm(segs, lambda g, k=k: g ^ k) for k in range(1, ZG)]
    jump = depth_perm(segs, lambda g: segs - 1 - g)

    keys = key_rows.reshape(steps * HEADS, D)
    values = value_rows.reshape(steps * HEADS, D)
    query = query_rows.reshape(tokens * HEADS, D)
    keys = pltpu.with_memory_space_constraint(keys, pltpu.HBM)
    values = pltpu.with_memory_space_constraint(values, pltpu.HBM)
    pair, z, r = factor_call(keys, values)
    sib = lax.ppermute(pair, "seq", swap)
    slots = small_call(chip_kernel, "chip", [pair, sib], [(MSG, D)] * XS)
    slots = exchange(slots, "seq", along_x, (2, 1, 3))
    reaches = [reach_call(query, r, z, sib, slots[0], 0)]
    xslots = slots
    (total,) = small_call(
        row_kernel, "row", [slots[i] for i in (0, 2, 1, 3)], [(MSG, D)], [(XS, MSG, D)], after=reaches[-1][0]
    )
    slots = exchange([total] * YS, "seq", along_y, (1, 3, 2))
    yslots = slots
    reaches.append(reach_call(query, r, z, sib, total, 1))
    (total,) = small_call(
        column_kernel, "column", [slots[i] for i in (0, 1, 3, 2)], [(MSG, D)], [(YS, MSG, D)], after=reaches[-1][0]
    )
    slots = exchange([total] * ZG, ("seq", "seg"), along_z, (1, 2, 3))
    path, start = small_call(
        path_kernel,
        "path",
        [*xslots, *(yslots[i] for i in (0, 1, 3, 2)), initial_state],
        [(XS, MSG, D), (D, D)],
        [(XS, MSG, D), (YS, MSG, D)],
        after=total,
    )
    reaches.append(reach_call(query, r, z, sib, path, 2))
    (lead,) = small_call(
        lead_kernel,
        "lead",
        [*slots, start],
        [(D, D)],
        [(ZG, MSG, D)],
        after=reaches[-1][0],
    )
    early = lax.ppermute(lead, ("seq", "seg"), jump)
    (fused,) = small_call(
        fuse_kernel,
        "fuse",
        [*slots, path],
        [(XS, MSG, D)],
        [(ZG, MSG, D)],
        after=lead,
    )
    slots = small_call(
        entry_kernel,
        "entry",
        [start, early, fused],
        [(D, D)] * XS,
        [(XS, D, D)],
    )
    slots = exchange(slots, "seq", along_x, (2, 1, 3))
    reaches.append(reach_call(query, r, z, sib, slots[0], 3))
    last = reaches[-1][0]
    for k in (2, 1, 3):
        slots[k], last = lax.optimization_barrier((slots[k], last))
    reaches[-1] = (last, reaches[-1][1])
    others = exchange(slots, "seq", [swap] * XS, (2, 1, 3))
    others[0] = lax.ppermute(slots[0], "seq", swap)
    arrays = [a for pair in reaches for a in pair] + [part[i] for part in (slots, others) for i in (0, 2, 1, 3)] + [out_gain]
    out = read_call(arrays, tokens)
    return out.reshape(1, tokens, HEADS, D)


def solution(mesh):
    return jax.shard_map(
        per_device,
        mesh=mesh,
        in_specs=(
            P("seg", "seq", None, None),
            P("seg", "seq", None, None, None),
            P("seg", "seq", None, None, None),
            P(),
            P(),
        ),
        out_specs=P("seg", "seq", None, None),
        check_vma=False,
    )
```
